32 devices in a mesh: dp: 8 (over z, y), tensor: 4 (over x, core).
Axes of the slice: x: 2, y: 2, z: 4, core: 2. Of those that a mesh axis runs over, the one named last changes fastest.
Arguments:
- tokens: bfloat16 [16384, 768], P(('dp', 'tensor')), may hold values from -6 to 6
- memory: bfloat16 [8192, 768], P(('dp', 'tensor')), may hold values from -6 to 6
- cotangent: bfloat16 [16384, 768], P(('dp', 'tensor')), may hold values from -6 to 6
- norm_gains: float32 [3, 768], replicated, may hold values from 0.5 to 1.5
- query_weight: bfloat16 [2, 768, 768], P(None, None, 'tensor'), may hold values from -0.0546875 to 0.0546875
- keyvalue_weight: bfloat16 [2, 2, 768, 768], P(None, None, None, 'tensor'), may hold values from -0.21875 to 0.21875
- output_weight: bfloat16 [2, 768, 768], P(None, 'tensor'), may hold values from -0.625 to 0.625
- bias_table: float32 [32, 12], P(None, 'tensor'), may hold values from -5 to 5
- inner_weight: bfloat16 [2, 768, 2048], P(None, None, 'tensor'), may hold values from -0.21875 to 0.21875
- outer_weight: bfloat16 [2048, 768], P('tensor'), may hold values from -0.1875 to 0.1875
- target_lengths: int32 [16, 12], P('dp'), may hold values from 0 to 512, as said below
- source_lengths: int32 [16, 12], P('dp'), may hold values from 0 to 42, as said below
Outputs:
- output_rows: bfloat16 [16384, 768], P(('dp', 'tensor'))
- tokens_grad: float32 [16384, 768], P(('dp', 'tensor'))
- memory_grad: float32 [8192, 768], P(('dp', 'tensor'))
- gains_grad: float32 [3, 768], replicated
- query_grad: float32 [2, 768, 768], P(None, None, 'tensor')
- keyvalue_grad: float32 [2, 2, 768, 768], P(None, None, None, 'tensor')
- output_grad: float32 [2, 768, 768], P(None, 'tensor')
- table_grad: float32 [32, 12], P(None, 'tensor')
- inner_grad: float32 [2, 768, 2048], P(None, None, 'tensor')
- outer_grad: float32 [2048, 768], P('tensor')
- model_stats: float32 [11, 768], replicated
- head_stats: float32 [6, 768], P(None, 'tensor')
- projection_stats: float32 [2, 768], P(None, 'tensor')
- unit_stats: float32 [3, 2048], P(None, 'tensor')
The draws below stay inside these ranges and needn't reach their ends.
Inputs may be any that keep to these rules, and one draw needn't show every extreme that they name: `target_lengths`: A row lists the decoder lengths of the documents packed in one slot in order; the first is 1 or more, zeros stand only after the last document, and a row sums to at most 1024. `source_lengths`: A row lists the encoder lengths of the same documents: 1 or more exactly where the decoder length is, zero elsewhere; a row sums to at most 512.
All inputs are finite; a program needn't handle non-finite values.
Results may differ from the reference program's by a relative error of at most 0.023.
The reference program's roundings to bfloat16 on the way count: a program that leaves them out, or rounds other values in their place, can miss the bound.
Values may be sent and summed in bfloat16 or wider, within the bound.
No kernel may reach another device: no remote copies, remote signals or barrier semaphores. Data moves between devices by JAX's collectives and lax.ppermute only.
A program may use at most 192 MiB of HBM per device.

```python
import math
import jax
import jax.numpy as jnp
import numpy as np
from jax import lax

D = 768
FF = 2048
H = 12
DH = 64
BUCKETS = 32
MAXDIST = 128
SLOT = 1024
MEM = 512
DOCS = 12
HD = 768
SLOTS = 16
TOKENS = 16384
MEMORY_ROWS = 8192


def packed_lengths(key):
    base_key = jax.random.fold_in(key, 11)
    level_key, length_key, slot_key, source_key = jax.random.split(base_key, 4)
    half_slot = SLOT // 2
    levels = jax.random.randint(level_key, (SLOTS, DOCS), 0, 7)
    ceiling = jnp.maximum(jnp.right_shift(jnp.full((SLOTS, DOCS), half_slot, jnp.int32), levels), 1)
    drawn_lengths = jax.random.randint(length_key, (SLOTS, DOCS), 0, 1 << 30) % ceiling + 1
    chosen = jax.random.randint(slot_key, (), 0, SLOTS)
    forced = (jnp.arange(SLOTS)[:, None] == chosen) & (jnp.arange(DOCS)[None, :] == 0)
    drawn_lengths = jnp.where(forced, half_slot, drawn_lengths)
    before = jnp.cumsum(drawn_lengths, axis=1) - drawn_lengths
    target = jnp.minimum(drawn_lengths, jnp.maximum(SLOT - before, 0))
    source_top = MEM // DOCS
    source = jax.random.randint(source_key, (SLOTS, DOCS), 1, source_top + 1)
    source = jnp.where(forced, source_top, source)
    source = jnp.where(target > 0, source, 0)
    return (target.astype(jnp.int32), source.astype(jnp.int32))


def draw_target_lengths(key, part):
    return packed_lengths(key)[0]


def draw_source_lengths(key, part):
    return packed_lengths(key)[1]


def shard_levels(own_key, extent, pieces, low, top_value):
    def one(dim, blocks):
        heights = jax.random.uniform(jax.random.fold_in(jax.random.fold_in(own_key, 6), dim), (blocks,), jnp.float32, low / len(pieces), top_value / len(pieces))
        return jnp.repeat(jnp.exp(heights), extent[dim] // blocks).reshape((-1,) + (1,) * (len(extent) - dim - 1))

    loudness = one(*pieces[0])
    for cut in pieces[1:]:
        loudness = loudness * one(*cut)
    return loudness


def noise(key, shape, scale, limit, cuts=(), held_as=jnp.bfloat16):
    values = jax.random.normal(key, shape, jnp.float32) * scale
    if len(cuts) > 0:
        values = shard_levels(key, shape, cuts, -0.22, 0.18) * values
    return jnp.clip(values, min=-limit, max=limit).astype(held_as)


def setup_inputs(seed: int = 0) -> dict:
    key_of = jax.random.split(jax.random.key(seed), 13)
    tokens = noise(key_of[0], (TOKENS, D), 1.0, 6.0, ((0, 32),))
    memory = noise(key_of[1], (MEMORY_ROWS, D), 1.0, 6.0, ((0, 32),))
    cotangent = noise(key_of[2], (TOKENS, D), 1.0, 6.0, ((0, 32),))
    norm_gains = jnp.clip(1.0 + 0.1 * jax.random.normal(key_of[3], (3, D), jnp.float32), 0.5, 1.5)
    query_weight = noise(key_of[4], (2, D, HD), (16 * D) ** -0.5, 0.0546875, ((2, 4),))
    keyvalue_weight = noise(key_of[5], (2, 2, D, HD), D ** -0.5, 0.21875, ((3, 4),))
    output_weight = noise(key_of[6], (2, HD, D), (HD // 8) ** -0.5, 0.625, ((1, 4),))
    bias_table = noise(key_of[7], (BUCKETS, H), 1.0, 5.0, ((1, 4),), jnp.float32)
    inner_weight = noise(key_of[8], (2, D, FF), D ** -0.5, 0.21875, ((2, 4),))
    outer_weight = noise(key_of[9], (FF, D), (FF // 2) ** -0.5, 0.1875, ((0, 4),))
    target_lengths = draw_target_lengths(jax.random.fold_in(key_of[12], 71), 0)
    source_lengths = draw_source_lengths(jax.random.fold_in(key_of[12], 71), 0)
    return dict(tokens=tokens, memory=memory, cotangent=cotangent, norm_gains=norm_gains, query_weight=query_weight, keyvalue_weight=keyvalue_weight, output_weight=output_weight, bias_table=bias_table, inner_weight=inner_weight, outer_weight=outer_weight, target_lengths=target_lengths, source_lengths=source_lengths)


NEG_FILL = -1e+30
NORM_EPS = 1e-06
HIGHEST = lax.Precision.HIGHEST

@jax.custom_vjp
def low(v):
    return lax.optimization_barrier(v.astype(jnp.bfloat16)).astype(jnp.float32)

@jax.custom_vjp
def low_back(v):
    return v

def low_keep(v):
    return (low(v), None)

def low_pass(kept, grad):
    return (grad,)

def back_keep(v):
    return (v, None)

def back_low(kept, grad):
    return (low(grad),)
low.defvjp(low_keep, low_pass)
low_back.defvjp(back_keep, back_low)

def bucket_list(position_count, buckets, max_reach):
    exact_count = buckets // 2
    chosen = []
    for spread in range(position_count):
        if spread < exact_count:
            chosen.append(spread)
        else:
            larger = exact_count + math.floor(math.log(spread / exact_count) / math.log(max_reach / exact_count) * (buckets - exact_count))
            chosen.append(min(larger, buckets - 1))
    return np.array(chosen, dtype=np.int32)

def segment_ids(lengths_row, position_count):
    ends = jnp.cumsum(lengths_row)
    places = jnp.arange(position_count, dtype=jnp.int32)
    passed = lax.optimization_barrier(jnp.sum((places[:, None] >= ends[None, :]).astype(jnp.int32), axis=1))
    return jnp.where(places < ends[-1], passed + 1, 0).astype(jnp.int32)

def matmul(left_side, right_side):
    return jnp.dot(left_side, right_side, precision=HIGHEST, preferred_element_type=jnp.float32)

def rms_normed(rows_in, gain_row):
    inverse_rms = lax.rsqrt(lax.optimization_barrier(jnp.mean(rows_in * rows_in, axis=-1, keepdims=True)) + NORM_EPS)
    return rows_in * inverse_rms * gain_row

def attention(queries, keys_all, values_all, bias_full, allowed, live_rows):
    split_query = queries.reshape(queries.shape[0], H, DH)
    split_key = keys_all.reshape(keys_all.shape[0], H, DH)
    split_value = values_all.reshape(values_all.shape[0], H, DH)
    scores = jnp.einsum('qhd,khd->hqk', split_query, split_key, precision=HIGHEST)
    if bias_full is not None:
        scores = scores + bias_full
    scores = low_back(scores)
    masked = jnp.where(allowed[None], scores, NEG_FILL)
    weights = low(jax.nn.softmax(masked, axis=-1))
    context = jnp.einsum('hqk,khd->qhd', weights, split_value, precision=HIGHEST)
    context = context * live_rows[:, None, None].astype(jnp.float32)
    return low_back(low(context.reshape(queries.shape[0], H * DH)))

def layer(params, slot_tokens, slot_memory, target_seg, source_seg, bucket_index):
    norm_gains, query_weight, keyvalue_weight, output_weight, bias_table, inner_weight, outer_weight = params
    places = jnp.arange(SLOT)
    live_rows = target_seg > 0
    self_allowed = (target_seg[:, None] == target_seg[None, :]) & live_rows[:, None] & (places[:, None] >= places[None, :])
    cross_allowed = (target_seg[:, None] == source_seg[None, :]) & live_rows[:, None]
    bias_full = jnp.transpose(jnp.take(bias_table, bucket_index, axis=0), (2, 0, 1))
    normed_first = low(rms_normed(slot_tokens, norm_gains[0]))
    self_query = low_back(low(matmul(normed_first, query_weight[0])))
    self_key = low_back(low(matmul(normed_first, keyvalue_weight[0, 0])))
    self_value = low_back(low(matmul(normed_first, keyvalue_weight[0, 1])))
    self_context = attention(self_query, self_key, self_value, bias_full, self_allowed, live_rows)
    after_self = slot_tokens + low_back(matmul(self_context, output_weight[0]))
    normed_second = low(rms_normed(after_self, norm_gains[1]))
    cross_query = low_back(low(matmul(normed_second, query_weight[1])))
    cross_key = low_back(low(matmul(slot_memory, keyvalue_weight[1, 0])))
    cross_value = low_back(low(matmul(slot_memory, keyvalue_weight[1, 1])))
    cross_context = attention(cross_query, cross_key, cross_value, None, cross_allowed, live_rows)
    after_cross = after_self + low_back(matmul(cross_context, output_weight[1]))
    normed_third = low(rms_normed(after_cross, norm_gains[2]))
    gate = low_back(matmul(normed_third, inner_weight[0]))
    up_part = low_back(matmul(normed_third, inner_weight[1]))
    hidden = low(jax.nn.gelu(gate, approximate=True) * up_part)
    return after_cross + low_back(matmul(hidden, outer_weight))

def reference(tokens, memory, cotangent, norm_gains, query_weight, keyvalue_weight, output_weight, bias_table, inner_weight, outer_weight, target_lengths, source_lengths):
    params = (norm_gains.astype(jnp.float32), query_weight.astype(jnp.float32), keyvalue_weight.astype(jnp.float32), output_weight.astype(jnp.float32), bias_table.astype(jnp.float32), inner_weight.astype(jnp.float32), outer_weight.astype(jnp.float32))
    slot_tokens = tokens.astype(jnp.float32).reshape(SLOTS, SLOT, D)
    slot_memory = memory.astype(jnp.float32).reshape(SLOTS, MEM, D)
    slot_grads = cotangent.astype(jnp.float32).reshape(SLOTS, SLOT, D)
    target_seg = jax.vmap(lambda length_row: segment_ids(length_row, SLOT))(target_lengths)
    source_seg = jax.vmap(lambda length_row: segment_ids(length_row, MEM))(source_lengths)
    offsets = np.maximum(np.arange(SLOT)[:, None] - np.arange(SLOT)[None, :], 0)
    bucket_index = jnp.asarray(bucket_list(SLOT, BUCKETS, MAXDIST)[offsets].astype(np.int32))

    def one_slot(carried, slot_parts):
        rows_in, memory_in, grad_in, target_in, source_in = slot_parts

        def forward(params_in, tokens_in, memory_rows):
            return layer(params_in, tokens_in, memory_rows, target_in, source_in, bucket_index)
        result, pullback = jax.vjp(forward, params, rows_in, memory_in)
        param_grads, tokens_part, memory_part = pullback(grad_in)
        carried = jax.tree.map(lambda total_part, slot_part: total_part + slot_part, carried, param_grads)
        return (carried, (result.astype(jnp.bfloat16), tokens_part, memory_part))
    start_grads = jax.tree.map(jnp.zeros_like, params)
    totals, outputs = lax.scan(one_slot, start_grads, (slot_tokens, slot_memory, slot_grads, target_seg, source_seg))
    results, tokens_parts, memory_parts = outputs
    gains_grad, query_grad, keyvalue_grad, output_grad, table_grad, inner_grad, outer_grad = totals
    query_sq = query_grad * query_grad
    keyvalue_sq = keyvalue_grad * keyvalue_grad
    output_sq = output_grad * output_grad
    inner_sq = inner_grad * inner_grad
    outer_sq = outer_grad * outer_grad
    model_stats = jnp.concatenate((lax.optimization_barrier(jnp.mean(query_sq, axis=2)), lax.optimization_barrier(jnp.mean(keyvalue_sq, axis=3)).reshape(4, D), lax.optimization_barrier(jnp.mean(inner_sq, axis=2)), lax.optimization_barrier(jnp.mean(output_sq, axis=1)), lax.optimization_barrier(jnp.mean(outer_sq, axis=0))[None]), axis=0)
    head_stats = jnp.concatenate((lax.optimization_barrier(jnp.mean(query_sq, axis=1)), lax.optimization_barrier(jnp.mean(keyvalue_sq, axis=2)).reshape(4, HD)), axis=0)
    projection_stats = lax.optimization_barrier(jnp.mean(output_sq, axis=2))
    unit_stats = jnp.concatenate((lax.optimization_barrier(jnp.mean(inner_sq, axis=1)), lax.optimization_barrier(jnp.mean(outer_sq, axis=1))[None]), axis=0)
    return (results.reshape(TOKENS, D), tokens_parts.reshape(TOKENS, D), memory_parts.reshape(MEMORY_ROWS, D), gains_grad, query_grad, keyvalue_grad, output_grad, table_grad, inner_grad, outer_grad, model_stats, head_stats, projection_stats, unit_stats)
```

```python
import math

import jax
import jax.numpy as jnp
import numpy as np
from jax import lax
from jax.experimental import pallas as pl
from jax.experimental.pallas import tpu as pltpu
from jax.sharding import PartitionSpec as P

D = 768
DH = 64
BUCKETS = 32
MAXDIST = 128
SLOT = 1024
MEM = 512
NORM_EPS = 1e-06
NEG_FILL = -1e30
BQ = 256
VM = pl.BlockSpec(memory_space=pltpu.VMEM)
SM = pl.BlockSpec(memory_space=pltpu.SMEM)
NT = (((1,), (1,)), ((), ()))
NN = (((1,), (0,)), ((), ()))
TN = (((0,), (0,)), ((), ()))
f32, bf16 = jnp.float32, jnp.bfloat16


def dg(a, b, dims):
    return lax.dot_general(a, b, dims, preferred_element_type=f32)


def blk(i):
    return pl.ds(pl.multiple_of(i * BQ, BQ), BQ)


def put_heads(ref, rows, wide):
    for h in range(3):
        ref[h, rows, :] = wide[:, h * 64:(h + 1) * 64].astype(ref.dtype)


def project(n_ref, w, out3):
    def body(i, _):
        put_heads(out3, blk(i), dg(n_ref[blk(i), :], w, NT))
        return 0
    lax.fori_loop(0, n_ref.shape[0] // BQ, body, 0)


def fill_bias(base_ref, bias_scr):
    span = base_ref.shape[1]
    for h in range(3):
        row = jnp.broadcast_to(base_ref[h:h + 1, :], (BQ, span))
        bias_scr[h] = pltpu.roll(row, 0, 1, stride=1, stride_axis=0)[:, :768]


def softmax_parts(s):
    m = jnp.max(s, axis=1, keepdims=True)
    e = jnp.exp(s - m)
    rl = 1.0 / jnp.sum(e, axis=1, keepdims=True)
    return e, m, rl


SELF_W = (256, 384, 512, 768)
CROSS_W = (128, 256, 512)


def self_scores(q, k, bias, ds, q0, width):
    s = dg(q, k, NT) + bias
    kpos = lax.broadcasted_iota(jnp.int32, (BQ, width), 1) + (q0 + BQ - width)
    return jnp.where(kpos >= ds, s, NEG_FILL)


def self_fwd_kernel(win, n_ref, w_ref, ds_ref, base_ref, q3, k3, v3, ctx_ref, st_ref, out_ref, bias_scr, c3):
    fill_bias(base_ref, bias_scr)
    project(n_ref, w_ref[0:192, :], q3)
    project(n_ref, w_ref[192:384, :], k3)
    project(n_ref, w_ref[384:576, :], v3)

    def block(i, _):
        q0 = pl.multiple_of(i * BQ, BQ)
        rows = pl.ds(q0, BQ)

        @pl.when(win[i] == 0)
        def _():
            ctx_ref[rows, :] = jnp.zeros((BQ, 192), bf16)
            st_ref[rows, :] = jnp.zeros((BQ, 8), f32)

        for n, width in enumerate(SELF_W):
            @pl.when(win[i] == n + 1)
            def _(width=width):
                keys = pl.ds(pl.multiple_of(q0 + (BQ - width), 128), width)
                ds = ds_ref[rows, :]
                for h in range(3):
                    s = self_scores(q3[h, rows, :], k3[h, keys, :], bias_scr[h, :, 768 - width:], ds, q0, width)
                    e, m, rl = softmax_parts(s)
                    p = (e * rl).astype(bf16)
                    c = dg(p, v3[h, keys, :], NN)
                    c = jnp.where(ds < 4096, c, 0.0)
                    ctx_ref[rows, h * 64:(h + 1) * 64] = c.astype(bf16)
                    st_ref[rows, h:h + 1] = m
                    st_ref[rows, h + 3:h + 4] = rl
        out_ref[rows, :] = dg(ctx_ref[rows, :], w_ref[576:768, :], NN)
        return 0
    lax.fori_loop(0, n_ref.shape[0] // BQ, block, 0)


def params(flops, byts, vmem=48):
    return dict(compiler_params=pltpu.CompilerParams(vmem_limit_bytes=vmem << 20),
                cost_estimate=pl.CostEstimate(flops=int(flops), bytes_accessed=int(byts), transcendentals=0))


def self_fwd(win, n, w, ds, base):
    R = n.shape[0]
    sd = jax.ShapeDtypeStruct
    return pl.pallas_call(
        self_fwd_kernel,
        in_specs=[SM, VM, VM, VM, VM],
        out_specs=[VM] * 6,
        out_shape=[sd((3, R, 64), bf16)] * 3 + [sd((R, 192), bf16), sd((R, 8), f32), sd((R, 768), f32)],
        scratch_shapes=[pltpu.VMEM((3, BQ, 768), f32), pltpu.VMEM((3, R, 64), f32)],
        name="self_fwd", **params(6e9, 10e6))(win, n, w, ds, base)


def diagonal_sums(scr, h):
    span = scr.shape[2]
    slabs = [scr[h, 8 * a:8 * a + 8, :] for a in range(BQ // 8)]
    step = 8
    while len(slabs) > 1:
        slabs = [slabs[j] + pltpu.roll(slabs[j + 1], span - step, 1) for j in range(0, len(slabs), 2)]
        step *= 2
    acc = slabs[0]
    row = lax.broadcasted_iota(jnp.int32, acc.shape, 0)
    for bit in (1, 2, 4):
        acc = jnp.where((row & bit) > 0, pltpu.roll(acc, span - bit, 1), acc)
    return jnp.sum(acc, axis=0, keepdims=True)


def self_bwd_kernel(win, b_ref, n_ref, w_ref, ds_ref, base_ref, q3, k3, v3, ctx_ref, st_ref,
                    dw_ref, dn_ref, db_ref, bias_scr, dbias_scr, g3, dq, dk, dv):
    R = n_ref.shape[0]
    fill_bias(base_ref, bias_scr)
    dbias_scr[...] = jnp.zeros(dbias_scr.shape, f32)
    dk[...] = jnp.zeros(dk.shape, f32)
    dv[...] = jnp.zeros(dv.shape, f32)

    def gpart(i, _):
        rows = blk(i)
        g = dg(b_ref[rows, :], w_ref[576:768, :], NT).astype(bf16)
        g = jnp.where(ds_ref[rows, :] < 4096, g, jnp.zeros_like(g))
        put_heads(g3, rows, g)
        return 0
    lax.fori_loop(0, R // BQ, gpart, 0)

    def block(i, _):
        q0 = pl.multiple_of(i * BQ, BQ)
        rows = pl.ds(q0, BQ)

        @pl.when(win[i] == 0)
        def _():
            dq[rows, :] = jnp.zeros((BQ, 192), bf16)

        for n, width in enumerate(SELF_W):
            @pl.when(win[i] == n + 1)
            def _(width=width):
                keys = pl.ds(pl.multiple_of(q0 + (BQ - width), 128), width)
                ds = ds_ref[rows, :]
                for h in range(3):
                    q = q3[h, rows, :]
                    k = k3[h, keys, :]
                    g = g3[h, rows, :]
                    s = self_scores(q, k, bias_scr[h, :, 768 - width:], ds, q0, width)
                    p = jnp.exp(s - st_ref[rows, h:h + 1]) * st_ref[rows, h + 3:h + 4]
                    wg = dg(g, v3[h, keys, :], NT)
                    inner = jnp.sum(p * wg, axis=1, keepdims=True)
                    sg = (p * (wg - inner)).astype(bf16)
                    dv[h, keys, :] += dg(p.astype(bf16), g, TN)
                    dk[h, keys, :] += dg(sg, q, TN)
                    dq[rows, h * 64:(h + 1) * 64] = dg(sg, k, NN).astype(bf16)
                    dbias_scr[h, :, 768 - width:768] += sg.astype(f32)
        return 0
    lax.fori_loop(0, R // BQ, block, 0)
    finish_bwd(dq, dk, dv, n_ref, n_ref, b_ref, ctx_ref, w_ref, dw_ref)

    def back(i, _):
        rows = blk(i)
        dkb = jnp.concatenate([dk[h, rows, :] for h in range(3)], axis=1).astype(bf16)
        dvb = jnp.concatenate([dv[h, rows, :] for h in range(3)], axis=1).astype(bf16)
        dn_ref[rows, :] = (dg(dq[rows, :], w_ref[0:192, :], NN) + dg(dkb, w_ref[192:384, :], NN)
                           + dg(dvb, w_ref[384:576, :], NN))
        return 0
    lax.fori_loop(0, R // BQ, back, 0)
    for h in range(3):
        db_ref[h:h + 1, :] = diagonal_sums(dbias_scr, h)


def finish_bwd(dq, dk, dv, nq_ref, nk_ref, b_ref, ctx_ref, w_ref, dw_ref):
    dw_ref[0:192, :] = dg(dq[...], nq_ref[...], TN).astype(dw_ref.dtype)
    for slot, src in ((1, dk), (2, dv)):
        wide = jnp.concatenate([src[h] for h in range(3)], axis=1).astype(bf16)
        dw_ref[192 * slot:192 * slot + 192, :] = dg(wide, nk_ref[...], TN).astype(dw_ref.dtype)
    dw_ref[576:768, :] = dg(ctx_ref[...], b_ref[...], TN).astype(dw_ref.dtype)


def self_bwd(win, b, n, w, ds, base, q3, k3, v3, ctx, st):
    R = n.shape[0]
    sd = jax.ShapeDtypeStruct
    return pl.pallas_call(
        self_bwd_kernel,
        in_specs=[SM] + [VM] * 10,
        out_specs=[VM] * 3,
        out_shape=[sd((768, 768), bf16), sd((R, 768), f32), sd((3, 1024), f32)],
        scratch_shapes=[pltpu.VMEM((3, BQ, 768), f32), pltpu.VMEM((3, BQ, 1024), f32), pltpu.VMEM((3, R, 64), bf16),
                        pltpu.VMEM((R, 192), bf16), pltpu.VMEM((3, R, 64), f32), pltpu.VMEM((3, R, 64), f32)],
        name="self_bwd", **params(14e9, 12e6))(win, b, n, w, ds, base, q3, k3, v3, ctx, st)


def cross_scores(q, k, tseg, sseg):
    return jnp.where(tseg == sseg, dg(q, k, NT), NEG_FILL)


def cross_kv_kernel(m_ref, w_ref, k3, v3):
    project(m_ref, w_ref[192:384, :], k3)
    project(m_ref, w_ref[384:576, :], v3)


def cross_kv(mem, w):
    sd = jax.ShapeDtypeStruct
    M = mem.shape[0]
    return pl.pallas_call(cross_kv_kernel, in_specs=[VM, VM], out_specs=[VM, VM],
                          out_shape=[sd((3, M, 64), bf16)] * 2, name="cross_kv", **params(1.5e9, 3e6, 32))(mem, w)


def cross_fwd_kernel(win, n_ref, w_ref, tseg_ref, sseg_ref, k3, v3, q3, ctx_ref, st_ref, out_ref):
    project(n_ref, w_ref[0:192, :], q3)

    def block(i, _):
        rows = blk(i)

        @pl.when(win[0, i] == 0)
        def _():
            ctx_ref[rows, :] = jnp.zeros((BQ, 192), bf16)
            st_ref[rows, :] = jnp.zeros((BQ, 8), f32)

        for n, width in enumerate(CROSS_W):
            @pl.when(win[0, i] == n + 1)
            def _(width=width):
                keys = pl.ds(pl.multiple_of(win[1, i], 128), width)
                tseg = tseg_ref[rows, :]
                sseg = sseg_ref[:, keys]
                for h in range(3):
                    s = cross_scores(q3[h, rows, :], k3[h, keys, :], tseg, sseg)
                    e, m, rl = softmax_parts(s)
                    c = dg((e * rl).astype(bf16), v3[h, keys, :], NN)
                    c = jnp.where(tseg > 0, c, 0.0)
                    ctx_ref[rows, h * 64:(h + 1) * 64] = c.astype(bf16)
                    st_ref[rows, h:h + 1] = m
                    st_ref[rows, h + 3:h + 4] = rl
        out_ref[rows, :] = dg(ctx_ref[rows, :], w_ref[576:768, :], NN)
        return 0
    lax.fori_loop(0, n_ref.shape[0] // BQ, block, 0)


def cross_fwd(win, n, w, tseg, sseg, k3, v3):
    R = n.shape[0]
    sd = jax.ShapeDtypeStruct
    return pl.pallas_call(
        cross_fwd_kernel,
        in_specs=[SM] + [VM] * 6, out_specs=[VM] * 4,
        out_shape=[sd((3, R, 64), bf16), sd((R, 192), bf16), sd((R, 8), f32), sd((R, 768), f32)],
        name="cross_fwd", **params(3e9, 8e6, 32))(win, n, w, tseg, sseg, k3, v3)


def cross_bwd_kernel(win, b_ref, n_ref, m_ref, w_ref, tseg_ref, sseg_ref, q3, k3, v3, ctx_ref, st_ref,
                     dw_ref, dn_ref, dm_ref, g3, dq, dk, dv):
    R = n_ref.shape[0]
    dk[...] = jnp.zeros(dk.shape, f32)
    dv[...] = jnp.zeros(dv.shape, f32)

    def block(i, _):
        rows = blk(i)
        tseg = tseg_ref[rows, :]
        g = dg(b_ref[rows, :], w_ref[576:768, :], NT).astype(bf16)
        g = jnp.where(tseg > 0, g, jnp.zeros_like(g))
        put_heads(g3, pl.ds(0, BQ), g)

        @pl.when(win[0, i] == 0)
        def _():
            dq[rows, :] = jnp.zeros((BQ, 192), bf16)

        for n, width in enumerate(CROSS_W):
            @pl.when(win[0, i] == n + 1)
            def _(width=width):
                keys = pl.ds(pl.multiple_of(win[1, i], 128), width)
                sseg = sseg_ref[:, keys]
                for h in range(3):
                    q = q3[h, rows, :]
                    k = k3[h, keys, :]
                    gh = g3[h]
                    s = cross_scores(q, k, tseg, sseg)
                    p = jnp.exp(s - st_ref[rows, h:h + 1]) * st_ref[rows, h + 3:h + 4]
                    wg = dg(gh, v3[h, keys, :], NT)
                    inner = jnp.sum(p * wg, axis=1, keepdims=True)
                    sg = (p * (wg - inner)).astype(bf16)
                    dv[h, keys, :] += dg(p.astype(bf16), gh, TN)
                    dk[h, keys, :] += dg(sg, q, TN)
                    dq[rows, h * 64:(h + 1) * 64] = dg(sg, k, NN).astype(bf16)
        dn_ref[rows, :] = dg(dq[rows, :], w_ref[0:192, :], NN)
        return 0
    lax.fori_loop(0, R // BQ, block, 0)
    finish_bwd(dq, dk, dv, n_ref, m_ref, b_ref, ctx_ref, w_ref, dw_ref)

    def back(i, _):
        rows = blk(i)
        dkb = jnp.concatenate([dk[h, rows, :] for h in range(3)], axis=1).astype(bf16)
        dvb = jnp.concatenate([dv[h, rows, :] for h in range(3)], axis=1).astype(bf16)
        dm_ref[rows, :] = dg(dkb, w_ref[192:384, :], NN) + dg(dvb, w_ref[384:576, :], NN)
        return 0
    lax.fori_loop(0, m_ref.shape[0] // BQ, back, 0)


def cross_bwd(win, b, n, mem, w, tseg, sseg, q3, k3, v3, ctx, st):
    R, M = n.shape[0], mem.shape[0]
    sd = jax.ShapeDtypeStruct
    return pl.pallas_call(
        cross_bwd_kernel,
        in_specs=[SM] + [VM] * 11, out_specs=[VM] * 3,
        out_shape=[sd((768, 768), bf16), sd((R, 768), f32), sd((M, 768), f32)],
        scratch_shapes=[pltpu.VMEM((3, BQ, 64), bf16), pltpu.VMEM((R, 192), bf16), pltpu.VMEM((3, M, 64), f32),
                        pltpu.VMEM((3, M, 64), f32)],
        name="cross_bwd", **params(8e9, 12e6, 40))(win, b, n, mem, w, tseg, sseg, q3, k3, v3, ctx, st)


def bucket_of(spread):
    exact_count = BUCKETS // 2
    if spread < exact_count:
        return spread
    larger = exact_count + math.floor(
        math.log(spread / exact_count) / math.log(MAXDIST / exact_count) * (BUCKETS - exact_count)
    )
    return min(larger, BUCKETS - 1)


def bias_lanes():
    lane = np.arange(1024)
    distance = 512 - np.where(lane < 768, lane, lane - 1024)
    buckets = np.array([bucket_of(max(int(n), 0)) for n in distance], np.int32)
    return distance, buckets


def base_rows(table):
    distance, buckets = bias_lanes()
    onehot = (jnp.asarray(buckets)[None, :] == jnp.arange(BUCKETS)[:, None]).astype(f32)
    rows = lax.dot_general(table, onehot, TN, precision=lax.Precision.HIGHEST, preferred_element_type=f32)
    return jnp.where(jnp.asarray(distance >= 0)[None, :], rows, NEG_FILL)


def bucket_sums(lane_sums):
    distance, buckets = bias_lanes()
    onehot = (jnp.asarray(buckets)[:, None] == jnp.arange(BUCKETS)[None, :]) & jnp.asarray(distance >= 0)[:, None]
    return lax.dot_general(
        onehot.astype(f32), lane_sums, (((0,), (1,)), ((), ())), precision=lax.Precision.HIGHEST,
        preferred_element_type=f32)


def running_sum(lengths):
    tri = np.tril(np.ones((lengths.shape[0],) * 2, bool))
    return jnp.sum(jnp.where(tri, lengths[None, :], 0), axis=1)


def slot_layout(tl, sl):
    ends = running_sum(tl)
    starts = ends - tl
    total = jnp.sum(tl)
    pos = jnp.arange(SLOT, dtype=jnp.int32)
    past = pos[:, None] >= ends[None, :]
    live = pos < total
    tseg = jnp.where(live, jnp.sum(past.astype(jnp.int32), axis=1) + 1, -1)
    doc_start = jnp.where(live, jnp.max(jnp.where(past, ends[None, :], 0), axis=1), 1 << 20)
    sends = running_sum(sl)
    spos = jnp.arange(MEM, dtype=jnp.int32)
    sseg = jnp.where(spos < jnp.sum(sl), jnp.sum((spos[:, None] >= sends[None, :]).astype(jnp.int32), axis=1) + 1, 0)
    q0 = jnp.arange(0, SLOT, BQ, dtype=jnp.int32)
    alive = q0 < total
    first = jnp.max(jnp.where(q0[:, None] >= ends[None, :], ends[None, :], 0), axis=1)
    need = q0 + BQ - (first // 128) * 128
    swin = 1 + sum((need > width).astype(jnp.int32) for width in SELF_W[:-1])
    swin = jnp.where(alive, swin, 0)
    last = jnp.minimum(q0 + BQ - 1, total - 1)
    low = jnp.sum(jnp.where(ends[None, :] <= q0[:, None], sl[None, :], 0), axis=1)
    high = jnp.sum(jnp.where(starts[None, :] <= last[:, None], sl[None, :], 0), axis=1)
    at1 = (low // 128) * 128
    at2 = jnp.minimum(at1, MEM - 256)
    fits1 = high - at1 <= 128
    fits2 = high - at2 <= 256
    cwin = jnp.where(fits1, 1, jnp.where(fits2, 2, 3))
    cat = jnp.where(fits1, at1, jnp.where(fits2, at2, 0))
    cross_win = jnp.stack((jnp.where(alive, cwin, 0), jnp.where(alive, cat, 0)))
    return tseg[:, None], doc_start[:, None], sseg[None, :], swin, cross_win


def rms_normed(rows_in, gain_row):
    inverse_rms = lax.rsqrt(jnp.mean(rows_in * rows_in, axis=-1, keepdims=True) + NORM_EPS)
    return (rows_in * inverse_rms * gain_row[None, :]).astype(bf16)


def rms_back(rows_in, gain_row, grad):
    r = lax.rsqrt(jnp.mean(rows_in * rows_in, axis=-1, keepdims=True) + NORM_EPS)
    scaled = grad * gain_row[None, :]
    back = r * scaled - rows_in * (r * r * r) * jnp.mean(scaled * rows_in, axis=-1, keepdims=True)
    return back, jnp.sum(grad * rows_in * r, axis=0)


def gated_unit(gate_in, up_in):
    return jax.nn.gelu(gate_in, approximate=True) * up_in


CORE = [(i, i ^ 1) for i in range(4)]
CHIP = [(i, i ^ 2) for i in range(4)]


def swap_core(v):
    return lax.ppermute(v, "tensor", CORE)


def swap_chip(v):
    return lax.ppermute(v, "tensor", CHIP)


def swap_dp(v, bit):
    return lax.ppermute(v, "dp", [(i, i ^ (1 << bit)) for i in range(lax.axis_size("dp"))])


def dp_bits():
    return int(math.log2(lax.axis_size("dp")))


def add16(a, b):
    return (a.astype(f32) + b.astype(f32)).astype(bf16)


def reduce_grads(own, away):
    d = lax.axis_index("dp")
    total = add16(own, swap_chip(away))
    for bit in range(dp_bits()):
        mine = lax.shift_right_logical(d, bit) & 1
        halves = total.reshape((2, total.shape[0] // 2) + total.shape[1:])
        sent = swap_dp(lax.dynamic_index_in_dim(halves, 1 - mine, 0, False), bit)
        total = add16(lax.dynamic_index_in_dim(halves, mine, 0, False), sent)
    for bit in reversed(range(dp_bits())):
        mine = lax.shift_right_logical(d, bit) & 1
        other = swap_dp(total, bit)
        total = jnp.where(mine == 0, jnp.concatenate((total, other)), jnp.concatenate((other, total)))
    return total.astype(f32)


def sum_small(v, core):
    if core:
        v = v + swap_core(v)
    v = v + swap_chip(v)
    for bit in range(dp_bits()):
        v = v + swap_dp(v, bit)
    return v


def after(value, *earlier):
    return lax.optimization_barrier((value,) + earlier)[0]


def on_device(tokens, memory, cotangent, norm_gains, query_weight, keyvalue_weight, output_weight, bias_table,
              inner_weight, outer_weight, target_lengths, source_lengths):
    t = lax.axis_index("tensor")
    core = t & 1
    slot = lax.shift_right_logical(t, 1)
    tl = lax.dynamic_index_in_dim(target_lengths, slot, 0, False)
    sl = lax.dynamic_index_in_dim(source_lengths, slot, 0, False)
    tseg, doc_start, sseg, swin, cwin = slot_layout(tl, sl)

    def joined(rows):
        other = swap_core(rows)
        return jnp.where(core == 0, jnp.concatenate((rows, other)), jnp.concatenate((other, rows)))

    def mine_of(rows):
        half = rows.shape[0] // 2
        return lax.dynamic_slice_in_dim(rows, core * half, half, 0)

    def theirs_of(rows):
        half = rows.shape[0] // 2
        return lax.dynamic_slice_in_dim(rows, (1 - core) * half, half, 0)

    def scattered(rows):
        return mine_of(rows) + swap_core(theirs_of(rows))

    stacks = [
        jnp.concatenate((query_weight[i].T, keyvalue_weight[i, 0].T, keyvalue_weight[i, 1].T, output_weight[i]))
        for i in range(2)
    ]
    away_self = swap_chip(stacks[0])
    away_table = swap_chip(bias_table)
    away_cross = swap_chip(after(stacks[1], away_self))
    away_inner = swap_chip(after(inner_weight, away_cross))
    away_outer = swap_chip(after(outer_weight, away_inner))
    wself = (stacks[0], away_self)
    wcross = (stacks[1], away_cross)
    winner = (inner_weight, away_inner)
    wouter = (outer_weight, away_outer)
    bases = (base_rows(bias_table), base_rows(away_table))

    residual = joined(tokens).astype(f32)
    mem = joined(memory)
    cot = joined(cotangent)
    n1 = rms_normed(residual, norm_gains[0])
    fs = [self_fwd(swin, n1, wself[p], doc_start, bases[p]) for p in range(2)]
    part = fs[0][5] + fs[1][5]
    after_self = residual + (part + swap_core(part))
    kv = [cross_kv(mem, wcross[p]) for p in range(2)]
    n2 = rms_normed(after_self, norm_gains[1])
    fc = [cross_fwd(cwin, n2, wcross[p], tseg, sseg, *kv[p]) for p in range(2)]
    part = fc[0][3] + fc[1][3]
    after_cross = after_self + (part + swap_core(part))
    n3 = rms_normed(after_cross, norm_gains[2])

    outs, thirds, keep = [], [], []
    for p in range(2):
        wi, wo = winner[p], wouter[p]
        gate = dg(n3, wi[0], NN)
        up = dg(n3, wi[1], NN)
        hidden, pull = jax.vjp(gated_unit, gate, up)
        hidden = hidden.astype(bf16)
        gate_grad, up_grad = pull(dg(cot, wo, NT))
        gate_grad, up_grad = gate_grad.astype(bf16), up_grad.astype(bf16)
        outs.append(dg(hidden, wo, NN))
        thirds.append(dg(gate_grad, wi[0], NT) + dg(up_grad, wi[1], NT))
        keep.append((hidden, gate_grad, up_grad))
    part = thirds[0] + thirds[1]
    third_grad = part + swap_core(part)
    output_rows = (mine_of(after_cross) + scattered(outs[0] + outs[1])).astype(bf16)
    dinner = [jnp.concatenate((dg(n3, keep[p][1], TN), dg(n3, keep[p][2], TN))).astype(bf16) for p in range(2)]
    douter = [dg(keep[p][0], cot, TN).astype(bf16) for p in range(2)]
    inner_sum = reduce_grads(*dinner).reshape(inner_weight.shape)
    outer_sum = reduce_grads(*douter)

    back, gain2 = rms_back(after_cross, norm_gains[2], third_grad)
    cross_out_grad = cot.astype(f32) + back
    branch = cross_out_grad.astype(bf16)
    bc = [None, None]
    for p in (1, 0):
        bc[p] = cross_bwd(cwin, branch, n2, mem, wcross[p], tseg, sseg, fc[p][0], *kv[p], *fc[p][1:3])
    part = bc[0][1] + bc[1][1]
    second_grad = part + swap_core(part)
    memory_grad = scattered(bc[0][2] + bc[1][2])
    cross_sum = reduce_grads(bc[0][0], bc[1][0])

    back, gain1 = rms_back(after_self, norm_gains[1], second_grad)
    self_out_grad = cross_out_grad + back
    branch = self_out_grad.astype(bf16)
    bs = [None, None]
    for p in (1, 0):
        bs[p] = self_bwd(swin, branch, n1, wself[p], doc_start, bases[p], *fs[p][:5])
    self_sum = reduce_grads(bs[0][0], bs[1][0])
    first_grad = scattered(bs[0][1] + bs[1][1])
    back, gain0 = rms_back(tokens.astype(f32), norm_gains[0], first_grad)
    tokens_grad = mine_of(self_out_grad) + back
    lanes = bs[0][2] + swap_chip(bs[1][2])
    for bit in range(dp_bits()):
        lanes = lanes + swap_dp(lanes, bit)
    table_sum = bucket_sums(lanes)
    gain0 = gain0 + swap_core(gain0)
    gains_total = sum_small(jnp.stack((gain0, gain1, gain2)), False)

    sq_self = (self_sum * self_sum).reshape(4, -1, D)
    sq_cross = (cross_sum * cross_sum).reshape(4, -1, D)
    sq_inner = inner_sum * inner_sum
    sq_outer = outer_sum * outer_sum
    ms, mc = jnp.sum(sq_self, axis=1), jnp.sum(sq_cross, axis=1)
    model_part = jnp.concatenate(
        (ms[:1], mc[:1], ms[1:3], mc[1:3], jnp.sum(sq_inner, axis=2), ms[3:], mc[3:], jnp.sum(sq_outer, axis=0)[None]))
    model_total = model_part + swap_core(model_part)
    model_total = model_total + swap_chip(model_total)
    hidden_units = outer_weight.shape[0] * lax.axis_size("tensor")
    divisors = jnp.array([D] * 6 + [hidden_units] * 2 + [D] * 2 + [hidden_units], f32)
    model_stats = model_total / divisors[:, None]
    hs, hc = jnp.sum(sq_self, axis=2) / D, jnp.sum(sq_cross, axis=2) / D
    head_stats = jnp.concatenate((hs[:1], hc[:1], hs[1:3], hc[1:3]))
    projection_stats = jnp.stack((hs[3], hc[3]))
    unit_stats = jnp.concatenate((jnp.sum(sq_inner, axis=1), jnp.sum(sq_outer, axis=1)[None])) / D
    sw = self_sum.reshape(4, -1, D)
    cw = cross_sum.reshape(4, -1, D)
    query_grad = jnp.stack((sw[0].T, cw[0].T))
    keyvalue_grad = jnp.stack((jnp.stack((sw[1].T, sw[2].T)), jnp.stack((cw[1].T, cw[2].T))))
    output_grad = jnp.stack((sw[3], cw[3]))
    return (output_rows, tokens_grad, memory_grad, gains_total, query_grad, keyvalue_grad, output_grad, table_sum,
            inner_sum, outer_sum, model_stats, head_stats, projection_stats, unit_stats)


def solution(mesh):
    rows = P(("dp", "tensor"), None)
    in_specs = (rows, rows, rows, P(), P(None, None, "tensor"), P(None, None, None, "tensor"), P(None, "tensor", None),
                P(None, "tensor"), P(None, None, "tensor"), P("tensor", None), P("dp", None), P("dp", None))
    out_specs = (rows, rows, rows, P(), P(None, None, "tensor"), P(None, None, None, "tensor"),
                 P(None, "tensor", None), P(None, "tensor"), P(None, None, "tensor"), P("tensor", None), P(),
                 P(None, "tensor"), P(None, "tensor"), P(None, "tensor"))
    return jax.shard_map(on_device, mesh=mesh, in_specs=in_specs, out_specs=out_specs, check_vma=False)
```

```python
import math

import jax
import jax.numpy as jnp
import numpy as np
from jax import lax
from jax.experimental import pallas as pl
from jax.experimental.pallas import tpu as pltpu
from jax.sharding import PartitionSpec as P

D = 768
DH = 64
BUCKETS = 32
MAXDIST = 128
SLOT = 1024
MEM = 512
NORM_EPS = 1e-06
NEG_FILL = -1e30
DEAD = 1 << 20
BQ = 256
COST = 0.02
VM = pl.BlockSpec(memory_space=pltpu.VMEM)
SM = pl.BlockSpec(memory_space=pltpu.SMEM)
NT = (((1,), (1,)), ((), ()))
NN = (((1,), (0,)), ((), ()))
TN = (((0,), (0,)), ((), ()))
f32, bf16, i32 = jnp.float32, jnp.bfloat16, jnp.int32
SELF_W = (256, 384, 512, 768)
CROSS_W = (128, 256, 512)
sd = jax.ShapeDtypeStruct


def dg(a, b, dims):
    return lax.dot_general(a, b, dims, preferred_element_type=f32)


def blk(i):
    return pl.ds(pl.multiple_of(i * BQ, BQ), BQ)


def loop(count, body):
    def step(i, carry):
        body(i)
        return carry
    lax.fori_loop(0, count, step, 0)


def call(kernel, name, args, outs, scratch=(), scalars=0, vmem=28, flops=1e9, out_specs=None):
    byts = sum(int(np.prod(a.shape)) * a.dtype.itemsize for a in tuple(args) + tuple(outs))
    return pl.pallas_call(
        kernel,
        in_specs=[SM] * scalars + [VM] * (len(args) - scalars),
        out_specs=list(out_specs) if out_specs else [VM] * len(outs),
        out_shape=list(outs),
        scratch_shapes=list(scratch),
        name=name,
        compiler_params=pltpu.CompilerParams(vmem_limit_bytes=vmem << 20),
        cost_estimate=pl.CostEstimate(flops=int(flops * COST), bytes_accessed=int(byts * COST), transcendentals=0),
    )(*args)


def bucket_of(spread):
    exact_count = BUCKETS // 2
    if spread < exact_count:
        return spread
    larger = exact_count + math.floor(
        math.log(spread / exact_count) / math.log(MAXDIST / exact_count) * (BUCKETS - exact_count)
    )
    return min(larger, BUCKETS - 1)


def bucket_starts():
    buckets = [bucket_of(n) for n in range(SLOT)]
    return [next(n for n in range(SLOT + 1) if n == SLOT or buckets[n] >= b) for b in range(BUCKETS)]


def layout_kernel(slot, tl_ref, sl_ref, ds_ref, tseg_ref, sseg_ref, swin, cwin):
    s = slot[0]
    docs = tl_ref.shape[1]
    tl = [tl_ref[s, j] for j in range(docs)]
    sl = [sl_ref[s, j] for j in range(docs)]
    ends, sends = [], []
    te, se = jnp.int32(0), jnp.int32(0)
    for j in range(docs):
        te, se = te + tl[j], se + sl[j]
        ends.append(te)
        sends.append(se)
    pos = lax.broadcasted_iota(i32, ds_ref.shape, 0)
    spos = lax.broadcasted_iota(i32, sseg_ref.shape, 1)
    start, seg, mseg = jnp.zeros_like(pos), jnp.ones_like(pos), jnp.ones_like(spos)
    for j in range(docs):
        past = pos >= ends[j]
        start = jnp.where(past, ends[j], start)
        seg = seg + past.astype(i32)
        mseg = mseg + (spos >= sends[j]).astype(i32)
    live = pos < te
    ds_ref[...] = jnp.where(live, start, DEAD)
    tseg_ref[...] = jnp.where(live, seg, -1)
    sseg_ref[...] = jnp.where(spos < se, mseg, 0)
    for i in range(SLOT // BQ):
        q0 = i * BQ
        first, low, high = jnp.int32(0), jnp.int32(0), jnp.int32(0)
        last = jnp.minimum(q0 + BQ - 1, te - 1)
        for j in range(docs):
            before = ends[j] <= q0
            first = jnp.where(before, ends[j], first)
            low = low + jnp.where(before, sl[j], 0)
            high = high + jnp.where(ends[j] - tl[j] <= last, sl[j], 0)
        need = q0 + BQ - lax.shift_left(lax.shift_right_logical(first, 7), 7)
        width = jnp.int32(1)
        for w in SELF_W[:-1]:
            width = width + jnp.where(need > w, 1, 0)
        swin[i] = jnp.where(q0 < te, width, 0)
        at1 = lax.shift_left(lax.shift_right_logical(low, 7), 7)
        at2 = jnp.minimum(at1, MEM - 256)
        one, two = high - at1 <= 128, high - at2 <= 256
        cwin[0, i] = jnp.where(q0 < te, jnp.where(one, 1, jnp.where(two, 2, 3)), 0)
        cwin[1, i] = jnp.where(one, at1, jnp.where(two, at2, 0))


def slot_layout(slot, tl, sl):
    return call(layout_kernel, "layout", (slot, tl, sl),
                (sd((SLOT, 1), i32), sd((SLOT, 1), i32), sd((1, MEM), i32), sd((4,), i32), sd((2, 4), i32)),
                scalars=3, flops=1e6, out_specs=(VM, VM, VM, SM, SM))


def pack_kernel(bits, q_ref, kv_ref, o_ref, *outs):
    for which in range(2):
        w_ref, half_ref = outs[2 * which:2 * which + 2]
        w_ref[0:192, :] = q_ref[which].T
        w_ref[192:384, :] = kv_ref[which, 0].T
        w_ref[384:576, :] = kv_ref[which, 1].T
        w_ref[576:768, :] = o_ref[which]
        half_ref[...] = half_rows(w_ref, bits[0])


def packed(bits, q, kv, o):
    return call(pack_kernel, "pack", (bits, q, kv, o), (sd((768, 768), bf16), sd((384, 768), bf16)) * 2, (), 1, flops=1e6)


def norm_kernel(x_ref, gain_ref, n_ref):
    x = x_ref[...].astype(f32)
    r = lax.rsqrt(jnp.mean(x * x, axis=-1, keepdims=True) + NORM_EPS)
    n_ref[...] = (x * r * gain_ref[...]).astype(bf16)


def norm_rows(x, gain):
    return call(norm_kernel, "norm", (x, gain), (sd(x.shape, bf16),), flops=1e6)[0]


def add_norm_kernel(x_ref, a_ref, b_ref, gain_ref, y_ref, n_ref):
    y = x_ref[...].astype(f32) + (a_ref[...] + b_ref[...])
    y_ref[...] = y
    r = lax.rsqrt(jnp.mean(y * y, axis=-1, keepdims=True) + NORM_EPS)
    n_ref[...] = (y * r * gain_ref[...]).astype(bf16)


def add_norm(x, a, b, gain):
    return call(add_norm_kernel, "add_norm", (x, a, b, gain), (sd(x.shape, f32), sd(x.shape, bf16)), flops=1e6)


def norm_back_kernel(terms):
    def kernel(v_ref, gain_ref, up_ref, *refs):
        total_ref, branch_ref, sum_ref = refs[terms:]
        grad = refs[0][...].astype(f32)
        for ref in refs[1:terms]:
            grad = grad + ref[...].astype(f32)
        v = v_ref[...].astype(f32)
        r = lax.rsqrt(jnp.mean(v * v, axis=-1, keepdims=True) + NORM_EPS)
        scaled = grad * gain_ref[...]
        back = r * scaled - v * ((r * r * r) * jnp.mean(scaled * v, axis=-1, keepdims=True))
        total = up_ref[...].astype(f32) + back
        total_ref[...] = total
        branch_ref[...] = total.astype(bf16)
        sum_ref[...] = jnp.sum(grad * v * r, axis=0, keepdims=True)
    return kernel


def norm_back(v, gain, up, *grads):
    return call(norm_back_kernel(len(grads)), "norm_back", (v, gain, up) + grads,
                (sd(v.shape, f32), sd(v.shape, bf16), sd((1, v.shape[1]), f32)), flops=1e6)


LANES = (slice(0, 128), slice(0, 128), slice(128, 192))


def head_of(rows128, h):
    if h == 2:
        return rows128
    lane = lax.broadcasted_iota(i32, rows128.shape, 1)
    return jnp.where((lane < 64) == (h == 0), rows128, jnp.zeros_like(rows128))


def pair_of(first, second):
    lane = lax.broadcasted_iota(i32, first.shape, 1)
    return jnp.where(lane < 64, first, second)


def half_rows(ref, which):
    half = ref.shape[0] // 2
    return ref[pl.ds(pl.multiple_of(which * half, half), half), :]


def join_rows(core, mine_ref, theirs_ref, all_ref):
    half = mine_ref.shape[0]
    at = pl.multiple_of(core * half, half)
    all_ref[pl.ds(at, half), :] = mine_ref[...]
    all_ref[pl.ds(pl.multiple_of(half - at, half), half), :] = theirs_ref[...]


def out_split(core, mine_ref, theirs_ref, before, value_of):
    for pos, ref in enumerate((mine_ref, theirs_ref)):
        value = value_of(core if pos == 0 else 1 - core)
        ref[...] = value if before is None else value + before[pos][...]


def fill_bias(table, bias_scr):
    lane = lax.broadcasted_iota(i32, (1, 1024), 1)
    distance = 512 - jnp.where(lane < 768, lane, lane - 1024)
    for h in range(3):
        row = jnp.full((1, 1024), table[0, h], f32)
        for b, first in enumerate(bucket_starts()):
            if b > 0:
                row = jnp.where(distance >= first, table[b, h], row)
        row = jnp.where(distance < 0, NEG_FILL, row)
        wide = jnp.broadcast_to(row, (BQ, 1024))
        bias_scr[h] = pltpu.roll(wide, 0, 1, stride=1, stride_axis=0)[:, :768]


def attend(scores, v_ref, keys, rows, live, ctx_ref, st_ref):
    s = [scores(h) for h in range(3)]
    m = [jnp.max(x, axis=1, keepdims=True) for x in s]
    e = [jnp.exp(x - y) for x, y in zip(s, m)]
    total = [jnp.sum(x, axis=1, keepdims=True) for x in e]
    p = [(x * (1.0 / y)).astype(bf16) for x, y in zip(e, total)]
    c = [dg(p[h], v_ref[keys, LANES[h]], NN) for h in range(3)]
    ctx_ref[rows, 0:128] = jnp.where(live, pair_of(c[0], c[1]), 0.0).astype(bf16)
    ctx_ref[rows, 128:192] = jnp.where(live, c[2], 0.0).astype(bf16)
    for h in range(3):
        st_ref[rows, h:h + 1] = m[h] + jnp.log(total[h])


def attend_back(scores, q_ref, k_ref, v_ref, g, keys, rows, st_ref, dq, dk, dv, extra):
    gs = [head_of(g[:, LANES[h]], h) for h in range(3)]
    s = [scores(h) for h in range(3)]
    wg = [dg(gs[h], v_ref[keys, LANES[h]], NT) for h in range(3)]
    p = [jnp.exp(s[h] - st_ref[rows, h:h + 1]) for h in range(3)]
    inner = [jnp.sum(p[h] * wg[h], axis=1, keepdims=True) for h in range(3)]
    sg = [(p[h] * (wg[h] - inner[h])).astype(bf16) for h in range(3)]
    p16 = [x.astype(bf16) for x in p]
    dvs = [dg(p16[h], gs[h], TN) for h in range(3)]
    dks = [dg(sg[h], head_of(q_ref[rows, LANES[h]], h), TN) for h in range(3)]
    dqs = [dg(sg[h], k_ref[keys, LANES[h]], NN) for h in range(3)]
    dv[keys, 0:128] += dvs[0] + dvs[1]
    dv[keys, 128:192] += dvs[2]
    dk[keys, 0:128] += dks[0] + dks[1]
    dk[keys, 128:192] += dks[2]
    dq[rows, 0:128] = pair_of(dqs[0], dqs[1]).astype(bf16)
    dq[rows, 128:192] = dqs[2].astype(bf16)
    extra(sg)


def self_scores(q_ref, k_ref, bias_scr, ds, q0, rows, keys, width):
    kpos = lax.broadcasted_iota(i32, (BQ, width), 1) + (q0 + BQ - width)
    shut = jnp.where(kpos >= ds, 0.0, NEG_FILL)
    return lambda h: dg(head_of(q_ref[rows, LANES[h]], h), k_ref[keys, LANES[h]], NT) + (
        bias_scr[h, :, 768 - width:] + shut)


def cross_scores(q_ref, k_ref, tseg, sseg, rows, keys):
    shut = jnp.where(tseg == sseg, 0.0, NEG_FILL)
    return lambda h: dg(head_of(q_ref[rows, LANES[h]], h), k_ref[keys, LANES[h]], NT) + shut


def project(n_ref, w_ref, *outs):
    for j, out in outs:
        out[...] = dg(n_ref[...], w_ref[192 * j:192 * j + 192, :], NT).astype(bf16)


def self_fwd_kernel(first):
    def kernel(core, win, table, *refs):
        if first:
            mine_in, theirs_in, w_ref, ds_ref, n_ref, ctx_ref, st_ref, om, ot, bias_scr, q, k, v = refs
            join_rows(core[0], mine_in, theirs_in, n_ref)
            before = None
        else:
            bits, n_ref, bm, bt, wa, wb, ds_ref, w_ref, ctx_ref, st_ref, om, ot, bias_scr, q, k, v = refs
            join_rows(bits[0], wa, wb, w_ref)
            before = (bm, bt)
        fill_bias(table, bias_scr)
        project(n_ref, w_ref, (0, q), (1, k), (2, v))

        def block(i):
            q0 = pl.multiple_of(i * BQ, BQ)
            rows = pl.ds(q0, BQ)

            @pl.when(win[i] == 0)
            def _():
                ctx_ref[rows, :] = jnp.zeros((BQ, 192), bf16)
                st_ref[rows, :] = jnp.zeros((BQ, 8), f32)

            for n, width in enumerate(SELF_W):
                @pl.when(win[i] == n + 1)
                def _(width=width):
                    keys = pl.ds(pl.multiple_of(q0 + (BQ - width), 128), width)
                    ds = ds_ref[rows, :]
                    attend(self_scores(q, k, bias_scr, ds, q0, rows, keys, width), v, keys, rows, ds < DEAD,
                           ctx_ref, st_ref)
        loop(SLOT // BQ, block)
        out_split(core[0], om, ot, before, lambda c: dg(half_rows(ctx_ref, c), w_ref[576:768, :], NN))
    return kernel


def att_outs():
    return [sd((SLOT, 192), bf16), sd((SLOT, 8), f32), sd((SLOT // 2, 768), f32), sd((SLOT // 2, 768), f32)]


WIDE16, WIDE32 = pltpu.VMEM((SLOT, 192), bf16), pltpu.VMEM((SLOT, 192), f32)
MEM16, MEM32 = pltpu.VMEM((MEM, 192), bf16), pltpu.VMEM((MEM, 192), f32)
BIAS = pltpu.VMEM((3, BQ, 768), f32)


def self_fwd_first(core, win, table, mine, theirs, w, ds):
    return call(self_fwd_kernel(True), "self_fwd", (core, win, table, mine, theirs, w, ds),
                [sd((SLOT, 768), bf16)] + att_outs(), [BIAS, WIDE16, WIDE16, WIDE16], 3, flops=4e9)


def self_fwd_second(core, win, table, bits, n, bm, bt, wa, wb, ds):
    return call(self_fwd_kernel(False), "self_fwd", (core, win, table, bits, n, bm, bt, wa, wb, ds),
                [sd((768, 768), bf16)] + att_outs(), [BIAS, WIDE16, WIDE16, WIDE16], 4, flops=4e9)


def diagonal_sums(scr, h):
    span = scr.shape[2]
    slabs = [scr[h, 8 * a:8 * a + 8, :] for a in range(BQ // 8)]
    step = 8
    while len(slabs) > 1:
        slabs = [slabs[j] + pltpu.roll(slabs[j + 1], span - step, 1) for j in range(0, len(slabs), 2)]
        step *= 2
    acc = slabs[0]
    row = lax.broadcasted_iota(i32, acc.shape, 0)
    for bit in (1, 2, 4):
        acc = jnp.where((row & bit) > 0, pltpu.roll(acc, span - bit, 1), acc)
    return jnp.sum(acc, axis=0, keepdims=True)


def weight_grads(dq, dk16, dv16, nq_ref, nk_ref, b_ref, ctx_ref, dw_ref):
    for j, (left, right) in enumerate(((dq, nq_ref), (dk16, nk_ref), (dv16, nk_ref), (ctx_ref, b_ref))):
        dw_ref[192 * j:192 * j + 192, :] = dg(left[...], right[...], TN).astype(dw_ref.dtype)


def self_bwd_kernel(first):
    def kernel(core, win, table, *refs):
        if first:
            mine_in, theirs_in, *ins = refs[:7]
            b_ref, *rest = refs[7:]
            join_rows(core[0], mine_in, theirs_in, b_ref)
            before = None
        else:
            b_ref, bm, bt, *ins = refs[:8]
            rest = refs[8:]
            before = (bm, bt)
        n_ref, w_ref, ds_ref, ctx_ref, st_ref = ins
        dw_ref, om, ot, db_ref, bias_scr, dbias_scr, q, k, v, g_scr, dq, dk, dv, dk16, dv16 = rest
        fill_bias(table, bias_scr)
        project(n_ref, w_ref, (0, q), (1, k), (2, v))
        dbias_scr[...] = jnp.zeros(dbias_scr.shape, f32)
        dk[...] = jnp.zeros(dk.shape, f32)
        dv[...] = jnp.zeros(dv.shape, f32)
        g = dg(b_ref[...], w_ref[576:768, :], NT).astype(bf16)
        g_scr[...] = jnp.where(ds_ref[...] < DEAD, g, jnp.zeros_like(g))

        def block(i):
            q0 = pl.multiple_of(i * BQ, BQ)
            rows = pl.ds(q0, BQ)

            @pl.when(win[i] == 0)
            def _():
                dq[rows, :] = jnp.zeros((BQ, 192), bf16)

            for n, width in enumerate(SELF_W):
                @pl.when(win[i] == n + 1)
                def _(width=width):
                    keys = pl.ds(pl.multiple_of(q0 + (BQ - width), 128), width)

                    def extra(sg):
                        for h in range(3):
                            dbias_scr[h, :, 768 - width:768] += sg[h].astype(f32)
                    attend_back(self_scores(q, k, bias_scr, ds_ref[rows, :], q0, rows, keys, width),
                                q, k, v, g_scr[rows, :], keys, rows, st_ref, dq, dk, dv, extra)
        loop(SLOT // BQ, block)
        dk16[...] = dk[...].astype(bf16)
        dv16[...] = dv[...].astype(bf16)
        weight_grads(dq, dk16, dv16, n_ref, n_ref, b_ref, ctx_ref, dw_ref)
        out_split(core[0], om, ot, before, lambda c: dg(half_rows(dq, c), w_ref[0:192, :], NN)
                  + dg(half_rows(dk16, c), w_ref[192:384, :], NN) + dg(half_rows(dv16, c), w_ref[384:576, :], NN))
        for h in range(3):
            db_ref[h:h + 1, :] = diagonal_sums(dbias_scr, h)
    return kernel


def self_bwd(first, core, win, table, lead, n, w, ds, saved):
    outs = [sd((768, 768), bf16), sd((SLOT // 2, 768), f32), sd((SLOT // 2, 768), f32), sd((3, 1024), f32)]
    scratch = [BIAS, pltpu.VMEM((3, BQ, 1024), f32)] + [WIDE16] * 5 + [WIDE32, WIDE32, WIDE16, WIDE16]
    args = (core, win, table) + tuple(lead) + (n, w, ds) + tuple(saved)
    if first:
        outs = [sd((SLOT, 768), bf16)] + outs
    return call(self_bwd_kernel(first), "self_bwd", args, outs, scratch, 3, vmem=32, flops=8e9)


def cross_kv_kernel(first):
    def kernel(core, *refs):
        if first:
            mine_in, theirs_in, w_ref, m_ref, k, v = refs
            join_rows(core[0], mine_in, theirs_in, m_ref)
        else:
            m_ref, wa, wb, w_ref, k, v = refs
            join_rows(core[0], wa, wb, w_ref)
        project(m_ref, w_ref, (1, k), (2, v))
    return kernel


def cross_kv_first(core, mine, theirs, w):
    outs = [sd((MEM, 768), bf16)] + [sd((MEM, 192), bf16)] * 2
    return call(cross_kv_kernel(True), "cross_kv", (core, mine, theirs, w), outs, (), 1)


def cross_kv_second(bits, mem, wa, wb):
    outs = [sd((768, 768), bf16)] + [sd((MEM, 192), bf16)] * 2
    return call(cross_kv_kernel(False), "cross_kv", (bits, mem, wa, wb), outs, (), 1)


def cross_fwd_kernel(first):
    def kernel(core, win, *refs):
        if first:
            mine_in, theirs_in, w_ref, tseg_ref, sseg_ref, k, v, n_ref, ctx_ref, st_ref, om, ot, q = refs
            join_rows(core[0], mine_in, theirs_in, n_ref)
            before = None
        else:
            n_ref, bm, bt, w_ref, tseg_ref, sseg_ref, k, v, ctx_ref, st_ref, om, ot, q = refs
            before = (bm, bt)
        project(n_ref, w_ref, (0, q))

        def block(i):
            rows = blk(i)

            @pl.when(win[0, i] == 0)
            def _():
                ctx_ref[rows, :] = jnp.zeros((BQ, 192), bf16)
                st_ref[rows, :] = jnp.zeros((BQ, 8), f32)

            for n, width in enumerate(CROSS_W):
                @pl.when(win[0, i] == n + 1)
                def _(width=width):
                    keys = pl.ds(pl.multiple_of(win[1, i], 128), width)
                    tseg, sseg = tseg_ref[rows, :], sseg_ref[:, keys]
                    attend(cross_scores(q, k, tseg, sseg, rows, keys), v, keys, rows, tseg > 0, ctx_ref, st_ref)
        loop(SLOT // BQ, block)
        out_split(core[0], om, ot, before, lambda c: dg(half_rows(ctx_ref, c), w_ref[576:768, :], NN))
    return kernel


def cross_fwd(first, core, win, lead, w, tseg, sseg, k3, v3):
    outs = ([sd((SLOT, 768), bf16)] if first else []) + att_outs()
    return call(cross_fwd_kernel(first), "cross_fwd", (core, win) + tuple(lead) + (w, tseg, sseg, k3, v3), outs, [WIDE16],
                2, flops=2e9)


def cross_bwd_kernel(first):
    def kernel(core, win, *refs):
        if first:
            mine_in, theirs_in, *ins = refs[:9]
            b_ref, *rest = refs[9:]
            join_rows(core[0], mine_in, theirs_in, b_ref)
            before = mem_before = None
        else:
            b_ref, bm, bt, cm, ct, *ins = refs[:12]
            rest = refs[12:]
            before, mem_before = (bm, bt), (cm, ct)
        n_ref, m_ref, w_ref, tseg_ref, sseg_ref, ctx_ref, st_ref = ins
        dw_ref, om, ot, mm, mt, q, k, v, g_scr, dq, dk, dv, dk16, dv16 = rest
        project(n_ref, w_ref, (0, q))
        project(m_ref, w_ref, (1, k), (2, v))
        dk[...] = jnp.zeros(dk.shape, f32)
        dv[...] = jnp.zeros(dv.shape, f32)
        g = dg(b_ref[...], w_ref[576:768, :], NT).astype(bf16)
        g_scr[...] = jnp.where(tseg_ref[...] > 0, g, jnp.zeros_like(g))

        def block(i):
            rows = blk(i)

            @pl.when(win[0, i] == 0)
            def _():
                dq[rows, :] = jnp.zeros((BQ, 192), bf16)

            for n, width in enumerate(CROSS_W):
                @pl.when(win[0, i] == n + 1)
                def _(width=width):
                    keys = pl.ds(pl.multiple_of(win[1, i], 128), width)
                    attend_back(cross_scores(q, k, tseg_ref[rows, :], sseg_ref[:, keys], rows, keys),
                                q, k, v, g_scr[rows, :], keys, rows, st_ref, dq, dk, dv, lambda sg: None)
        loop(SLOT // BQ, block)
        dk16[...] = dk[...].astype(bf16)
        dv16[...] = dv[...].astype(bf16)
        weight_grads(dq, dk16, dv16, n_ref, m_ref, b_ref, ctx_ref, dw_ref)
        out_split(core[0], om, ot, before, lambda c: dg(half_rows(dq, c), w_ref[0:192, :], NN))
        out_split(core[0], mm, mt, mem_before, lambda c: dg(half_rows(dk16, c), w_ref[192:384, :], NN)
                  + dg(half_rows(dv16, c), w_ref[384:576, :], NN))
    return kernel


def cross_bwd(first, core, win, lead, n, mem, w, tseg, sseg, ctx, st):
    outs = [sd((768, 768), bf16)] + [sd((SLOT // 2, 768), f32)] * 2 + [sd((MEM // 2, 768), f32)] * 2
    if first:
        outs = [sd((SLOT, 768), bf16)] + outs
    scratch = [WIDE16, MEM16, MEM16, WIDE16, WIDE16, MEM32, MEM32, MEM16, MEM16]
    return call(cross_bwd_kernel(first), "cross_bwd",
                (core, win) + tuple(lead) + (n, mem, w, tseg, sseg, ctx, st), outs, scratch, 2, flops=5e9)


GELU_C = math.sqrt(2.0 / math.pi)


def ffn_rows(n_ref, c_ref, wi_ref, wo_ref, o_ref, t_ref, h_ref, g_ref, u_ref, base):
    def block(i):
        rows = blk(i)
        keep = pl.ds(pl.multiple_of(base + i * BQ, BQ), BQ)
        n = n_ref[rows, :]
        gate, up = dg(n, wi_ref[0], NN), dg(n, wi_ref[1], NN)
        hid = dg(c_ref[rows, :], wo_ref[...], NT)
        square = gate * gate
        th = jnp.tanh(GELU_C * (gate + 0.044715 * (gate * square)))
        half = 0.5 * (1.0 + th)
        gelu = gate * half
        slope = half + (0.5 * GELU_C) * gate * (1.0 - th * th) * (1.0 + (3 * 0.044715) * square)
        h = (gelu * up).astype(bf16)
        gg = (hid * up * slope).astype(bf16)
        ug = (hid * gelu).astype(bf16)
        h_ref[keep, :], g_ref[keep, :], u_ref[keep, :] = h, gg, ug
        o_ref[rows, :] = dg(h, wo_ref[...], NN)
        t_ref[rows, :] = dg(gg, wi_ref[0], NT) + dg(ug, wi_ref[1], NT)
    loop(n_ref.shape[0] // BQ, block)


def ffn_weight_grads(na, nb, ca, cb, h_ref, g_ref, u_ref, put):
    half = na.shape[0]
    for j, (la, lb, right) in enumerate(((na, nb, g_ref), (na, nb, u_ref), (ca, cb, h_ref))):
        put(j, dg(la[...], right[0:half, :], TN) + dg(lb[...], right[half:2 * half, :], TN))


def ffn_first_kernel(na, nb, ca, cb, wi_ref, wo_ref, oa, ob, ta, tb, dw_ref, h_ref, g_ref, u_ref):
    ffn_rows(na, ca, wi_ref, wo_ref, oa, ta, h_ref, g_ref, u_ref, 0)
    ffn_rows(nb, cb, wi_ref, wo_ref, ob, tb, h_ref, g_ref, u_ref, na.shape[0])

    def put(j, value):
        dw_ref[768 * j:768 * j + 768, :] = value
    ffn_weight_grads(na, nb, ca, cb, h_ref, g_ref, u_ref, put)


def ffn_first(na, nb, ca, cb, wi, wo):
    rows, units = na.shape[0], wo.shape[0]
    return call(ffn_first_kernel, "ffn_first", (na, nb, ca, cb, wi, wo),
                [sd((rows, 768), f32)] * 4 + [sd((2304, units), f32)], [pltpu.VMEM((2 * rows, units), bf16)] * 3, vmem=36)


def ffn_second_kernel(na, nb, ca, cb, wi_ref, wo_ref, oa, ob, ta, tb, h_ref, g_ref, u_ref):
    ffn_rows(na, ca, wi_ref, wo_ref, oa, ta, h_ref, g_ref, u_ref, 0)
    ffn_rows(nb, cb, wi_ref, wo_ref, ob, tb, h_ref, g_ref, u_ref, na.shape[0])


def ffn_second(na, nb, ca, cb, wi, wo):
    rows, units = na.shape[0], wo.shape[0]
    return call(ffn_second_kernel, "ffn_second", (na, nb, ca, cb, wi, wo),
                [sd((rows, 768), f32)] * 4 + [sd((2 * rows, units), bf16)] * 3)


def ffn_grads_kernel(na, nb, ca, cb, h_ref, g_ref, u_ref, dw_ref, a_ref, b_ref):
    def put(j, value):
        value = (value + dw_ref[768 * j:768 * j + 768, :]).astype(bf16)
        if j == 0:
            a_ref[0:768, :] = value
        elif j == 1:
            a_ref[768:1152, :] = value[0:384]
            b_ref[0:384, :] = value[384:768]
        else:
            b_ref[384:1152, :] = value
    ffn_weight_grads(na, nb, ca, cb, h_ref, g_ref, u_ref, put)


def ffn_grads(na, nb, ca, cb, h, g, u, dw):
    units = h.shape[1]
    return call(ffn_grads_kernel, "ffn_grads", (na, nb, ca, cb, h, g, u, dw), [sd((1152, units), bf16)] * 2)


def ffn_finish_kernel(bits, a0, a1, b0, b1, gi, go, model, unit, scr):
    quarter = a0.shape[0]
    for base, bit, own, other in ((0, bits[0], a0, a1), (2 * quarter, bits[1], b0, b1)):
        scr[pl.ds(pl.multiple_of(base + bit * quarter, 16), quarter), :] = own[...]
        scr[pl.ds(pl.multiple_of(base + (1 - bit) * quarter, 16), quarter), :] = other[...]
    for j in range(2):
        g = scr[768 * j:768 * j + 768, :].astype(f32)
        gi[j] = g
        sq = g * g
        model[j:j + 1, :] = jnp.transpose(jnp.sum(sq, axis=1, keepdims=True))
        unit[j:j + 1, :] = jnp.sum(sq, axis=0, keepdims=True) * (1.0 / D)
    g = scr[1536:2304, :].astype(f32)
    go[...] = jnp.transpose(g)
    sq = g * g
    model[2:3, :] = jnp.transpose(jnp.sum(sq, axis=1, keepdims=True))
    unit[2:3, :] = jnp.sum(sq, axis=0, keepdims=True) * (1.0 / D)


def ffn_finish(bits, a0, a1, b0, b1):
    units = a0.shape[1]
    return call(ffn_finish_kernel, "ffn_finish", (bits, a0, a1, b0, b1),
                [sd((2, 768, units), f32), sd((units, 768), f32), sd((3, 768), f32), sd((3, units), f32)],
                [pltpu.VMEM((2304, units), bf16)], 1, flops=1e6)


def finish_kernel(bits, sa0, sa1, sb0, sb1, ca0, ca1, cb0, cb1, fm_ref, qg, kvg, og, model, head, proj, s_ref, c_ref):
    for ref, a0, a1, b0, b1 in ((s_ref, sa0, sa1, sb0, sb1), (c_ref, ca0, ca1, cb0, cb1)):
        for base, bit, own, other in ((0, bits[0], a0, a1), (384, bits[1], b0, b1)):
            ref[pl.ds(pl.multiple_of(base + bit * 192, 16), 192), :] = own[...]
            ref[pl.ds(pl.multiple_of(base + (1 - bit) * 192, 16), 192), :] = other[...]

    def turned(ref, j):
        return jnp.transpose(ref[192 * j:192 * j + 192, :].astype(f32))

    def one(ref, j, out_ref, at, row, head_row):
        w = turned(ref, j)
        out_ref[at] = w
        sq = w * w
        model[row:row + 1, :] = jnp.transpose(jnp.sum(sq, axis=1, keepdims=True))
        head[head_row:head_row + 1, :] = jnp.sum(sq, axis=0, keepdims=True) * (1.0 / D)

    for a, ref in enumerate((s_ref, c_ref)):
        one(ref, 0, qg, a, a, a)
        one(ref, 1, kvg, (a, 0), 2 + 2 * a, 2 + 2 * a)
        one(ref, 2, kvg, (a, 1), 3 + 2 * a, 3 + 2 * a)
        w = ref[576:768, :].astype(f32)
        og[a] = w
        model[8 + a:9 + a, :] = jnp.sum(w * w, axis=0, keepdims=True)
        w = turned(ref, 3)
        proj[a:a + 1, :] = jnp.sum(w * w, axis=0, keepdims=True) * (1.0 / D)
    model[6:8, :] = fm_ref[0:2, :]
    model[10:11, :] = fm_ref[2:3, :]


def finish(bits, self_parts, cross_parts, ffn_model):
    outs = [sd((2, 768, 192), f32), sd((2, 2, 768, 192), f32), sd((2, 192, 768), f32), sd((11, 768), f32),
            sd((6, 192), f32), sd((2, 192), f32)]
    return call(finish_kernel, "finish", (bits,) + tuple(self_parts) + tuple(cross_parts) + (ffn_model,), outs,
                [pltpu.VMEM((768, 768), bf16)] * 2, 1, flops=1e6)


CORE = [(i, i ^ 1) for i in range(4)]
CHIP = [(i, i ^ 2) for i in range(4)]


def swap_core(v):
    return lax.ppermute(v, "tensor", CORE)


def swap_chip(v):
    return lax.ppermute(v, "tensor", CHIP)


def swap_dp(v, bit):
    return lax.ppermute(v, "dp", [(i, i ^ (1 << bit)) for i in range(lax.axis_size("dp"))])


def dp_bits():
    return int(math.log2(lax.axis_size("dp")))


def after(value, *earlier):
    return lax.optimization_barrier((value,) + earlier)[0]


def add16(a, b):
    return (a.astype(f32) + b.astype(f32)).astype(bf16)


def halves(total, bit):
    mine = lax.shift_right_logical(lax.axis_index("dp"), bit) & 1
    pair = total.reshape((2, total.shape[0] // 2) + total.shape[1:])
    return lax.dynamic_index_in_dim(pair, mine, 0, False), lax.dynamic_index_in_dim(pair, 1 - mine, 0, False)


def rejoin(total, other, bit):
    mine = lax.shift_right_logical(lax.axis_index("dp"), bit) & 1
    return jnp.where(mine == 0, jnp.concatenate((total, other)), jnp.concatenate((other, total)))


def start(total, bit):
    keep, give = halves(total, bit)
    return keep, swap_dp(give, bit)


def middle(a, b):
    both = jnp.concatenate((a, b))
    return both, swap_dp(both, 2)


def middle_rest(both):
    for bit in range(3, dp_bits()):
        both = add16(both, swap_dp(both, bit))
    return jnp.split(both, 2)


def sync(*values):
    return lax.optimization_barrier(values)


def bucket_sums(lane_sums):
    lane = np.arange(1024)
    distance = 512 - np.where(lane < 768, lane, lane - 1024)
    buckets = jnp.asarray(np.array([bucket_of(max(int(n), 0)) for n in distance], np.int32))
    onehot = (buckets[:, None] == jnp.arange(BUCKETS)[None, :]) & jnp.asarray(distance >= 0)[:, None]
    return lax.dot_general(onehot.astype(f32), lane_sums, (((0,), (1,)), ((), ())), precision=lax.Precision.HIGHEST,
                           preferred_element_type=f32)


def on_device(tokens, memory, cotangent, norm_gains, query_weight, keyvalue_weight, output_weight, bias_table,
              inner_weight, outer_weight, target_lengths, source_lengths):
    t, d = lax.axis_index("tensor"), lax.axis_index("dp")
    core = (t & 1).reshape(1).astype(i32)
    slot = lax.shift_right_logical(t, 1).reshape(1).astype(i32)
    bits = jnp.stack((d & 1, lax.shift_right_logical(d, 1) & 1)).astype(i32)
    gains = [norm_gains[i:i + 1] for i in range(3)]

    w_self, half_self, w_cross, half_cross = packed(bits, query_weight, keyvalue_weight, output_weight)
    wa = swap_chip(half_self)
    n1m = norm_rows(tokens, gains[0])
    n1t = swap_core(n1m)
    table_away = swap_chip(bias_table)
    ds, tseg, sseg, swin, cwin = slot_layout(slot, target_lengths, source_lengths)
    n1, *s_own, pm, pt = self_fwd_first(core, swin, bias_table, n1m, n1t, w_self, ds)
    wa, n1, half_cross, memory, cotangent = sync(wa, n1, half_cross, memory, cotangent)
    wb = swap_dp(wa, 0)
    ca = swap_chip(half_cross)
    mem_t, cot_t = swap_core(memory), swap_core(cotangent)
    mem, ck_own, cv_own = cross_kv_first(core, memory, mem_t, w_cross)
    wb, ca, cotangent, n1 = sync(wb, ca, cotangent, n1)
    cb = swap_dp(ca, 0)
    cot_pm = swap_chip(cotangent)
    w_self_away, *s_away, pm, pt = self_fwd_second(core, swin, table_away, bits, n1, pm, pt, wa, wb, ds)
    after_self, n2m = add_norm(tokens, pm, swap_core(pt), gains[1])

    n2t = swap_core(n2m)
    n2, *c_own, pm, pt = cross_fwd(True, core, cwin, (n2m, n2t), w_cross, tseg, sseg, ck_own, cv_own)
    cb, pm, pt, n2 = sync(cb, pm, pt, n2)
    w_cross_away, ck_away, cv_away = cross_kv_second(bits, mem, ca, cb)
    *c_away, pm, pt = cross_fwd(False, core, cwin, (n2, pm, pt), w_cross_away, tseg, sseg, ck_away, cv_away)
    pm, pt, cot_pm = sync(pm, pt, cot_pm)
    after_cross, n3m = add_norm(after_self, pm, swap_core(pt), gains[2])

    n3pm = swap_chip(n3m)
    n3t, cot_pt = swap_core(n3m), swap_core(cot_pm)
    oa, ob, ta, tb, dw = ffn_first(n3m, n3t, cotangent, cot_t, inner_weight, outer_weight)
    n3pm, oa, ob, ta, tb, dw = sync(n3pm, oa, ob, ta, tb, dw)
    n3pt = swap_core(n3pm)
    oc, od, tc, td, hh, gg, ug = ffn_second(n3pm, n3pt, cot_pm, cot_pt, inner_weight, outer_weight)
    third_away = swap_chip((tc + swap_core(td)).astype(bf16))
    third_core = swap_core(tb)
    fa, fb = ffn_grads(n3pm, n3pt, cot_pm, cot_pt, hh, gg, ug, dw)
    fa, fb, third_away, third_core = sync(fa, fb, third_away, third_core)
    fa, fa_in = start(fa, 0)
    fb, fb_in = start(fb, 1)
    cross_out_m, branch_m, gain2 = norm_back(after_cross, gains[2], cotangent, ta, third_core, third_away)

    branch_t = swap_core(branch_m)
    branch_m, branch_t, fa_in, fb_in = sync(branch_m, branch_t, fa_in, fb_in)
    fa, fa_in = start(add16(fa, fa_in), 1)
    fb, fb_in = start(add16(fb, fb_in), 0)
    branch, c_out, pm, pt, mm, mt = cross_bwd(True, core, cwin, (branch_m, branch_t), n2, mem, w_cross_away, tseg, sseg,
                                              *c_away)
    branch, c_out, pm, pt, mm, mt, fa_in, fb_in = sync(branch, c_out, pm, pt, mm, mt, fa_in, fb_in)
    c_in = swap_chip(c_out)
    f_mid, f_in = middle(add16(fa, fa_in), add16(fb, fb_in))
    c_sum, pm, pt, mm, mt = cross_bwd(False, core, cwin, (branch, pm, pt, mm, mt), n2, mem, w_cross, tseg, sseg, *c_own)
    self_out_m, branch_m, gain1 = norm_back(after_self, gains[1], cross_out_m, pm, swap_core(pt))

    branch_t = swap_core(branch_m)
    branch, s_out, pm, pt, lanes_away = self_bwd(True, core, swin, table_away, (branch_m, branch_t), n1, w_self_away,
                                                 ds, s_away)
    branch, s_out, pm, pt, lanes_away, f_in, c_in = sync(branch, s_out, pm, pt, lanes_away, f_in, c_in)
    s_in = swap_chip(s_out)
    lanes_in = swap_chip(lanes_away)
    fa, fb = middle_rest(add16(f_mid, f_in))
    fa_in, fb_in = swap_dp(fa, 1), swap_dp(fb, 0)
    c_a, c_b = jnp.split(add16(c_sum, c_in), 2)
    c_a, ca_in = start(c_a, 0)
    c_b, cb_in = start(c_b, 1)
    s_sum, pm, pt, lanes_own = self_bwd(False, core, swin, bias_table, (branch, pm, pt), n1, w_self, ds, s_own)
    s_sum, pm, pt, lanes_own, lanes_in, fa_in, fb_in, ca_in, cb_in, od = sync(
        s_sum, pm, pt, lanes_own, lanes_in, fa_in, fb_in, ca_in, cb_in, od)

    pt_in, od_in, ob_in, mt_in = swap_core(pt), swap_core(od), swap_core(ob), swap_core(mt)
    fa, fb = rejoin(fa, fa_in, 1), rejoin(fb, fb_in, 0)
    fa_in, fb_in = swap_dp(fa, 0), swap_dp(fb, 1)
    c_a, ca_in = start(add16(c_a, ca_in), 1)
    c_b, cb_in = start(add16(c_b, cb_in), 0)
    tokens_grad, _, gain0 = norm_back(tokens, gains[0], self_out_m, pm, pt_in)
    memory_grad = mm + mt_in
    out_away = (oc + od_in).astype(bf16)
    small = jnp.concatenate((gain0, gain1, gain2))
    s_in, ca_in, cb_in, small, out_away, s_sum = sync(s_in, ca_in, cb_in, small, out_away, s_sum)
    s_a, s_b = jnp.split(add16(s_sum, s_in), 2)
    s_a, sa_in = start(s_a, 0)
    s_b, sb_in = start(s_b, 1)
    c_mid, c_in = middle(add16(c_a, ca_in), add16(c_b, cb_in))
    out_in = swap_chip(out_away)
    small = small + swap_core(small)
    small = small + swap_chip(small)
    small = jnp.concatenate((jnp.pad(small, ((0, 0), (0, 256))), lanes_own + lanes_in))
    sa_in, sb_in, c_in, fa_in, fb_in, small = sync(sa_in, sb_in, c_in, fa_in, fb_in, small)
    s_a, sa_in = start(add16(s_a, sa_in), 1)
    s_b, sb_in = start(add16(s_b, sb_in), 0)
    c_a, c_b = middle_rest(add16(c_mid, c_in))
    ca_in, cb_in = swap_dp(c_a, 1), swap_dp(c_b, 0)
    small = small + swap_dp(small, 0)
    sa_in, sb_in, ca_in, cb_in, fa_in, fb_in, small = sync(sa_in, sb_in, ca_in, cb_in, fa_in, fb_in, small)
    s_mid, s_in = middle(add16(s_a, sa_in), add16(s_b, sb_in))
    c_a, c_b = rejoin(c_a, ca_in, 1), rejoin(c_b, cb_in, 0)
    ca_in, cb_in = swap_dp(c_a, 0), swap_dp(c_b, 1)
    inner_sum, outer_sum, ffn_model, unit_stats = ffn_finish(bits, fa, fa_in, fb, fb_in)
    small = small + swap_dp(small, 1)
    s_in, ffn_model, ca_in, cb_in, small = sync(s_in, ffn_model, ca_in, cb_in, small)
    s_a, s_b = middle_rest(add16(s_mid, s_in))
    sa_in, sb_in = swap_dp(s_a, 1), swap_dp(s_b, 0)
    for bit in range(2, dp_bits()):
        small = small + swap_dp(small, bit)
    output_rows = (after_cross + ((oa + ob_in) + out_in.astype(f32))).astype(bf16)
    s_a, s_b = rejoin(s_a, sa_in, 1), rejoin(s_b, sb_in, 0)
    sa_in, sb_in = swap_dp(s_a, 0), swap_dp(s_b, 1)
    gains_total = small[:3, :D]
    table_sum = bucket_sums(small[3:])
    query_grad, keyvalue_grad, output_grad, model_part, head_stats, projection_stats = finish(
        bits, (s_a, sa_in, s_b, sb_in), (c_a, ca_in, c_b, cb_in), ffn_model)
    diagonal = lax.ppermute(model_part, "tensor", [(i, i ^ 3) for i in range(4)])
    model_total = (model_part + swap_core(model_part)) + (swap_chip(model_part) + diagonal)
    hidden_units = outer_weight.shape[0] * lax.axis_size("tensor")
    divisors = jnp.array([D] * 6 + [hidden_units] * 2 + [D] * 2 + [hidden_units], f32)
    model_stats = model_total / divisors[:, None]
    return (output_rows, tokens_grad, memory_grad, gains_total, query_grad, keyvalue_grad, output_grad, table_sum,
            inner_sum, outer_sum, model_stats, head_stats, projection_stats, unit_stats)


def solution(mesh):
    rows = P(("dp", "tensor"), None)
    in_specs = (rows, rows, rows, P(), P(None, None, "tensor"), P(None, None, None, "tensor"), P(None, "tensor", None),
                P(None, "tensor"), P(None, None, "tensor"), P("tensor", None), P("dp", None), P("dp", None))
    out_specs = (rows, rows, rows, P(), P(None, None, "tensor"), P(None, None, None, "tensor"),
                 P(None, "tensor", None), P(None, "tensor"), P(None, None, "tensor"), P("tensor", None), P(),
                 P(None, "tensor"), P(None, "tensor"), P(None, "tensor"))
    return jax.shard_map(on_device, mesh=mesh, in_specs=in_specs, out_specs=out_specs, check_vma=False)
```

```python
import math

import jax
import jax.numpy as jnp
import numpy as np
from jax import lax
from jax.experimental import pallas as pl
from jax.experimental.pallas import tpu as pltpu
from jax.sharding import PartitionSpec as P

D = 768
DH = 64
BUCKETS = 32
MAXDIST = 128
SLOT = 1024
MEM = 512
NORM_EPS = 1e-06
NEG_FILL = -1e30
DEAD = 1 << 20
BQ = 256
COST = 0.02
VM = pl.BlockSpec(memory_space=pltpu.VMEM)
SM = pl.BlockSpec(memory_space=pltpu.SMEM)
NT = (((1,), (1,)), ((), ()))
NN = (((1,), (0,)), ((), ()))
TN = (((0,), (0,)), ((), ()))
f32, bf16, i32 = jnp.float32, jnp.bfloat16, jnp.int32
SELF_W = (256, 384, 512, 768)
CROSS_W = (128, 256, 512)
sd = jax.ShapeDtypeStruct


def dg(a, b, dims):
    return lax.dot_general(a, b, dims, preferred_element_type=f32)


def blk(i):
    return pl.ds(pl.multiple_of(i * BQ, BQ), BQ)


def loop(count, body):
    def step(i, carry):
        body(i)
        return carry
    lax.fori_loop(0, count, step, 0)


def call(kernel, name, args, outs, scratch=(), scalars=0, vmem=12, flops=1e9, out_specs=None):
    byts = sum(int(np.prod(a.shape)) * a.dtype.itemsize for a in tuple(args) + tuple(outs))
    return pl.pallas_call(
        kernel,
        in_specs=[SM] * scalars + [VM] * (len(args) - scalars),
        out_specs=list(out_specs) if out_specs else [VM] * len(outs),
        out_shape=list(outs),
        scratch_shapes=list(scratch),
        name=name,
        compiler_params=pltpu.CompilerParams(vmem_limit_bytes=vmem << 20),
        cost_estimate=pl.CostEstimate(flops=int(flops * COST), bytes_accessed=int(byts * COST), transcendentals=0),
    )(*args)


def bucket_of(spread):
    exact_count = BUCKETS // 2
    if spread < exact_count:
        return spread
    larger = exact_count + math.floor(
        math.log(spread / exact_count) / math.log(MAXDIST / exact_count) * (BUCKETS - exact_count)
    )
    return min(larger, BUCKETS - 1)


def bucket_starts():
    buckets = [bucket_of(n) for n in range(SLOT)]
    return [next(n for n in range(SLOT + 1) if n == SLOT or buckets[n] >= b) for b in range(BUCKETS)]


def layout_kernel(slot, tl_ref, sl_ref, seg_ref, sseg_ref, swin, cwin):
    s = slot[0]
    docs = tl_ref.shape[1]
    tl = [tl_ref[s, j] for j in range(docs)]
    sl = [sl_ref[s, j] for j in range(docs)]
    ends, sends = [], []
    te, se = jnp.int32(0), jnp.int32(0)
    for j in range(docs):
        te, se = te + tl[j], se + sl[j]
        ends.append(te)
        sends.append(se)
    pos = lax.broadcasted_iota(i32, (1, SLOT), 1)
    spos = lax.broadcasted_iota(i32, sseg_ref.shape, 1)
    start, seg, mseg = jnp.zeros_like(pos), jnp.ones_like(pos), jnp.ones_like(spos)
    for j in range(docs):
        past = pos >= ends[j]
        start = jnp.where(past, ends[j], start)
        seg = seg + past.astype(i32)
        mseg = mseg + (spos >= sends[j]).astype(i32)
    live = pos < te
    seg_ref[...] = jnp.zeros(seg_ref.shape, i32)
    seg_ref[0:1, :] = jnp.where(live, start, DEAD)
    seg_ref[1:2, :] = jnp.where(live, seg, -1)
    sseg_ref[...] = jnp.where(spos < se, mseg, 0)
    for i in range(SLOT // BQ):
        q0 = i * BQ
        first, low, high = jnp.int32(0), jnp.int32(0), jnp.int32(0)
        last = jnp.minimum(q0 + BQ - 1, te - 1)
        for j in range(docs):
            before = ends[j] <= q0
            first = jnp.where(before, ends[j], first)
            low = low + jnp.where(before, sl[j], 0)
            high = high + jnp.where(ends[j] - tl[j] <= last, sl[j], 0)
        need = q0 + BQ - lax.shift_left(lax.shift_right_logical(first, 7), 7)
        width = jnp.int32(1)
        for w in SELF_W[:-1]:
            width = width + jnp.where(need > w, 1, 0)
        swin[i] = jnp.where(q0 < te, width, 0)
        at1 = lax.shift_left(lax.shift_right_logical(low, 7), 7)
        at2 = jnp.minimum(at1, MEM - 256)
        one, two = high - at1 <= 128, high - at2 <= 256
        cwin[0, i] = jnp.where(q0 < te, jnp.where(one, 1, jnp.where(two, 2, 3)), 0)
        cwin[1, i] = jnp.where(one, at1, jnp.where(two, at2, 0))


def slot_layout(slot, tl, sl):
    return call(layout_kernel, "layout", (slot, tl, sl),
                (sd((8, SLOT), i32), sd((1, MEM), i32), sd((4,), i32), sd((2, 4), i32)),
                scalars=3, flops=1e6, out_specs=(VM, VM, SM, SM))


def pack_kernel(bits, wi_ref, wo_ref, fa, fb):
    inner = wi_ref[bits[0]]
    outer = half_rows(wo_ref, bits[0])
    fa[...] = inner[0:576]
    fb[0:192, :] = inner[576:768]
    fb[192:448, :] = outer[:, 0:512]
    fb[448:576, 0:256] = outer[0:128, 512:768]
    fb[448:576, 256:512] = outer[128:256, 512:768]


def packed(bits, wi, wo):
    return call(pack_kernel, "pack", (bits, wi, wo), (sd((576, 512), bf16),) * 2, (), 1)


def own_weights(which, q_ref, kv_ref, o_ref):
    return (q_ref.at[which], kv_ref.at[which, 0], kv_ref.at[which, 1], o_ref.at[which])


def away_weights(w_ref):
    return tuple(w_ref.at[192 * j:192 * j + 192] for j in range(4))


def norm_kernel(x_ref, gain_ref, n_ref):
    x = x_ref[...].astype(f32)
    r = lax.rsqrt(jnp.mean(x * x, axis=-1, keepdims=True) + NORM_EPS)
    n_ref[...] = (x * r * gain_ref[...]).astype(bf16)


def norm_rows(x, gain):
    return call(norm_kernel, "norm", (x, gain), (sd(x.shape, bf16),), flops=1e6)[0]


def add_norm_kernel(x_ref, a_ref, b_ref, gain_ref, y_ref, n_ref):
    y = x_ref[...].astype(f32) + (a_ref[...] + b_ref[...])
    y_ref[...] = y
    r = lax.rsqrt(jnp.mean(y * y, axis=-1, keepdims=True) + NORM_EPS)
    n_ref[...] = (y * r * gain_ref[...]).astype(bf16)


def add_norm(x, a, b, gain):
    return call(add_norm_kernel, "add_norm", (x, a, b, gain), (sd(x.shape, f32), sd(x.shape, bf16)), flops=1e6)


def norm_back_kernel(terms):
    def kernel(v_ref, gain_ref, up_ref, *refs):
        total_ref, branch_ref, sum_ref = refs[terms:]
        grad = refs[0][...].astype(f32)
        for ref in refs[1:terms]:
            grad = grad + ref[...].astype(f32)
        v = v_ref[...].astype(f32)
        r = lax.rsqrt(jnp.mean(v * v, axis=-1, keepdims=True) + NORM_EPS)
        scaled = grad * gain_ref[...]
        back = r * scaled - v * ((r * r * r) * jnp.mean(scaled * v, axis=-1, keepdims=True))
        total = up_ref[...].astype(f32) + back
        total_ref[...] = total
        branch_ref[...] = total.astype(bf16)
        sum_ref[...] = jnp.sum(grad * v * r, axis=0, keepdims=True)
    return kernel


def norm_back(v, gain, up, *grads):
    return call(norm_back_kernel(len(grads)), "norm_back", (v, gain, up) + grads,
                (sd(v.shape, f32), sd(v.shape, bf16), sd((1, v.shape[1]), f32)), flops=1e6)


LANES = (slice(0, 128), slice(0, 128), slice(128, 192))


def head_of(rows128, h):
    if h == 2:
        return rows128
    lane = lax.broadcasted_iota(i32, rows128.shape, 1)
    return jnp.where((lane < 64) == (h == 0), rows128, jnp.zeros_like(rows128))


def pair_of(first, second):
    lane = lax.broadcasted_iota(i32, first.shape, 1)
    return jnp.where(lane < 64, first, second)


def half_rows(ref, which):
    half = ref.shape[0] // 2
    return ref[pl.ds(pl.multiple_of(which * half, half), half), :]


def join_rows(core, mine_ref, theirs_ref, all_ref):
    half = mine_ref.shape[0]
    at = pl.multiple_of(core * half, half)
    all_ref[pl.ds(at, half), :] = mine_ref[...]
    all_ref[pl.ds(pl.multiple_of(half - at, half), half), :] = theirs_ref[...]


def out_split(core, mine_ref, theirs_ref, before, value_of):
    for pos, ref in enumerate((mine_ref, theirs_ref)):
        value = value_of(core if pos == 0 else 1 - core)
        ref[...] = value if before is None else value + before[pos][...]


def fill_bias(table, bias_scr):
    lane = lax.broadcasted_iota(i32, (1, 1024), 1)
    distance = 512 - jnp.where(lane < 768, lane, lane - 1024)
    for h in range(3):
        row = jnp.full((1, 1024), table[0, h], f32)
        for b, first in enumerate(bucket_starts()):
            if b > 0:
                row = jnp.where(distance >= first, table[b, h], row)
        row = jnp.where(distance < 0, NEG_FILL, row)
        wide = jnp.broadcast_to(row, (BQ, 1024))
        bias_scr[h] = pltpu.roll(wide, 0, 1, stride=1, stride_axis=0)[:, :768]


def attend(scores, v_ref, keys, rows, live, ctx_ref, st_ref):
    s = [scores(h) for h in range(3)]
    m = [jnp.max(x, axis=1, keepdims=True) for x in s]
    e = [jnp.exp(x - y) for x, y in zip(s, m)]
    total = [jnp.sum(x, axis=1, keepdims=True) for x in e]
    p = [(x * (1.0 / y)).astype(bf16) for x, y in zip(e, total)]
    c = [dg(p[h], v_ref[keys, LANES[h]], NN) for h in range(3)]
    ctx_ref[rows, 0:128] = jnp.where(live, pair_of(c[0], c[1]), 0.0).astype(bf16)
    ctx_ref[rows, 128:192] = jnp.where(live, c[2], 0.0).astype(bf16)
    for h in range(3):
        st_ref[rows, h:h + 1] = m[h] + jnp.log(total[h])


def attend_back(scores, q_ref, k_ref, v_ref, g, keys, rows, st_ref, dq, dk, dv, extra):
    gs = [head_of(g[:, LANES[h]], h) for h in range(3)]
    s = [scores(h) for h in range(3)]
    wg = [dg(gs[h], v_ref[keys, LANES[h]], NT) for h in range(3)]
    p = [jnp.exp(s[h] - st_ref[rows, h:h + 1]) for h in range(3)]
    inner = [jnp.sum(p[h] * wg[h], axis=1, keepdims=True) for h in range(3)]
    sg = [(p[h] * (wg[h] - inner[h])).astype(bf16) for h in range(3)]
    p16 = [x.astype(bf16) for x in p]
    dvs = [dg(p16[h], gs[h], TN) for h in range(3)]
    dks = [dg(sg[h], head_of(q_ref[rows, LANES[h]], h), TN) for h in range(3)]
    dqs = [dg(sg[h], k_ref[keys, LANES[h]], NN) for h in range(3)]
    dv[keys, 0:128] += dvs[0] + dvs[1]
    dv[keys, 128:192] += dvs[2]
    dk[keys, 0:128] += dks[0] + dks[1]
    dk[keys, 128:192] += dks[2]
    dq[rows, 0:128] = pair_of(dqs[0], dqs[1]).astype(bf16)
    dq[rows, 128:192] = dqs[2].astype(bf16)
    extra(sg)


def self_scores(q_ref, k_ref, bias_scr, ds, q0, rows, keys, width):
    kpos = lax.broadcasted_iota(i32, (BQ, width), 1) + (q0 + BQ - width)
    shut = jnp.where(kpos >= ds, 0.0, NEG_FILL)
    return lambda h: dg(head_of(q_ref[rows, LANES[h]], h), k_ref[keys, LANES[h]], NT) + (
        bias_scr[h, :, 768 - width:] + shut)


def cross_scores(q_ref, k_ref, tseg, sseg, rows, keys):
    shut = jnp.where(tseg == sseg, 0.0, NEG_FILL)
    return lambda h: dg(head_of(q_ref[rows, LANES[h]], h), k_ref[keys, LANES[h]], NT) + shut


def project(n_ref, ws, *outs):
    for j, out in outs:
        out[...] = dg(n_ref[...], ws[j][...], NT).astype(bf16)


def self_attend(core, win, table, n_ref, ws, cols, before, ctx_ref, st_ref, om, ot, bias_scr, q, k, v, st):
    fill_bias(table, bias_scr)
    project(n_ref, ws, (0, q), (1, k), (2, v))

    def block(i):
        q0 = pl.multiple_of(i * BQ, BQ)
        rows = pl.ds(q0, BQ)

        @pl.when(win[i] == 0)
        def _():
            ctx_ref[rows, :] = jnp.zeros((BQ, 192), bf16)
            st[rows, :] = jnp.zeros((BQ, 8), f32)

        for n, width in enumerate(SELF_W):
            @pl.when(win[i] == n + 1)
            def _(width=width):
                keys = pl.ds(pl.multiple_of(q0 + (BQ - width), 128), width)
                ds = cols[rows, 0:1]
                attend(self_scores(q, k, bias_scr, ds, q0, rows, keys, width), v, keys, rows, ds < DEAD, ctx_ref, st)
    loop(SLOT // BQ, block)
    st_ref[...] = jnp.transpose(st[...])
    out_split(core[0], om, ot, before, lambda c: dg(half_rows(ctx_ref, c), ws[3][...], NN))


def self_fwd_first_kernel(core, win, table, mine_in, theirs_in, wq, wkv, wo, seg, n_ref, ctx, st, om, ot, cols, *scr):
    cols[...] = jnp.transpose(seg[...])
    join_rows(core[0], mine_in, theirs_in, n_ref)
    self_attend(core, win, table, n_ref, own_weights(0, wq, wkv, wo), cols, None, ctx, st, om, ot, *scr)


def self_fwd_second_kernel(core, win, table, bits, n_ref, bm, bt, wa, wb, seg, w_ref, ctx, st, om, ot, cols, *scr):
    cols[...] = jnp.transpose(seg[...])
    join_rows(bits[0], wa, wb, w_ref)
    self_attend(core, win, table, n_ref, away_weights(w_ref), cols, (bm, bt), ctx, st, om, ot, *scr)


HALF32 = sd((SLOT // 2, 768), f32)
ATT = [sd((SLOT, 192), bf16), sd((8, SLOT), f32)]
STACK = sd((768, 768), bf16)
WIDE16, WIDE32 = pltpu.VMEM((SLOT, 192), bf16), pltpu.VMEM((SLOT, 192), f32)
MEM16, MEM32 = pltpu.VMEM((MEM, 192), bf16), pltpu.VMEM((MEM, 192), f32)
BIAS = pltpu.VMEM((3, BQ, 768), f32)
COLS, STATS = pltpu.VMEM((SLOT, 8), i32), pltpu.VMEM((SLOT, 8), f32)


def self_fwd_first(core, win, table, mine, theirs, weights, seg):
    return call(self_fwd_first_kernel, "self_fwd", (core, win, table, mine, theirs) + weights + (seg,),
                [sd((SLOT, 768), bf16)] + ATT + [HALF32, HALF32], [COLS, BIAS, WIDE16, WIDE16, WIDE16, STATS], 3, vmem=14)


def self_fwd_second(core, win, table, bits, n, bm, bt, wa, wb, seg):
    return call(self_fwd_second_kernel, "self_fwd", (core, win, table, bits, n, bm, bt, wa, wb, seg),
                [STACK] + ATT + [HALF32, HALF32], [COLS, BIAS, WIDE16, WIDE16, WIDE16, STATS], 4, vmem=14)


def diagonal_sums(scr, h):
    span = scr.shape[2]
    slabs = [scr[h, 8 * a:8 * a + 8, :] for a in range(BQ // 8)]
    step = 8
    while len(slabs) > 1:
        slabs = [slabs[j] + pltpu.roll(slabs[j + 1], span - step, 1) for j in range(0, len(slabs), 2)]
        step *= 2
    acc = slabs[0]
    row = lax.broadcasted_iota(i32, acc.shape, 0)
    for bit in (1, 2, 4):
        acc = jnp.where((row & bit) > 0, pltpu.roll(acc, span - bit, 1), acc)
    return jnp.sum(acc, axis=0, keepdims=True)


def weight_grads(dq, dk16, dv16, nq_ref, nk_ref, b_ref, ctx_ref, a_ref, put_late):
    a_ref[0:192, :] = dg(dq[...], nq_ref[...], TN).astype(bf16)
    a_ref[192:384, :] = dg(dk16[...], nk_ref[...], TN).astype(bf16)
    put_late(0, dg(dv16[...], nk_ref[...], TN).astype(bf16))
    put_late(1, dg(ctx_ref[...], b_ref[...], TN).astype(bf16))


def put_plain(ref, rows):
    def put(half, value):
        ref[rows * half:rows * half + rows, :] = value
    return put


def self_bwd_core(core, win, table, b_ref, n_ref, ws, seg, ctx_ref, st_ref, before, a_ref, put, om, ot, db_ref,
                  cols, st, bias_scr, dbias_scr, q, k, v, g_scr, dq, dk, dv, dk16, dv16):
    cols[...] = jnp.transpose(seg[...])
    st[...] = jnp.transpose(st_ref[...])
    fill_bias(table, bias_scr)
    project(n_ref, ws, (0, q), (1, k), (2, v))
    dbias_scr[...] = jnp.zeros(dbias_scr.shape, f32)
    dk[...] = jnp.zeros(dk.shape, f32)
    dv[...] = jnp.zeros(dv.shape, f32)
    g = dg(b_ref[...], ws[3][...], NT).astype(bf16)
    g_scr[...] = jnp.where(cols[:, 0:1] < DEAD, g, jnp.zeros_like(g))

    def block(i):
        q0 = pl.multiple_of(i * BQ, BQ)
        rows = pl.ds(q0, BQ)

        @pl.when(win[i] == 0)
        def _():
            dq[rows, :] = jnp.zeros((BQ, 192), bf16)

        for n, width in enumerate(SELF_W):
            @pl.when(win[i] == n + 1)
            def _(width=width):
                keys = pl.ds(pl.multiple_of(q0 + (BQ - width), 128), width)

                def extra(sg):
                    for h in range(3):
                        dbias_scr[h, :, 768 - width:768] += sg[h].astype(f32)
                attend_back(self_scores(q, k, bias_scr, cols[rows, 0:1], q0, rows, keys, width),
                            q, k, v, g_scr[rows, :], keys, rows, st, dq, dk, dv, extra)
    loop(SLOT // BQ, block)
    dk16[...] = dk[...].astype(bf16)
    dv16[...] = dv[...].astype(bf16)
    weight_grads(dq, dk16, dv16, n_ref, n_ref, b_ref, ctx_ref, a_ref, put)
    out_split(core[0], om, ot, before, lambda c: dg(half_rows(dq, c), ws[0][...], NN)
              + dg(half_rows(dk16, c), ws[1][...], NN) + dg(half_rows(dv16, c), ws[2][...], NN))
    for h in range(3):
        db_ref[h:h + 1, :] = diagonal_sums(dbias_scr, h)


SELF_BWD_SCRATCH = ([COLS, STATS, BIAS, pltpu.VMEM((3, BQ, 1024), f32)] + [WIDE16] * 5
                    + [WIDE32, WIDE32, WIDE16, WIDE16])
PART = sd((384, 768), bf16)


def self_bwd_first_kernel(core, win, table, mine_in, theirs_in, n_ref, w_ref, seg, ctx, st, b_ref, a_ref, late_ref,
                          om, ot, db_ref, *scr):
    join_rows(core[0], mine_in, theirs_in, b_ref)
    self_bwd_core(core, win, table, b_ref, n_ref, away_weights(w_ref), seg, ctx, st, None, a_ref, put_plain(late_ref, 192),
                  om, ot, db_ref, *scr)


def self_bwd_second_kernel(core, win, table, b_ref, bm, bt, n_ref, wq, wkv, wo, seg, ctx, st, a_ref, late_ref, om, ot,
                           db_ref, *scr):
    self_bwd_core(core, win, table, b_ref, n_ref, own_weights(0, wq, wkv, wo), seg, ctx, st, (bm, bt), a_ref,
                  put_plain(late_ref, 192), om, ot, db_ref, *scr)


def self_bwd_first(core, win, table, mine, theirs, n, w, seg, ctx, st):
    return call(self_bwd_first_kernel, "self_bwd", (core, win, table, mine, theirs, n, w, seg, ctx, st),
                [sd((SLOT, 768), bf16), PART, PART, HALF32, HALF32, sd((3, 1024), f32)], SELF_BWD_SCRATCH, 3, vmem=28)


def self_bwd_second(core, win, table, b, bm, bt, n, weights, seg, ctx, st):
    return call(self_bwd_second_kernel, "self_bwd", (core, win, table, b, bm, bt, n) + weights + (seg, ctx, st),
                [PART, PART, HALF32, HALF32, sd((3, 1024), f32)], SELF_BWD_SCRATCH, 3, vmem=28)


def cross_fwd_kernel(core, win, bits, mine_in, theirs_in, mem_mine, mem_theirs, wq, wkv, wo, wa, wb, seg, sseg_ref,
                     n_ref, m_ref, w_ref, ctx0, st0, ctx1, st1, om, ot, cols, q, k, v, st):
    cols[...] = jnp.transpose(seg[...])
    join_rows(core[0], mine_in, theirs_in, n_ref)
    join_rows(core[0], mem_mine, mem_theirs, m_ref)
    join_rows(bits[0], wa, wb, w_ref)
    own, away = own_weights(1, wq, wkv, wo), away_weights(w_ref)
    for ws, ctx_ref, st_ref in ((own, ctx0, st0), (away, ctx1, st1)):
        project(n_ref, ws, (0, q))
        project(m_ref, ws, (1, k), (2, v))

        def block(i, ctx_ref=ctx_ref):
            rows = blk(i)

            @pl.when(win[0, i] == 0)
            def _():
                ctx_ref[rows, :] = jnp.zeros((BQ, 192), bf16)
                st[rows, :] = jnp.zeros((BQ, 8), f32)

            for n, width in enumerate(CROSS_W):
                @pl.when(win[0, i] == n + 1)
                def _(width=width):
                    keys = pl.ds(pl.multiple_of(win[1, i], 128), width)
                    tseg, sseg = cols[rows, 1:2], sseg_ref[:, keys]
                    attend(cross_scores(q, k, tseg, sseg, rows, keys), v, keys, rows, tseg > 0, ctx_ref, st)
        loop(SLOT // BQ, block)
        st_ref[...] = jnp.transpose(st[...])
    out_split(core[0], om, ot, None, lambda c: dg(half_rows(ctx0, c), own[3][...], NN)
              + dg(half_rows(ctx1, c), away[3][...], NN))


def cross_fwd(core, win, bits, mine, theirs, mem_mine, mem_theirs, weights, wa, wb, seg, sseg):
    return call(cross_fwd_kernel, "cross_fwd",
                (core, win, bits, mine, theirs, mem_mine, mem_theirs) + weights + (wa, wb, seg, sseg),
                [sd((SLOT, 768), bf16), sd((MEM, 768), bf16), STACK] + ATT + ATT + [HALF32, HALF32],
                [COLS, WIDE16, MEM16, MEM16, STATS], 3, vmem=12)


def cross_bwd_core(core, win, b_ref, n_ref, m_ref, ws, seg, sseg_ref, ctx_ref, st_ref, before, mem_before, a_ref, put,
                   om, ot, mm, mt, cols, st, q, k, v, g_scr, dq, dk, dv, dk16, dv16):
    cols[...] = jnp.transpose(seg[...])
    st[...] = jnp.transpose(st_ref[...])
    project(n_ref, ws, (0, q))
    project(m_ref, ws, (1, k), (2, v))
    dk[...] = jnp.zeros(dk.shape, f32)
    dv[...] = jnp.zeros(dv.shape, f32)
    g = dg(b_ref[...], ws[3][...], NT).astype(bf16)
    g_scr[...] = jnp.where(cols[:, 1:2] > 0, g, jnp.zeros_like(g))

    def block(i):
        rows = blk(i)

        @pl.when(win[0, i] == 0)
        def _():
            dq[rows, :] = jnp.zeros((BQ, 192), bf16)

        for n, width in enumerate(CROSS_W):
            @pl.when(win[0, i] == n + 1)
            def _(width=width):
                keys = pl.ds(pl.multiple_of(win[1, i], 128), width)
                attend_back(cross_scores(q, k, cols[rows, 1:2], sseg_ref[:, keys], rows, keys),
                            q, k, v, g_scr[rows, :], keys, rows, st, dq, dk, dv, lambda sg: None)
    loop(SLOT // BQ, block)
    dk16[...] = dk[...].astype(bf16)
    dv16[...] = dv[...].astype(bf16)
    weight_grads(dq, dk16, dv16, n_ref, m_ref, b_ref, ctx_ref, a_ref, put)
    out_split(core[0], om, ot, before, lambda c: dg(half_rows(dq, c), ws[0][...], NN))
    out_split(core[0], mm, mt, mem_before, lambda c: dg(half_rows(dk16, c), ws[1][...], NN)
              + dg(half_rows(dv16, c), ws[2][...], NN))


CROSS_BWD_SCRATCH = [COLS, STATS, WIDE16, MEM16, MEM16, WIDE16, WIDE16, MEM32, MEM32, MEM16, MEM16]
HALFMEM = sd((MEM // 2, 768), f32)


def cross_bwd_first_kernel(core, win, mine_in, theirs_in, n_ref, m_ref, w_ref, seg, sseg, ctx, st, b_ref, a_ref, late_ref,
                           om, ot, mm, mt, *scr):
    join_rows(core[0], mine_in, theirs_in, b_ref)
    cross_bwd_core(core, win, b_ref, n_ref, m_ref, away_weights(w_ref), seg, sseg, ctx, st, None, None, a_ref,
                   put_plain(late_ref, 192), om, ot, mm, mt, *scr)


def cross_bwd_second_kernel(core, win, b_ref, bm, bt, cm, ct, n_ref, m_ref, wq, wkv, wo, seg, sseg, ctx, st,
                            a_ref, late_ref, om, ot, mm, mt, *scr):
    cross_bwd_core(core, win, b_ref, n_ref, m_ref, own_weights(1, wq, wkv, wo), seg, sseg, ctx, st, (bm, bt), (cm, ct),
                   a_ref, put_plain(late_ref, 192), om, ot, mm, mt, *scr)


def cross_bwd_first(core, win, mine, theirs, n, mem, w, seg, sseg, ctx, st):
    return call(cross_bwd_first_kernel, "cross_bwd", (core, win, mine, theirs, n, mem, w, seg, sseg, ctx, st),
                [sd((SLOT, 768), bf16), PART, PART, HALF32, HALF32, HALFMEM, HALFMEM], CROSS_BWD_SCRATCH, 2, vmem=18)


def cross_bwd_second(core, win, b, before, n, mem, weights, seg, sseg, ctx, st):
    return call(cross_bwd_second_kernel, "cross_bwd",
                (core, win, b) + tuple(before) + (n, mem) + weights + (seg, sseg, ctx, st),
                [PART, PART, HALF32, HALF32, HALFMEM, HALFMEM], CROSS_BWD_SCRATCH, 2, vmem=18)


GELU_C = math.sqrt(2.0 / math.pi)


def ffn_rows(n_ref, c_ref, wg, wu, wo, o_ref, t_ref, before, h_ref, g_ref, u_ref, base):
    def block(i):
        rows = blk(i)
        keep = pl.ds(pl.multiple_of(base + i * BQ, BQ), BQ)
        n = n_ref[rows, :]
        gate, up = dg(n, wg[...], NN), dg(n, wu[...], NN)
        hid = dg(c_ref[rows, :], wo[...], NT)
        square = gate * gate
        th = jnp.tanh(GELU_C * (gate + 0.044715 * (gate * square)))
        half = 0.5 * (1.0 + th)
        gelu = gate * half
        slope = half + (0.5 * GELU_C) * gate * (1.0 - th * th) * (1.0 + (3 * 0.044715) * square)
        h = (gelu * up).astype(bf16)
        gg = (hid * up * slope).astype(bf16)
        ug = (hid * gelu).astype(bf16)
        h_ref[keep, :], g_ref[keep, :], u_ref[keep, :] = h, gg, ug
        out = dg(h, wo[...], NN)
        third = dg(gg, wg[...], NT) + dg(ug, wu[...], NT)
        if before is not None:
            out, third = out + before[0][rows, :], third + before[1][rows, :]
        o_ref[rows, :], t_ref[rows, :] = out, third
    loop(n_ref.shape[0] // BQ, block)


def ffn_weight_grads(na, nb, ca, cb, h_ref, g_ref, u_ref, a_ref, put_late):
    half = na.shape[0]

    def value(left, ra, rb):
        return (dg(left[0:half, :], ra[...], TN) + dg(left[half:2 * half, :], rb[...], TN)).astype(bf16)
    a_ref[0:512, :] = value(g_ref, na, nb)
    up = value(u_ref, na, nb)
    a_ref[512:768, :] = up[0:256]
    outer = value(h_ref, ca, cb)
    put_late(0, jnp.concatenate((up[256:512], outer[0:128])))
    put_late(1, outer[128:512])


def ffn_first_kernel(na, nb, ca, cb, wi, wo, oa, ob, ta, tb, a_ref, b_ref, h_ref, g_ref, u_ref):
    wg, wu = wi.at[0], wi.at[1]
    ffn_rows(na, ca, wg, wu, wo, oa, ta, None, h_ref, g_ref, u_ref, 0)
    ffn_rows(nb, cb, wg, wu, wo, ob, tb, None, h_ref, g_ref, u_ref, na.shape[0])
    ffn_weight_grads(na, nb, ca, cb, h_ref, g_ref, u_ref, a_ref, put_plain(b_ref, 384))


def ffn_first(na, nb, ca, cb, wi, wo):
    rows, units = na.shape[0], wo.shape[0]
    return call(ffn_first_kernel, "ffn_first", (na, nb, ca, cb, wi, wo),
                [sd((rows, 768), f32)] * 4 + [STACK] * 2, [pltpu.VMEM((2 * rows, units), bf16)] * 3,
                vmem=20)


def ffn_second_kernel(bits, na, nb, ca, cb, wa0, wa1, wb0, wb1, pa, pb, sa, sb, own_b, oa, ob, ta, tb, a_ref, keep_ref,
                      give_ref, h_ref, g_ref, u_ref, w2, wo):
    for side, first, rest in ((bits[0], wa0, wa1), (1 - bits[0], wb0, wb1)):
        w2[side, 0:576, :] = first[...]
        w2[side, 576:768, :] = rest[0:192, :]
        at = pl.multiple_of(side * 256, 128)
        wo[pl.ds(at, 256), 0:512] = rest[192:448, :]
        wo[pl.ds(at, 128), 512:768] = rest[448:576, 0:256]
        wo[pl.ds(pl.multiple_of(at + 128, 128), 128), 512:768] = rest[448:576, 256:512]
    wg, wu = w2.at[0], w2.at[1]
    ffn_rows(na, ca, wg, wu, wo, oa, ta, (pa, sa), h_ref, g_ref, u_ref, 0)
    ffn_rows(nb, cb, wg, wu, wo, ob, tb, (pb, sb), h_ref, g_ref, u_ref, na.shape[0])
    bit = bits[0]

    def put(half, value):
        own = own_b[384 * half:384 * half + 384, :]
        for cond, ref in ((bit == half, keep_ref), (bit != half, give_ref)):
            @pl.when(cond)
            def _(ref=ref):
                ref[0:384, :] = own
                ref[384:768, :] = value
    ffn_weight_grads(na, nb, ca, cb, h_ref, g_ref, u_ref, a_ref, put)


def ffn_second(bits, na, nb, ca, cb, weights, before, own_b):
    rows, units = na.shape[0], weights[0].shape[1]
    return call(ffn_second_kernel, "ffn_second", (bits, na, nb, ca, cb) + tuple(weights) + tuple(before) + (own_b,),
                [sd((rows, 768), f32)] * 4 + [STACK] * 3,
                [pltpu.VMEM((2 * rows, units), bf16)] * 3 + [pltpu.VMEM((2, 768, units), bf16), pltpu.VMEM((units, 768), bf16)],
                1, vmem=22)


def merge_kernel(actions, outs):
    def kernel(bits, *refs):
        ins, dest = refs[:len(refs) - outs], refs[len(refs) - outs:]

        def total(terms, extra, count):
            value = None
            for src, at in terms:
                part = ins[src][pl.ds(pl.multiple_of(at + extra, 16), count), :].astype(f32)
                value = part if value is None else value + part
            return value.astype(bf16)

        for action in actions:
            if action[0] == "split":
                _, terms, count, bit, (keep, kat), (give, gat) = action
                half = count // 2
                dest[keep][kat:kat + half, :] = total(terms, bits[bit] * half, half)
                dest[give][gat:gat + half, :] = total(terms, (1 - bits[bit]) * half, half)
            elif action[0] == "sum":
                _, terms, count, (out, at) = action
                dest[out][at:at + count, :] = total(terms, 0, count)
            else:
                _, (own, own_at), (other, other_at), count, bit, (out, at) = action
                dest[out][pl.ds(pl.multiple_of(at + bits[bit] * count, 16), count), :] = ins[own][own_at:own_at + count, :]
                dest[out][pl.ds(pl.multiple_of(at + (1 - bits[bit]) * count, 16), count), :] = (
                    ins[other][other_at:other_at + count, :])
    return kernel


def merge(bits, ins, actions, sizes):
    outs = [sd((rows, 768), bf16) for rows in sizes]
    return call(merge_kernel(actions, len(outs)), "merge", (bits,) + tuple(ins), outs, (), 1, vmem=16)


def ffn_finish_kernel(bits, fin, y_in, z_in, gi, go, model, unit, scr):
    def place(base, bit, own, other):
        scr[pl.ds(pl.multiple_of(base + bit * 384, 16), 384), :] = own
        scr[pl.ds(pl.multiple_of(base + (1 - bit) * 384, 16), 384), :] = other
    place(0, bits[1], fin[0:384, :], z_in[...])
    place(768, bits[0], fin[384:768, :], y_in[...])
    for j in range(3):
        g = scr[512 * j:512 * j + 512, :].astype(f32)
        if j < 2:
            gi[j] = jnp.transpose(g)
        else:
            go[...] = g
        sq = g * g
        model[j:j + 1, :] = jnp.sum(sq, axis=0, keepdims=True)
        unit[j:j + 1, :] = jnp.transpose(jnp.sum(sq, axis=1, keepdims=True)) * (1.0 / D)


def ffn_finish(bits, fin, y_in, z_in):
    units = 512
    return call(ffn_finish_kernel, "ffn_finish", (bits, fin, y_in, z_in),
                [sd((2, 768, units), f32), sd((units, 768), f32), sd((3, 768), f32), sd((3, units), f32)],
                [pltpu.VMEM((3 * units, 768), bf16)], 1, vmem=20)


def finish_kernel(bits, s_fin, s_y, s_z, c_fin, c_y, c_z, fm_ref, qg, kvg, og, model, head, proj, scr):
    for a, (fin, y_in, z_in) in enumerate(((s_fin, s_y, s_z), (c_fin, c_y, c_z))):
        for base, bit, own, other in ((0, bits[1], fin[0:192, :], z_in), (384, bits[0], fin[192:384, :], y_in)):
            scr[pl.ds(pl.multiple_of(base + bit * 192, 16), 192), :] = own
            scr[pl.ds(pl.multiple_of(base + (1 - bit) * 192, 16), 192), :] = other[...]
        for j, (out, row) in enumerate(((qg.at[a], a), (kvg.at[a, 0], 2 + 2 * a), (kvg.at[a, 1], 3 + 2 * a),
                                        (og.at[a], 8 + a))):
            w = scr[192 * j:192 * j + 192, :].astype(f32)
            out[...] = w
            sq = w * w
            model[row:row + 1, :] = jnp.sum(sq, axis=0, keepdims=True)
            side = jnp.transpose(jnp.sum(sq, axis=1, keepdims=True)) * (1.0 / D)
            if j < 3:
                head[row:row + 1, :] = side
            else:
                proj[a:a + 1, :] = side
    model[6:8, :] = fm_ref[0:2, :]
    model[10:11, :] = fm_ref[2:3, :]


def finish(bits, self_parts, cross_parts, ffn_model):
    outs = [sd((2, 192, 768), f32), sd((2, 2, 192, 768), f32), sd((2, 192, 768), f32), sd((11, 768), f32),
            sd((6, 192), f32), sd((2, 192), f32)]
    return call(finish_kernel, "finish", (bits,) + tuple(self_parts) + tuple(cross_parts) + (ffn_model,), outs,
                [pltpu.VMEM((768, 768), bf16)], 1, vmem=16)


CORE = [(i, i ^ 1) for i in range(4)]
CHIP = [(i, i ^ 2) for i in range(4)]


def swap_core(v):
    return lax.ppermute(v, "tensor", CORE)


def swap_chip(v):
    return lax.ppermute(v, "tensor", CHIP)


def swap_dp(v, bit):
    return lax.ppermute(v, "dp", [(i, i ^ (1 << bit)) for i in range(lax.axis_size("dp"))])


def dp_bits():
    return int(math.log2(lax.axis_size("dp")))


def after(value, *earlier):
    return lax.optimization_barrier((value,) + earlier)[0]


def sync(*values):
    return lax.optimization_barrier(values)


def past(value, bit):
    for one in range(bit, dp_bits()):
        value = (value.astype(f32) + swap_dp(value, one).astype(f32)).astype(bf16)
    return value


def bucket_sums(lane_sums):
    lane = np.arange(1024)
    distance = 512 - np.where(lane < 768, lane, lane - 1024)
    buckets = jnp.asarray(np.array([bucket_of(max(int(n), 0)) for n in distance], np.int32))
    onehot = (buckets[:, None] == jnp.arange(BUCKETS)[None, :]) & jnp.asarray(distance >= 0)[:, None]
    return lax.dot_general(onehot.astype(f32), lane_sums, (((0,), (1,)), ((), ())), precision=lax.Precision.HIGHEST,
                           preferred_element_type=f32)


def on_device(tokens, memory, cotangent, norm_gains, query_weight, keyvalue_weight, output_weight, bias_table,
              inner_weight, outer_weight, target_lengths, source_lengths):
    t, d = lax.axis_index("tensor"), lax.axis_index("dp")
    core = (t & 1).reshape(1).astype(i32)
    slot = lax.shift_right_logical(t, 1).reshape(1).astype(i32)
    bits = (lax.shift_right_logical(d, jnp.arange(3)) & 1).astype(i32)
    gains = [norm_gains[i:i + 1] for i in range(3)]
    weights = (jnp.swapaxes(query_weight, 1, 2), jnp.swapaxes(keyvalue_weight, 2, 3), output_weight)

    def y_half(i):
        low = jnp.concatenate((weights[0][i], weights[1][i, 0]))
        return jnp.where(bits[0] == 0, low, jnp.concatenate((weights[1][i, 1], weights[2][i])))

    half_self = y_half(0)
    wa = swap_chip(half_self)
    tokens = sync(tokens, half_self)[0]
    n1m = norm_rows(tokens, gains[0])
    n1t = swap_core(n1m)
    table_away = swap_chip(bias_table)
    seg, sseg, swin, cwin = slot_layout(slot, target_lengths, source_lengths)
    n1, ctx_s0, st_s0, pm, pt = self_fwd_first(core, swin, bias_table, n1m, n1t, weights, seg)
    half_cross = y_half(1)
    wa, n1, half_cross, memory, cotangent = sync(wa, n1, half_cross, memory, cotangent)
    wb = swap_dp(wa, 0)
    ca = swap_chip(half_cross)
    mem_t, cot_t = swap_core(memory), swap_core(cotangent)
    half_fa, half_fb = packed(bits, inner_weight, outer_weight)
    wb, ca, half_fa, half_fb, n1 = sync(wb, ca, half_fa, half_fb, n1)
    cb = swap_dp(ca, 0)
    fa0 = swap_chip(half_fa)
    w_self_away, ctx_s1, st_s1, pm, pt = self_fwd_second(core, swin, table_away, bits, n1, pm, pt, wa, wb, seg)
    pm, pt, cb, fa0 = sync(pm, pt, cb, fa0)
    fb0 = swap_dp(fa0, 0)
    fa1 = swap_chip(half_fb)
    after_self, n2m = add_norm(tokens, pm, swap_core(pt), gains[1])

    n2, mem, w_cross_away, ctx_c0, st_c0, ctx_c1, st_c1, pm, pt = cross_fwd(
        core, cwin, bits, n2m, swap_core(n2m), memory, mem_t, weights, ca, cb, seg, sseg)
    pm, pt, fb0, fa1 = sync(pm, pt, fb0, fa1)
    fb1 = swap_dp(fa1, 0)
    after_cross, n3m = add_norm(after_self, pm, swap_core(pt), gains[2])

    n3t = swap_core(n3m)
    oa, ob, ta, tb, f_a, f_b = ffn_first(n3m, n3t, cotangent, cot_t, inner_weight, outer_weight)
    fb1, n3m, n3t, f_a = sync(fb1, n3m, n3t, f_a)
    oa, ob, ta, tb, f_out, f_keep, f_give = ffn_second(bits, n3m, n3t, cotangent, cot_t, (fa0, fa1, fb0, fb1),
                                                       (oa, ob, ta, tb), f_b)
    fx, fy = swap_chip(f_out), swap_dp(f_give, 0)
    cross_out_m, branch_m, gain2 = norm_back(after_cross, gains[2], cotangent, ta, swap_core(tb))

    branch, c_out, c_late, pm, pt, mm, mt = cross_bwd_first(core, cwin, branch_m, swap_core(branch_m), n2, mem,
                                                            w_cross_away, seg, sseg, ctx_c1, st_c1)
    branch, c_out, c_late, pm, pt, mm, mt, fx, fy = sync(branch, c_out, c_late, pm, pt, mm, mt, fx, fy)
    fa_k, zp, xp, fb_o, cb_k, yp = merge(
        bits, (f_a, fx, f_keep, fy, c_late),
        (("split", ((0, 0), (1, 0)), 768, 1, (0, 0), (1, 0)),
         ("sum", ((2, 384), (3, 384)), 384, (2, 0)),
         ("sum", ((2, 0), (3, 0)), 384, (3, 0)),
         ("split", ((4, 0),), 384, 0, (4, 0), (5, 0))), (384, 384, 384, 384, 192, 192))
    xi, yi, zi = swap_chip(xp), swap_dp(yp, 0), swap_dp(zp, 1)
    branch, zp = sync(branch, zp)
    c_a, c_own, pm, pt, mm, mt = cross_bwd_second(core, cwin, branch, (pm, pt, mm, mt), n2, mem, weights, seg, sseg,
                                                  ctx_c0, st_c0)
    c_a, c_own, pm, pt, mm, mt, xi, yi, zi, c_out = sync(c_a, c_own, pm, pt, mm, mt, xi, yi, zi, c_out)
    fa_k, fb_k, cb_o, xp, yp, zp = merge(
        bits, (fa_k, zi, fb_o, xi, c_out, cb_k, yi, c_own),
        (("split", ((0, 0), (1, 0)), 384, 0, (0, 0), (4, 0)),
         ("split", ((2, 0), (3, 0)), 384, 1, (1, 0), (5, 0)),
         ("sum", ((4, 0),), 384, (3, 0)),
         ("sum", ((5, 0), (6, 0)), 192, (3, 384)),
         ("split", ((7, 0),), 384, 0, (2, 0), (4, 192))), (192, 192, 192, 576, 384, 192))
    xi, yi, zi = swap_chip(xp), swap_dp(yp, 0), swap_dp(zp, 1)
    self_out_m, branch_m, gain1 = norm_back(after_self, gains[1], cross_out_m, pm, swap_core(pt))

    branch, s_out, s_late, pm, pt, lanes_away = self_bwd_first(core, swin, table_away, branch_m, swap_core(branch_m), n1,
                                                               w_self_away, seg, ctx_s1, st_s1)
    branch, s_out, s_late, pm, pt, lanes_away, xi, yi, zi = sync(
        branch, s_out, s_late, pm, pt, lanes_away, xi, yi, zi)
    f_k, ca_k, cb_k, sb_k, z2p, zp, yp = merge(
        bits, (fa_k, yi, fb_k, zi, c_a, xi, cb_o, s_late),
        (("split", ((0, 0), (1, 0)), 192, 2, (0, 0), (4, 0)),
         ("split", ((2, 0), (3, 0)), 192, 2, (0, 96), (4, 96)),
         ("split", ((4, 0), (5, 0)), 384, 1, (1, 0), (5, 0)),
         ("split", ((6, 0), (1, 192), (5, 384)), 192, 1, (2, 0), (5, 192)),
         ("split", ((7, 0),), 384, 0, (3, 0), (6, 0))), (192, 192, 96, 192, 192, 288, 192))
    xi, yi, zi, z2i = swap_chip(s_out), swap_dp(yp, 0), swap_dp(zp, 1), swap_dp(z2p, 2)
    lanes_in = swap_chip(lanes_away)
    branch, zp = sync(branch, zp)
    s_a, s_own, pm, pt, lanes_own = self_bwd_second(core, swin, bias_table, branch, pm, pt, n1, weights, seg, ctx_s0, st_s0)
    s_a, s_own, pm, pt, lanes_own, lanes_in, xi, yi, zi, z2i = sync(
        s_a, s_own, pm, pt, lanes_own, lanes_in, xi, yi, zi, z2i)

    f_own, ca_k, cb_k, sa_k, sb_o, xp, yp, zp = merge(
        bits, (f_k, z2i, ca_k, zi, cb_k, s_a, xi, sb_k, yi, s_own),
        (("sum", ((0, 0), (1, 0)), 192, (0, 0)),
         ("split", ((2, 0), (3, 0)), 192, 0, (1, 0), (6, 0)),
         ("sum", ((4, 0), (3, 192)), 96, (2, 0)),
         ("split", ((5, 0), (6, 0)), 384, 1, (3, 0), (7, 0)),
         ("sum", ((7, 0), (8, 0)), 192, (5, 0)),
         ("split", ((9, 0),), 384, 0, (4, 0), (6, 96))), (192, 96, 96, 192, 192, 192, 288, 192))
    f_own = past(f_own, 3)
    yi, zi, z2i, xi = swap_dp(yp, 0), swap_dp(zp, 1), swap_dp(f_own, 2), swap_chip(xp)
    pt_in, mt_in, ob_in = swap_core(pt), swap_core(mt), swap_core(ob)
    tokens_grad, _, gain0 = norm_back(tokens, gains[0], self_out_m, pm, pt_in)
    small = jnp.concatenate((gain0, gain1, gain2))
    yi, zi, z2i, xi, small = sync(yi, zi, z2i, xi, small)
    f_own, c_mid, sa_k, sb_k, yp, zp = merge(
        bits, (f_own, z2i, ca_k, yi, cb_k, sa_k, zi, sb_o, xi),
        (("join", (0, 0), (1, 0), 96, 2, (0, 0)),
         ("join", (0, 96), (1, 96), 96, 2, (0, 192)),
         ("join", (0, 0), (1, 0), 96, 2, (4, 0)),
         ("join", (0, 96), (1, 96), 96, 2, (5, 0)),
         ("sum", ((2, 0), (3, 0)), 96, (1, 0)),
         ("sum", ((4, 0),), 96, (1, 96)),
         ("split", ((5, 0), (6, 0)), 192, 0, (2, 0), (4, 192)),
         ("split", ((7, 0), (3, 96), (8, 0)), 192, 1, (3, 0), (5, 192))), (384, 192, 96, 96, 288, 288))
    yi, zi, z2i = swap_dp(yp, 0), swap_dp(zp, 1), swap_dp(c_mid, 2)
    small = small + swap_core(small)
    memory_grad = mm + mt_in
    output_rows = (after_cross + (oa + ob_in)).astype(bf16)
    yi, zi, z2i, small, memory_grad, output_rows = sync(yi, zi, z2i, small, memory_grad, output_rows)
    f_fin, c_own, s_mid, yp, zp = merge(
        bits, (f_own, yi, zi, c_mid, z2i, sa_k, sb_k),
        (("join", (0, 0), (1, 0), 192, 0, (0, 0)),
         ("join", (0, 192), (2, 0), 192, 1, (0, 384)),
         ("join", (0, 0), (1, 0), 192, 0, (4, 0)),
         ("join", (0, 192), (2, 0), 192, 1, (3, 0)),
         ("sum", ((3, 0), (4, 0)), 192, (1, 0)),
         ("sum", ((3, 0), (4, 0)), 96, (3, 384)),
         ("sum", ((3, 96), (4, 96)), 96, (4, 384)),
         ("sum", ((5, 0), (1, 192)), 96, (2, 0)),
         ("sum", ((6, 0), (2, 192)), 96, (2, 96))), (768, 192, 192, 480, 480))
    if dp_bits() > 3:
        c_own = past(c_own, 3)
        yp, zp = jnp.concatenate((yp[:384], c_own[:96])), jnp.concatenate((zp[:384], c_own[96:]))
    yi, zi, z2i = swap_dp(yp, 0), swap_dp(zp, 1), swap_dp(s_mid, 2)
    small = small + swap_chip(small)
    small = jnp.concatenate((jnp.pad(small, ((0, 0), (0, 256))), lanes_own + lanes_in))
    yi, zi, z2i, small = sync(yi, zi, z2i, small)
    f_y, f_z = yi[:384], zi[:384]
    c_fin, s_own, yp, zp = merge(
        bits, (c_own, yi, zi, s_mid, z2i),
        (("join", (0, 0), (1, 384), 96, 0, (0, 0)),
         ("join", (0, 96), (2, 384), 96, 1, (0, 192)),
         ("join", (0, 0), (1, 384), 96, 0, (3, 0)),
         ("join", (0, 96), (2, 384), 96, 1, (2, 0)),
         ("sum", ((3, 0), (4, 0)), 192, (1, 0)),
         ("sum", ((3, 0), (4, 0)), 96, (2, 192)),
         ("sum", ((3, 96), (4, 96)), 96, (3, 192))), (384, 192, 288, 288))
    if dp_bits() > 3:
        s_own = past(s_own, 3)
        yp, zp = jnp.concatenate((yp[:192], s_own[:96])), jnp.concatenate((zp[:192], s_own[96:]))
    yi, zi = swap_dp(yp, 0), swap_dp(zp, 1)
    inner_sum, outer_sum, ffn_model, unit_stats = ffn_finish(bits, f_fin, f_y, f_z)
    small = small + swap_dp(small, 0)
    yi, zi, ffn_model, small = sync(yi, zi, ffn_model, small)
    c_y, c_z = yi[:192], zi[:192]
    s_fin, yp, zp = merge(
        bits, (s_own, yi, zi),
        (("join", (0, 0), (1, 192), 96, 0, (0, 0)),
         ("join", (0, 96), (2, 192), 96, 1, (0, 192)),
         ("join", (0, 0), (1, 192), 96, 0, (2, 0)),
         ("join", (0, 96), (2, 192), 96, 1, (1, 0))), (384, 192, 192))
    s_y, s_z = swap_dp(yp, 0), swap_dp(zp, 1)
    for bit in range(1, dp_bits()):
        small = small + swap_dp(small, bit)
    gains_total = small[:3, :D]
    table_sum = bucket_sums(small[3:])
    query_t, keyvalue_t, output_grad, model_part, head_stats, projection_stats = finish(
        bits, (s_fin, s_y, s_z), (c_fin, c_y, c_z), ffn_model)
    query_grad, keyvalue_grad = jnp.swapaxes(query_t, 1, 2), jnp.swapaxes(keyvalue_t, 2, 3)
    diagonal = lax.ppermute(model_part, "tensor", [(i, i ^ 3) for i in range(4)])
    model_total = (model_part + swap_core(model_part)) + (swap_chip(model_part) + diagonal)
    hidden_units = outer_weight.shape[0] * lax.axis_size("tensor")
    divisors = jnp.array([D] * 6 + [hidden_units] * 2 + [D] * 2 + [hidden_units], f32)
    model_stats = model_total / divisors[:, None]
    return (output_rows, tokens_grad, memory_grad, gains_total, query_grad, keyvalue_grad, output_grad, table_sum,
            inner_sum, outer_sum, model_stats, head_stats, projection_stats, unit_stats)


def solution(mesh):
    rows = P(("dp", "tensor"), None)
    in_specs = (rows, rows, rows, P(), P(None, None, "tensor"), P(None, None, None, "tensor"), P(None, "tensor", None),
                P(None, "tensor"), P(None, None, "tensor"), P("tensor", None), P("dp", None), P("dp", None))
    out_specs = (rows, rows, rows, P(), P(None, None, "tensor"), P(None, None, None, "tensor"),
                 P(None, "tensor", None), P(None, "tensor"), P(None, None, "tensor"), P("tensor", None), P(),
                 P(None, "tensor"), P(None, "tensor"), P(None, "tensor"))
    return jax.shard_map(on_device, mesh=mesh, in_specs=in_specs, out_specs=out_specs, check_vma=False)
```

```python
import math

import jax
import jax.numpy as jnp
import numpy as np
from jax import lax
from jax.experimental import pallas as pl
from jax.experimental.pallas import tpu as pltpu
from jax.sharding import PartitionSpec as P

D = 768
DH = 64
BUCKETS = 32
MAXDIST = 128
SLOT = 1024
MEM = 512
NORM_EPS = 1e-06
NEG_FILL = -1e30
DEAD = 1 << 20
BQ = 256
COST = 0.02
VM = pl.BlockSpec(memory_space=pltpu.VMEM)
SM = pl.BlockSpec(memory_space=pltpu.SMEM)
NT = (((1,), (1,)), ((), ()))
NN = (((1,), (0,)), ((), ()))
TN = (((0,), (0,)), ((), ()))
f32, bf16, i32 = jnp.float32, jnp.bfloat16, jnp.int32
SELF_W = (256, 384, 512, 768)
CROSS_W = (128, 256, 512)
sd = jax.ShapeDtypeStruct


def dg(a, b, dims):
    return lax.dot_general(a, b, dims, preferred_element_type=f32)


def blk(i):
    return pl.ds(pl.multiple_of(i * BQ, BQ), BQ)


def loop(count, body):
    def step(i, carry):
        body(i)
        return carry
    lax.fori_loop(0, count, step, 0)


def call(kernel, name, args, outs, scratch=(), scalars=0, vmem=12, flops=1e9, out_specs=None):
    byts = sum(int(np.prod(a.shape)) * a.dtype.itemsize for a in tuple(args) + tuple(outs))
    return pl.pallas_call(
        kernel,
        in_specs=[SM] * scalars + [VM] * (len(args) - scalars),
        out_specs=list(out_specs) if out_specs else [VM] * len(outs),
        out_shape=list(outs),
        scratch_shapes=list(scratch),
        name=name,
        compiler_params=pltpu.CompilerParams(vmem_limit_bytes=vmem << 20),
        cost_estimate=pl.CostEstimate(flops=int(flops * COST), bytes_accessed=int(byts * COST), transcendentals=0),
    )(*args)


def bucket_of(spread):
    exact_count = BUCKETS // 2
    if spread < exact_count:
        return spread
    larger = exact_count + math.floor(
        math.log(spread / exact_count) / math.log(MAXDIST / exact_count) * (BUCKETS - exact_count)
    )
    return min(larger, BUCKETS - 1)


def bucket_starts():
    buckets = [bucket_of(n) for n in range(SLOT)]
    return [next(n for n in range(SLOT + 1) if n == SLOT or buckets[n] >= b) for b in range(BUCKETS)]


def layout_kernel(slot, tl_ref, sl_ref, seg_ref, sseg_ref, swin, cwin):
    s = slot[0]
    docs = tl_ref.shape[1]
    tl = [tl_ref[s, j] for j in range(docs)]
    sl = [sl_ref[s, j] for j in range(docs)]
    ends, sends = [], []
    te, se = jnp.int32(0), jnp.int32(0)
    for j in range(docs):
        te, se = te + tl[j], se + sl[j]
        ends.append(te)
        sends.append(se)
    pos = lax.broadcasted_iota(i32, (1, SLOT), 1)
    spos = lax.broadcasted_iota(i32, sseg_ref.shape, 1)
    start, seg, mseg = jnp.zeros_like(pos), jnp.ones_like(pos), jnp.ones_like(spos)
    for j in range(docs):
        past = pos >= ends[j]
        start = jnp.where(past, ends[j], start)
        seg = seg + past.astype(i32)
        mseg = mseg + (spos >= sends[j]).astype(i32)
    live = pos < te
    seg_ref[...] = jnp.zeros(seg_ref.shape, i32)
    seg_ref[0:1, :] = jnp.where(live, start, DEAD)
    seg_ref[1:2, :] = jnp.where(live, seg, -1)
    sseg_ref[...] = jnp.where(spos < se, mseg, 0)
    for i in range(SLOT // BQ):
        q0 = i * BQ
        first, low, high = jnp.int32(0), jnp.int32(0), jnp.int32(0)
        last = jnp.minimum(q0 + BQ - 1, te - 1)
        for j in range(docs):
            before = ends[j] <= q0
            first = jnp.where(before, ends[j], first)
            low = low + jnp.where(before, sl[j], 0)
            high = high + jnp.where(ends[j] - tl[j] <= last, sl[j], 0)
        need = q0 + BQ - lax.shift_left(lax.shift_right_logical(first, 7), 7)
        width = jnp.int32(1)
        for w in SELF_W[:-1]:
            width = width + jnp.where(need > w, 1, 0)
        swin[i] = jnp.where(q0 < te, width, 0)
        at1 = lax.shift_left(lax.shift_right_logical(low, 7), 7)
        at2 = jnp.minimum(at1, MEM - 256)
        one, two = high - at1 <= 128, high - at2 <= 256
        cwin[0, i] = jnp.where(q0 < te, jnp.where(one, 1, jnp.where(two, 2, 3)), 0)
        cwin[1, i] = jnp.where(one, at1, jnp.where(two, at2, 0))


def slot_layout(slot, tl, sl):
    return call(layout_kernel, "layout", (slot, tl, sl),
                (sd((8, SLOT), i32), sd((1, MEM), i32), sd((4,), i32), sd((2, 4), i32)),
                scalars=3, flops=1e6, out_specs=(VM, VM, SM, SM))


def quarter_of(bits, step):
    y, z = bits[0], bits[1]
    return (1 - y if step & 1 else y), (1 - z if step & 2 else z)


def quarters_kernel(bits, q_ref, kv_ref, o_ref, out):
    n = bits[0] + 2 * bits[1]
    for cond, ref in ((n == 0, q_ref.at[0]), ((n == 1) | (n == 2), kv_ref.at[0, 0]), (n == 3, o_ref.at[0])):
        @pl.when(cond)
        def _(ref=ref):
            out[0] = ref[...]


def weight_quarters(bits, q, kv, o):
    one = (1, 192, 768)
    both = pl.pallas_call(
        quarters_kernel,
        grid_spec=pltpu.PrefetchScalarGridSpec(
            num_scalar_prefetch=1, grid=(2,),
            in_specs=[pl.BlockSpec(one, lambda i, bits: (i, 0, 0)),
                      pl.BlockSpec((1, 1, 192, 768), lambda i, bits: (i, jnp.where(bits[0] + 2 * bits[1] == 2, 1, 0), 0, 0)),
                      pl.BlockSpec(one, lambda i, bits: (i, 0, 0))],
            out_specs=pl.BlockSpec(one, lambda i, bits: (i, 0, 0))),
        out_shape=sd((2, 192, 768), bf16),
        name="quarters",
        compiler_params=pltpu.CompilerParams(vmem_limit_bytes=8 << 20),
        cost_estimate=pl.CostEstimate(flops=0, bytes_accessed=2400000, transcendentals=0))(bits, q, kv, o)
    return both[0], both[1]


def join_quarters(bits, parts, w_ref):
    for step, part in enumerate(parts[:3]):
        y, z = quarter_of(bits, step)
        w_ref[pl.ds(pl.multiple_of((y + 2 * z) * 192, 16), 192), :] = part[...]
    y, z = quarter_of(bits, 3)
    for n, part in enumerate(parts[3:]):
        w_ref[pl.ds(pl.multiple_of((y + 2 * z) * 192 + 96 * n, 16), 96), :] = part[...]


def pack_kernel(bits, wi_ref, wo_ref, f_ref):
    y, z = bits[0], bits[1]
    f_ref[0:384, :] = wi_ref[y, pl.ds(pl.multiple_of(z * 384, 128), 384), :]
    outer = wo_ref[pl.ds(pl.multiple_of((2 * y + z) * 128, 128), 128), :]
    f_ref[384:512, :] = outer[:, 0:512]
    f_ref[512:576, 0:256] = outer[0:64, 512:768]
    f_ref[512:576, 256:512] = outer[64:128, 512:768]


def packed(bits, wi, wo):
    return call(pack_kernel, "pack", (bits, wi, wo), (sd((576, 512), bf16),), (), 1)[0]


def own_weights(which, q_ref, kv_ref, o_ref):
    return (q_ref.at[which], kv_ref.at[which, 0], kv_ref.at[which, 1], o_ref.at[which])


def away_weights(w_ref):
    return tuple(w_ref.at[192 * j:192 * j + 192] for j in range(4))


def norm_kernel(x_ref, gain_ref, n_ref):
    x = x_ref[...].astype(f32)
    r = lax.rsqrt(jnp.mean(x * x, axis=-1, keepdims=True) + NORM_EPS)
    n_ref[...] = (x * r * gain_ref[...]).astype(bf16)


def norm_rows(x, gain):
    return call(norm_kernel, "norm", (x, gain), (sd(x.shape, bf16),), flops=1e6)[0]


def add_norm_kernel(x_ref, a_ref, b_ref, gain_ref, y_ref, n_ref):
    y = x_ref[...].astype(f32) + (a_ref[...] + b_ref[...])
    y_ref[...] = y
    r = lax.rsqrt(jnp.mean(y * y, axis=-1, keepdims=True) + NORM_EPS)
    n_ref[...] = (y * r * gain_ref[...]).astype(bf16)


def add_norm(x, a, b, gain):
    return call(add_norm_kernel, "add_norm", (x, a, b, gain), (sd(x.shape, f32), sd(x.shape, bf16)), flops=1e6)


def norm_back_kernel(terms):
    def kernel(v_ref, gain_ref, up_ref, *refs):
        total_ref, branch_ref, sum_ref = refs[terms:]
        grad = refs[0][...].astype(f32)
        for ref in refs[1:terms]:
            grad = grad + ref[...].astype(f32)
        v = v_ref[...].astype(f32)
        r = lax.rsqrt(jnp.mean(v * v, axis=-1, keepdims=True) + NORM_EPS)
        scaled = grad * gain_ref[...]
        back = r * scaled - v * ((r * r * r) * jnp.mean(scaled * v, axis=-1, keepdims=True))
        total = up_ref[...].astype(f32) + back
        total_ref[...] = total
        branch_ref[...] = total.astype(bf16)
        sum_ref[...] = jnp.sum(grad * v * r, axis=0, keepdims=True)
    return kernel


def norm_back(v, gain, up, *grads):
    return call(norm_back_kernel(len(grads)), "norm_back", (v, gain, up) + grads,
                (sd(v.shape, f32), sd(v.shape, bf16), sd((1, v.shape[1]), f32)), flops=1e6)


LANES = (slice(0, 128), slice(0, 128), slice(128, 192))


def head_of(rows128, h):
    if h == 2:
        return rows128
    lane = lax.broadcasted_iota(i32, rows128.shape, 1)
    return jnp.where((lane < 64) == (h == 0), rows128, jnp.zeros_like(rows128))


def pair_of(first, second):
    lane = lax.broadcasted_iota(i32, first.shape, 1)
    return jnp.where(lane < 64, first, second)


def half_rows(ref, which):
    half = ref.shape[0] // 2
    return ref[pl.ds(pl.multiple_of(which * half, half), half), :]


def join_rows(core, mine_ref, theirs_ref, all_ref):
    half = mine_ref.shape[0]
    at = pl.multiple_of(core * half, half)
    all_ref[pl.ds(at, half), :] = mine_ref[...]
    all_ref[pl.ds(pl.multiple_of(half - at, half), half), :] = theirs_ref[...]


def out_split(core, mine_ref, theirs_ref, before, value_of):
    for pos, ref in enumerate((mine_ref, theirs_ref)):
        value = value_of(core if pos == 0 else 1 - core)
        ref[...] = value if before is None else value + before[pos][...]


def fill_bias(table, bias_scr):
    lane = lax.broadcasted_iota(i32, (1, 1024), 1)
    distance = 512 - jnp.where(lane < 768, lane, lane - 1024)
    for h in range(3):
        row = jnp.full((1, 1024), table[0, h], f32)
        for b, first in enumerate(bucket_starts()):
            if b > 0:
                row = jnp.where(distance >= first, table[b, h], row)
        row = jnp.where(distance < 0, NEG_FILL, row)
        wide = jnp.broadcast_to(row, (BQ, 1024))
        bias_scr[h] = pltpu.roll(wide, 0, 1, stride=1, stride_axis=0)[:, :768]


def attend(scores, v_ref, keys, rows, live, ctx_ref, st_ref):
    s = [scores(h) for h in range(3)]
    m = [jnp.max(x, axis=1, keepdims=True) for x in s]
    e = [jnp.exp(x - y) for x, y in zip(s, m)]
    total = [jnp.sum(x, axis=1, keepdims=True) for x in e]
    p = [(x * (1.0 / y)).astype(bf16) for x, y in zip(e, total)]
    c = [dg(p[h], v_ref[keys, LANES[h]], NN) for h in range(3)]
    ctx_ref[rows, 0:128] = jnp.where(live, pair_of(c[0], c[1]), 0.0).astype(bf16)
    ctx_ref[rows, 128:192] = jnp.where(live, c[2], 0.0).astype(bf16)
    for h in range(3):
        st_ref[rows, h:h + 1] = m[h] + jnp.log(total[h])


def attend_back(scores, q_ref, k_ref, v_ref, g, keys, rows, st_ref, dq, dk, dv, extra):
    gs = [head_of(g[:, LANES[h]], h) for h in range(3)]
    s = [scores(h) for h in range(3)]
    wg = [dg(gs[h], v_ref[keys, LANES[h]], NT) for h in range(3)]
    p = [jnp.exp(s[h] - st_ref[rows, h:h + 1]) for h in range(3)]
    inner = [jnp.sum(p[h] * wg[h], axis=1, keepdims=True) for h in range(3)]
    sg = [(p[h] * (wg[h] - inner[h])).astype(bf16) for h in range(3)]
    p16 = [x.astype(bf16) for x in p]
    dvs = [dg(p16[h], gs[h], TN) for h in range(3)]
    dks = [dg(sg[h], head_of(q_ref[rows, LANES[h]], h), TN) for h in range(3)]
    dqs = [dg(sg[h], k_ref[keys, LANES[h]], NN) for h in range(3)]
    dv[keys, 0:128] += dvs[0] + dvs[1]
    dv[keys, 128:192] += dvs[2]
    dk[keys, 0:128] += dks[0] + dks[1]
    dk[keys, 128:192] += dks[2]
    dq[rows, 0:128] = pair_of(dqs[0], dqs[1]).astype(bf16)
    dq[rows, 128:192] = dqs[2].astype(bf16)
    extra(sg)


def self_scores(q_ref, k_ref, bias_scr, ds, q0, rows, keys, width):
    kpos = lax.broadcasted_iota(i32, (BQ, width), 1) + (q0 + BQ - width)
    shut = jnp.where(kpos >= ds, 0.0, NEG_FILL)
    return lambda h: dg(head_of(q_ref[rows, LANES[h]], h), k_ref[keys, LANES[h]], NT) + (
        bias_scr[h, :, 768 - width:] + shut)


def cross_scores(q_ref, k_ref, tseg, sseg, rows, keys):
    shut = jnp.where(tseg == sseg, 0.0, NEG_FILL)
    return lambda h: dg(head_of(q_ref[rows, LANES[h]], h), k_ref[keys, LANES[h]], NT) + shut


def project(n_ref, ws, *outs):
    for j, out in outs:
        out[...] = dg(n_ref[...], ws[j][...], NT).astype(bf16)


def self_attend(core, win, table, n_ref, ws, cols, before, ctx_ref, st_ref, om, ot, bias_scr, q, k, v, st):
    fill_bias(table, bias_scr)
    project(n_ref, ws, (0, q), (1, k), (2, v))

    def block(i):
        q0 = pl.multiple_of(i * BQ, BQ)
        rows = pl.ds(q0, BQ)

        @pl.when(win[i] == 0)
        def _():
            ctx_ref[rows, :] = jnp.zeros((BQ, 192), bf16)
            st[rows, :] = jnp.zeros((BQ, 8), f32)

        for n, width in enumerate(SELF_W):
            @pl.when(win[i] == n + 1)
            def _(width=width):
                keys = pl.ds(pl.multiple_of(q0 + (BQ - width), 128), width)
                ds = cols[rows, 0:1]
                attend(self_scores(q, k, bias_scr, ds, q0, rows, keys, width), v, keys, rows, ds < DEAD, ctx_ref, st)
    loop(SLOT // BQ, block)
    st_ref[...] = jnp.transpose(st[...])
    out_split(core[0], om, ot, before, lambda c: dg(half_rows(ctx_ref, c), ws[3][...], NN))


def self_fwd_first_kernel(core, win, table, mine_in, theirs_in, wq, wkv, wo, seg, n_ref, ctx, st, om, ot, cols, *scr):
    cols[...] = jnp.transpose(seg[...])
    join_rows(core[0], mine_in, theirs_in, n_ref)
    self_attend(core, win, table, n_ref, own_weights(0, wq, wkv, wo), cols, None, ctx, st, om, ot, *scr)


def self_fwd_second_kernel(core, win, table, bits, n_ref, bm, bt, w0, wy, wz, wd, we, seg, w_ref, ctx, st, om, ot, cols,
                           *scr):
    cols[...] = jnp.transpose(seg[...])
    join_quarters(bits, (w0, wy, wz, wd, we), w_ref)
    self_attend(core, win, table, n_ref, away_weights(w_ref), cols, (bm, bt), ctx, st, om, ot, *scr)


HALF32 = sd((SLOT // 2, 768), f32)
ATT = [sd((SLOT, 192), bf16), sd((8, SLOT), f32)]
STACK = sd((768, 768), bf16)
WIDE16, WIDE32 = pltpu.VMEM((SLOT, 192), bf16), pltpu.VMEM((SLOT, 192), f32)
MEM16, MEM32 = pltpu.VMEM((MEM, 192), bf16), pltpu.VMEM((MEM, 192), f32)
BIAS = pltpu.VMEM((3, BQ, 768), f32)
COLS, STATS = pltpu.VMEM((SLOT, 8), i32), pltpu.VMEM((SLOT, 8), f32)


def self_fwd_first(core, win, table, mine, theirs, weights, seg):
    return call(self_fwd_first_kernel, "self_fwd", (core, win, table, mine, theirs) + weights + (seg,),
                [sd((SLOT, 768), bf16)] + ATT + [HALF32, HALF32], [COLS, BIAS, WIDE16, WIDE16, WIDE16, STATS], 3, vmem=14)


def self_fwd_second(core, win, table, bits, n, bm, bt, parts, seg):
    return call(self_fwd_second_kernel, "self_fwd", (core, win, table, bits, n, bm, bt) + tuple(parts) + (seg,),
                [STACK] + ATT + [HALF32, HALF32], [COLS, BIAS, WIDE16, WIDE16, WIDE16, STATS], 4, vmem=14)


def diagonal_sums(scr, h):
    span = scr.shape[2]
    slabs = [scr[h, 8 * a:8 * a + 8, :] for a in range(BQ // 8)]
    step = 8
    while len(slabs) > 1:
        slabs = [slabs[j] + pltpu.roll(slabs[j + 1], span - step, 1) for j in range(0, len(slabs), 2)]
        step *= 2
    acc = slabs[0]
    row = lax.broadcasted_iota(i32, acc.shape, 0)
    for bit in (1, 2, 4):
        acc = jnp.where((row & bit) > 0, pltpu.roll(acc, span - bit, 1), acc)
    return jnp.sum(acc, axis=0, keepdims=True)


def weight_grads(dq, dk16, dv16, nq_ref, nk_ref, b_ref, ctx_ref, a_ref, put_late):
    a_ref[0:192, :] = dg(dq[...], nq_ref[...], TN).astype(bf16)
    a_ref[192:384, :] = dg(dk16[...], nk_ref[...], TN).astype(bf16)
    put_late(0, dg(dv16[...], nk_ref[...], TN).astype(bf16))
    put_late(1, dg(ctx_ref[...], b_ref[...], TN).astype(bf16))


def put_plain(ref, rows):
    def put(half, value):
        ref[rows * half:rows * half + rows, :] = value
    return put


def self_bwd_core(core, win, table, b_ref, n_ref, ws, seg, ctx_ref, st_ref, before, a_ref, put, om, ot, db_ref,
                  cols, st, bias_scr, dbias_scr, q, k, v, g_scr, dq, dk, dv, dk16, dv16):
    cols[...] = jnp.transpose(seg[...])
    st[...] = jnp.transpose(st_ref[...])
    fill_bias(table, bias_scr)
    project(n_ref, ws, (0, q), (1, k), (2, v))
    dbias_scr[...] = jnp.zeros(dbias_scr.shape, f32)
    dk[...] = jnp.zeros(dk.shape, f32)
    dv[...] = jnp.zeros(dv.shape, f32)
    g = dg(b_ref[...], ws[3][...], NT).astype(bf16)
    g_scr[...] = jnp.where(cols[:, 0:1] < DEAD, g, jnp.zeros_like(g))

    def block(i):
        q0 = pl.multiple_of(i * BQ, BQ)
        rows = pl.ds(q0, BQ)

        @pl.when(win[i] == 0)
        def _():
            dq[rows, :] = jnp.zeros((BQ, 192), bf16)

        for n, width in enumerate(SELF_W):
            @pl.when(win[i] == n + 1)
            def _(width=width):
                keys = pl.ds(pl.multiple_of(q0 + (BQ - width), 128), width)

                def extra(sg):
                    for h in range(3):
                        dbias_scr[h, :, 768 - width:768] += sg[h].astype(f32)
                attend_back(self_scores(q, k, bias_scr, cols[rows, 0:1], q0, rows, keys, width),
                            q, k, v, g_scr[rows, :], keys, rows, st, dq, dk, dv, extra)
    loop(SLOT // BQ, block)
    dk16[...] = dk[...].astype(bf16)
    dv16[...] = dv[...].astype(bf16)
    weight_grads(dq, dk16, dv16, n_ref, n_ref, b_ref, ctx_ref, a_ref, put)
    out_split(core[0], om, ot, before, lambda c: dg(half_rows(dq, c), ws[0][...], NN)
              + dg(half_rows(dk16, c), ws[1][...], NN) + dg(half_rows(dv16, c), ws[2][...], NN))
    for h in range(3):
        db_ref[h:h + 1, :] = diagonal_sums(dbias_scr, h)


SELF_BWD_SCRATCH = ([COLS, STATS, BIAS, pltpu.VMEM((3, BQ, 1024), f32)] + [WIDE16] * 5
                    + [WIDE32, WIDE32, WIDE16, WIDE16])
PART = sd((384, 768), bf16)


def self_bwd_first_kernel(core, win, table, mine_in, theirs_in, n_ref, w_ref, seg, ctx, st, b_ref, a_ref, late_ref,
                          om, ot, db_ref, *scr):
    join_rows(core[0], mine_in, theirs_in, b_ref)
    self_bwd_core(core, win, table, b_ref, n_ref, away_weights(w_ref), seg, ctx, st, None, a_ref, put_plain(late_ref, 192),
                  om, ot, db_ref, *scr)


def self_bwd_second_kernel(core, win, table, b_ref, bm, bt, n_ref, wq, wkv, wo, seg, ctx, st, a_ref, late_ref, om, ot,
                           db_ref, *scr):
    self_bwd_core(core, win, table, b_ref, n_ref, own_weights(0, wq, wkv, wo), seg, ctx, st, (bm, bt), a_ref,
                  put_plain(late_ref, 192), om, ot, db_ref, *scr)


def self_bwd_first(core, win, table, mine, theirs, n, w, seg, ctx, st):
    return call(self_bwd_first_kernel, "self_bwd", (core, win, table, mine, theirs, n, w, seg, ctx, st),
                [sd((SLOT, 768), bf16), PART, PART, HALF32, HALF32, sd((3, 1024), f32)], SELF_BWD_SCRATCH, 3, vmem=28)


def self_bwd_second(core, win, table, b, bm, bt, n, weights, seg, ctx, st):
    return call(self_bwd_second_kernel, "self_bwd", (core, win, table, b, bm, bt, n) + weights + (seg, ctx, st),
                [PART, PART, HALF32, HALF32, sd((3, 1024), f32)], SELF_BWD_SCRATCH, 3, vmem=28)


def cross_fwd_kernel(core, win, bits, mine_in, theirs_in, mem_mine, mem_theirs, wq, wkv, wo, w0, wy, wz, wd, we, seg,
                     sseg_ref, n_ref, m_ref, w_ref, ctx0, st0, ctx1, st1, om, ot, cols, q, k, v, st):
    cols[...] = jnp.transpose(seg[...])
    join_rows(core[0], mine_in, theirs_in, n_ref)
    join_rows(core[0], mem_mine, mem_theirs, m_ref)
    join_quarters(bits, (w0, wy, wz, wd, we), w_ref)
    own, away = own_weights(1, wq, wkv, wo), away_weights(w_ref)
    for ws, ctx_ref, st_ref in ((own, ctx0, st0), (away, ctx1, st1)):
        project(n_ref, ws, (0, q))
        project(m_ref, ws, (1, k), (2, v))

        def block(i, ctx_ref=ctx_ref):
            rows = blk(i)

            @pl.when(win[0, i] == 0)
            def _():
                ctx_ref[rows, :] = jnp.zeros((BQ, 192), bf16)
                st[rows, :] = jnp.zeros((BQ, 8), f32)

            for n, width in enumerate(CROSS_W):
                @pl.when(win[0, i] == n + 1)
                def _(width=width):
                    keys = pl.ds(pl.multiple_of(win[1, i], 128), width)
                    tseg, sseg = cols[rows, 1:2], sseg_ref[:, keys]
                    attend(cross_scores(q, k, tseg, sseg, rows, keys), v, keys, rows, tseg > 0, ctx_ref, st)
        loop(SLOT // BQ, block)
        st_ref[...] = jnp.transpose(st[...])
    out_split(core[0], om, ot, None, lambda c: dg(half_rows(ctx0, c), own[3][...], NN)
              + dg(half_rows(ctx1, c), away[3][...], NN))


def cross_fwd(core, win, bits, mine, theirs, mem_mine, mem_theirs, weights, parts, seg, sseg):
    return call(cross_fwd_kernel, "cross_fwd",
                (core, win, bits, mine, theirs, mem_mine, mem_theirs) + weights + tuple(parts) + (seg, sseg),
                [sd((SLOT, 768), bf16), sd((MEM, 768), bf16), STACK] + ATT + ATT + [HALF32, HALF32],
                [COLS, WIDE16, MEM16, MEM16, STATS], 3, vmem=12)


def cross_bwd_core(core, win, b_ref, n_ref, m_ref, ws, seg, sseg_ref, ctx_ref, st_ref, before, mem_before, a_ref, put,
                   om, ot, mm, mt, cols, st, q, k, v, g_scr, dq, dk, dv, dk16, dv16):
    cols[...] = jnp.transpose(seg[...])
    st[...] = jnp.transpose(st_ref[...])
    project(n_ref, ws, (0, q))
    project(m_ref, ws, (1, k), (2, v))
    dk[...] = jnp.zeros(dk.shape, f32)
    dv[...] = jnp.zeros(dv.shape, f32)
    g = dg(b_ref[...], ws[3][...], NT).astype(bf16)
    g_scr[...] = jnp.where(cols[:, 1:2] > 0, g, jnp.zeros_like(g))

    def block(i):
        rows = blk(i)

        @pl.when(win[0, i] == 0)
        def _():
            dq[rows, :] = jnp.zeros((BQ, 192), bf16)

        for n, width in enumerate(CROSS_W):
            @pl.when(win[0, i] == n + 1)
            def _(width=width):
                keys = pl.ds(pl.multiple_of(win[1, i], 128), width)
                attend_back(cross_scores(q, k, cols[rows, 1:2], sseg_ref[:, keys], rows, keys),
                            q, k, v, g_scr[rows, :], keys, rows, st, dq, dk, dv, lambda sg: None)
    loop(SLOT // BQ, block)
    dk16[...] = dk[...].astype(bf16)
    dv16[...] = dv[...].astype(bf16)
    weight_grads(dq, dk16, dv16, n_ref, m_ref, b_ref, ctx_ref, a_ref, put)
    out_split(core[0], om, ot, before, lambda c: dg(half_rows(dq, c), ws[0][...], NN))
    out_split(core[0], mm, mt, mem_before, lambda c: dg(half_rows(dk16, c), ws[1][...], NN)
              + dg(half_rows(dv16, c), ws[2][...], NN))


CROSS_BWD_SCRATCH = [COLS, STATS, WIDE16, MEM16, MEM16, WIDE16, WIDE16, MEM32, MEM32, MEM16, MEM16]
HALFMEM = sd((MEM // 2, 768), f32)


def cross_bwd_first_kernel(core, win, mine_in, theirs_in, n_ref, m_ref, w_ref, seg, sseg, ctx, st, b_ref, a_ref, late_ref,
                           om, ot, mm, mt, *scr):
    join_rows(core[0], mine_in, theirs_in, b_ref)
    cross_bwd_core(core, win, b_ref, n_ref, m_ref, away_weights(w_ref), seg, sseg, ctx, st, None, None, a_ref,
                   put_plain(late_ref, 192), om, ot, mm, mt, *scr)


def cross_bwd_second_kernel(core, win, b_ref, bm, bt, cm, ct, n_ref, m_ref, wq, wkv, wo, seg, sseg, ctx, st,
                            a_ref, late_ref, om, ot, mm, mt, *scr):
    cross_bwd_core(core, win, b_ref, n_ref, m_ref, own_weights(1, wq, wkv, wo), seg, sseg, ctx, st, (bm, bt), (cm, ct),
                   a_ref, put_plain(late_ref, 192), om, ot, mm, mt, *scr)


def cross_bwd_first(core, win, mine, theirs, n, mem, w, seg, sseg, ctx, st):
    return call(cross_bwd_first_kernel, "cross_bwd", (core, win, mine, theirs, n, mem, w, seg, sseg, ctx, st),
                [sd((SLOT, 768), bf16), PART, PART, HALF32, HALF32, HALFMEM, HALFMEM], CROSS_BWD_SCRATCH, 2, vmem=18)


def cross_bwd_second(core, win, b, before, n, mem, weights, seg, sseg, ctx, st):
    return call(cross_bwd_second_kernel, "cross_bwd",
                (core, win, b) + tuple(before) + (n, mem) + weights + (seg, sseg, ctx, st),
                [PART, PART, HALF32, HALF32, HALFMEM, HALFMEM], CROSS_BWD_SCRATCH, 2, vmem=18)


GELU_C = math.sqrt(2.0 / math.pi)


def ffn_rows(n_ref, c_ref, wg, wu, wo, o_ref, t_ref, before, h_ref, g_ref, u_ref, base):
    def block(i):
        rows = blk(i)
        keep = pl.ds(pl.multiple_of(base + i * BQ, BQ), BQ)
        n = n_ref[rows, :]
        gate, up = dg(n, wg[...], NN), dg(n, wu[...], NN)
        hid = dg(c_ref[rows, :], wo[...], NT)
        square = gate * gate
        th = jnp.tanh(GELU_C * (gate + 0.044715 * (gate * square)))
        half = 0.5 * (1.0 + th)
        gelu = gate * half
        slope = half + (0.5 * GELU_C) * gate * (1.0 - th * th) * (1.0 + (3 * 0.044715) * square)
        h = (gelu * up).astype(bf16)
        gg = (hid * up * slope).astype(bf16)
        ug = (hid * gelu).astype(bf16)
        h_ref[keep, :], g_ref[keep, :], u_ref[keep, :] = h, gg, ug
        out = dg(h, wo[...], NN)
        third = dg(gg, wg[...], NT) + dg(ug, wu[...], NT)
        if before is not None:
            out, third = out + before[0][rows, :], third + before[1][rows, :]
        o_ref[rows, :], t_ref[rows, :] = out, third
    loop(n_ref.shape[0] // BQ, block)


def ffn_core(bits, na, nb, ca, cb, wg, wu, wo, before_a, before_b, outs, h_ref, g_ref, u_ref, dw):
    oa, ob, ta, tb, x_ref, y_keep, y_give, z_keep, z_give = outs
    half = na.shape[0]
    ffn_rows(na, ca, wg, wu, wo, oa, ta, before_a, h_ref, g_ref, u_ref, 0)
    ffn_rows(nb, cb, wg, wu, wo, ob, tb, before_b, h_ref, g_ref, u_ref, half)
    for j, (left, ra, rb) in enumerate(((g_ref, na, nb), (u_ref, na, nb), (h_ref, ca, cb))):
        dw[512 * j:512 * j + 512, :] = (dg(left[0:half, :], ra[...], TN) + dg(left[half:2 * half, :], rb[...], TN)).astype(
            bf16)
    x_ref[...] = dw[0:384, :]
    for base, bit, keep, give in ((384, bits[0], y_keep, y_give), (960, bits[1], z_keep, z_give)):
        keep[...] = dw[pl.ds(pl.multiple_of(base + bit * 288, 16), 288), :]
        give[...] = dw[pl.ds(pl.multiple_of(base + (1 - bit) * 288, 16), 288), :]


def ffn_away_kernel(bits, na, nb, ca, cb, f0, fy, fz, fd, fe, *refs):
    w2, wo, far = refs[-3:]
    far[0:288, :] = fd[...]
    far[288:576, :] = fe[...]
    for step, part in enumerate((f0, fy, fz, far)):
        y, z = quarter_of(bits, step)
        w2[y, pl.ds(pl.multiple_of(z * 384, 128), 384), :] = part[0:384, :]
        at = pl.multiple_of((2 * y + z) * 128, 128)
        wo[pl.ds(at, 128), 0:512] = part[384:512, :]
        wo[pl.ds(at, 64), 512:768] = part[512:576, 0:256]
        wo[pl.ds(pl.multiple_of(at + 64, 64), 64), 512:768] = part[512:576, 256:512]
    ffn_core(bits, na, nb, ca, cb, w2.at[0], w2.at[1], wo, None, None, refs[:9], *refs[9:13])


def ffn_own_kernel(bits, na, nb, ca, cb, wi, wo, pa, pb, sa, sb, *refs):
    ffn_core(bits, na, nb, ca, cb, wi.at[0], wi.at[1], wo, (pa, sa), (pb, sb), refs[:9], *refs[9:13])


def ffn_outs(rows):
    return [sd((rows, 768), f32)] * 4 + [sd((384, 768), bf16)] + [sd((288, 768), bf16)] * 4


def ffn_scratch(rows, units):
    return [pltpu.VMEM((2 * rows, units), bf16)] * 3 + [pltpu.VMEM((3 * units, 768), bf16)]


def ffn_away(bits, na, nb, ca, cb, weights):
    rows, units = na.shape[0], weights[0].shape[1]
    scratch = ffn_scratch(rows, units) + [pltpu.VMEM((2, 768, units), bf16), pltpu.VMEM((units, 768), bf16),
                                          pltpu.VMEM((576, units), bf16)]
    return call(ffn_away_kernel, "ffn_away", (bits, na, nb, ca, cb) + tuple(weights), ffn_outs(rows), scratch, 1, vmem=22)


def ffn_own(bits, na, nb, ca, cb, wi, wo, before):
    rows, units = na.shape[0], wo.shape[0]
    return call(ffn_own_kernel, "ffn_own", (bits, na, nb, ca, cb, wi, wo) + tuple(before), ffn_outs(rows),
                ffn_scratch(rows, units), 1, vmem=20)


def merge_kernel(actions, outs):
    def kernel(bits, *refs):
        ins, dest = refs[:len(refs) - outs], refs[len(refs) - outs:]

        def total(terms, extra, count):
            value = None
            for src, at in terms:
                part = ins[src][pl.ds(pl.multiple_of(at + extra, 16), count), :].astype(f32)
                value = part if value is None else value + part
            return value.astype(bf16)

        for action in actions:
            if action[0] == "split":
                _, terms, count, bit, (keep, kat), (give, gat) = action
                half = count // 2
                dest[keep][kat:kat + half, :] = total(terms, bits[bit] * half, half)
                dest[give][gat:gat + half, :] = total(terms, (1 - bits[bit]) * half, half)
            elif action[0] == "sum":
                _, terms, count, (out, at) = action
                dest[out][at:at + count, :] = total(terms, 0, count)
            else:
                _, (own, own_at), (other, other_at), count, bit, (out, at) = action
                dest[out][pl.ds(pl.multiple_of(at + bits[bit] * count, 16), count), :] = ins[own][own_at:own_at + count, :]
                dest[out][pl.ds(pl.multiple_of(at + (1 - bits[bit]) * count, 16), count), :] = (
                    ins[other][other_at:other_at + count, :])
    return kernel


def merge(bits, ins, actions, sizes):
    outs = [sd((rows, 768), bf16) for rows in sizes]
    return call(merge_kernel(actions, len(outs)), "merge", (bits,) + tuple(ins), outs, (), 1, vmem=16)


def ffn_finish_kernel(bits, fin, y_in, z_in, gi, go, model, unit, scr):
    for base, half, bit, own, other in ((0, 192, bits[0], fin[0:192, :], y_in[0:192, :]),
                                        (384, 288, bits[0], fin[192:480, :], y_in[192:480, :]),
                                        (960, 288, bits[1], fin[480:768, :], z_in[...])):
        scr[pl.ds(pl.multiple_of(base + bit * half, 16), half), :] = own
        scr[pl.ds(pl.multiple_of(base + (1 - bit) * half, 16), half), :] = other
    for j in range(3):
        g = scr[512 * j:512 * j + 512, :].astype(f32)
        if j < 2:
            gi[j] = jnp.transpose(g)
        else:
            go[...] = g
        sq = g * g
        model[j:j + 1, :] = jnp.sum(sq, axis=0, keepdims=True)
        unit[j:j + 1, :] = jnp.transpose(jnp.sum(sq, axis=1, keepdims=True)) * (1.0 / D)


def ffn_finish(bits, fin, y_in, z_in):
    units = 512
    return call(ffn_finish_kernel, "ffn_finish", (bits, fin, y_in, z_in),
                [sd((2, 768, units), f32), sd((units, 768), f32), sd((3, 768), f32), sd((3, units), f32)],
                [pltpu.VMEM((3 * units, 768), bf16)], 1, vmem=20)


def finish_kernel(bits, s_fin, s_y, s_z, c_fin, c_y, c_z, fm_ref, qg, kvg, og, model, head, proj, scr):
    for a, (fin, y_in, z_in) in enumerate(((s_fin, s_y, s_z), (c_fin, c_y, c_z))):
        for base, bit, own, other in ((0, bits[1], fin[0:192, :], z_in), (384, bits[0], fin[192:384, :], y_in)):
            scr[pl.ds(pl.multiple_of(base + bit * 192, 16), 192), :] = own
            scr[pl.ds(pl.multiple_of(base + (1 - bit) * 192, 16), 192), :] = other[...]
        for j, (out, row) in enumerate(((qg.at[a], a), (kvg.at[a, 0], 2 + 2 * a), (kvg.at[a, 1], 3 + 2 * a),
                                        (og.at[a], 8 + a))):
            w = scr[192 * j:192 * j + 192, :].astype(f32)
            out[...] = w
            sq = w * w
            model[row:row + 1, :] = jnp.sum(sq, axis=0, keepdims=True)
            side = jnp.transpose(jnp.sum(sq, axis=1, keepdims=True)) * (1.0 / D)
            if j < 3:
                head[row:row + 1, :] = side
            else:
                proj[a:a + 1, :] = side
    model[6:8, :] = fm_ref[0:2, :]
    model[10:11, :] = fm_ref[2:3, :]


def finish(bits, self_parts, cross_parts, ffn_model):
    outs = [sd((2, 192, 768), f32), sd((2, 2, 192, 768), f32), sd((2, 192, 768), f32), sd((11, 768), f32),
            sd((6, 192), f32), sd((2, 192), f32)]
    return call(finish_kernel, "finish", (bits,) + tuple(self_parts) + tuple(cross_parts) + (ffn_model,), outs,
                [pltpu.VMEM((768, 768), bf16)], 1, vmem=16)


CORE = [(i, i ^ 1) for i in range(4)]
CHIP = [(i, i ^ 2) for i in range(4)]


def swap_core(v):
    return lax.ppermute(v, "tensor", CORE)


def swap_chip(v):
    return lax.ppermute(v, "tensor", CHIP)


def swap_dp(v, bit):
    return lax.ppermute(v, "dp", [(i, i ^ (1 << bit)) for i in range(lax.axis_size("dp"))])


def dp_bits():
    return int(math.log2(lax.axis_size("dp")))


def after(value, *earlier):
    return lax.optimization_barrier((value,) + earlier)[0]


def sync(*values):
    return lax.optimization_barrier(values)


def over_group(v):
    diagonal = lax.ppermute(v, "tensor", [(i, i ^ 3) for i in range(4)])
    return (v + swap_core(v)) + (swap_chip(v) + diagonal)


def over_first_bits(v):
    diagonal = lax.ppermute(v, "dp", [(i, i ^ 3) for i in range(lax.axis_size("dp"))])
    return (v + swap_dp(v, 0)) + (swap_dp(v, 1) + diagonal)


def past(value, bit):
    for one in range(bit, dp_bits()):
        value = (value.astype(f32) + swap_dp(value, one).astype(f32)).astype(bf16)
    return value


def bucket_sums(lane_sums):
    lane = np.arange(1024)
    distance = 512 - np.where(lane < 768, lane, lane - 1024)
    buckets = jnp.asarray(np.array([bucket_of(max(int(n), 0)) for n in distance], np.int32))
    onehot = (buckets[:, None] == jnp.arange(BUCKETS)[None, :]) & jnp.asarray(distance >= 0)[:, None]
    return lax.dot_general(onehot.astype(f32), lane_sums, (((0,), (1,)), ((), ())), precision=lax.Precision.HIGHEST,
                           preferred_element_type=f32)


def on_device(tokens, memory, cotangent, norm_gains, query_weight, keyvalue_weight, output_weight, bias_table,
              inner_weight, outer_weight, target_lengths, source_lengths):
    t, d = lax.axis_index("tensor"), lax.axis_index("dp")
    core = (t & 1).reshape(1).astype(i32)
    slot = lax.shift_right_logical(t, 1).reshape(1).astype(i32)
    bits = (lax.shift_right_logical(d, jnp.arange(3)) & 1).astype(i32)
    gains = [norm_gains[i:i + 1] for i in range(3)]
    weights = (jnp.swapaxes(query_weight, 1, 2), jnp.swapaxes(keyvalue_weight, 2, 3), output_weight)

    q_self, q_cross = weight_quarters(bits, *weights)
    s0 = swap_chip(q_self)
    tokens = sync(tokens, q_self)[0]
    n1m = norm_rows(tokens, gains[0])
    n1t = swap_core(n1m)
    table_away = swap_chip(bias_table)
    seg, sseg, swin, cwin = slot_layout(slot, target_lengths, source_lengths)
    n1, ctx_s0, st_s0, pm, pt = self_fwd_first(core, swin, bias_table, n1m, n1t, weights, seg)
    s0, n1, q_cross, memory, cotangent, table_away = sync(s0, n1, q_cross, memory, cotangent, table_away)
    sy, sz = swap_dp(s0, 0), swap_dp(s0, 1)
    c0 = swap_chip(q_cross)
    mem_t, cot_t = swap_core(memory), swap_core(cotangent)
    f_q = packed(bits, inner_weight, outer_weight)
    sy, sz, c0, f_q, n1 = sync(sy, sz, c0, f_q, n1)
    s3, s4 = swap_dp(sz[:96], 0), swap_dp(sy[96:], 1)
    s3, s4, c0, f_q, n1 = sync(s3, s4, c0, f_q, n1)
    cy, cz = swap_dp(c0, 0), swap_dp(c0, 1)
    f0 = swap_chip(f_q)
    w_self_away, ctx_s1, st_s1, pm, pt = self_fwd_second(core, swin, table_away, bits, n1, pm, pt, (s0, sy, sz, s3, s4), seg)
    f0, cy, cz, pm, pt = sync(f0, cy, cz, pm, pt)
    c3, c4 = swap_dp(cz[:96], 0), swap_dp(cy[96:], 1)
    fy, fz = swap_dp(f0, 0), swap_dp(f0, 1)
    after_self, n2m = add_norm(tokens, pm, swap_core(pt), gains[1])
    c3, c4, n2m = sync(c3, c4, n2m)

    n2, mem, w_cross_away, ctx_c0, st_c0, ctx_c1, st_c1, pm, pt = cross_fwd(
        core, cwin, bits, n2m, swap_core(n2m), memory, mem_t, weights, (c0, cy, cz, c3, c4), seg, sseg)
    fy, fz, pm, pt = sync(fy, fz, pm, pt)
    f3, f4 = swap_dp(fz[:288], 0), swap_dp(fy[288:], 1)
    after_cross, n3m = add_norm(after_self, pm, swap_core(pt), gains[2])

    n3t = swap_core(n3m)
    oa, ob, ta, tb, px, pyk, pyg, pzk, pzg = ffn_away(bits, n3m, n3t, cotangent, cot_t, (f0, fy, fz, f3, f4))
    n3m, px, pyg, pzg = sync(n3m, px, pyg, pzg)
    xi, yi, zi = swap_chip(px), swap_dp(pyg, 0), swap_dp(pzg, 1)
    oa, ob, ta, tb, ox, oyk, oyg, ozk, ozg = ffn_own(bits, n3m, n3t, cotangent, cot_t, inner_weight, outer_weight,
                                                     (oa, ob, ta, tb))
    xi, yi, zi, oa, ob, ta, tb, ox, oyg, ozg = sync(xi, yi, zi, oa, ob, ta, tb, ox, oyg, ozg)
    fx_k, xp, yp = merge(
        bits, (ox, xi, pyk, yi, pzk, zi, oyg),
        (("split", ((0, 0), (1, 0)), 384, 0, (0, 0), (2, 0)),
         ("sum", ((2, 0), (3, 0)), 288, (1, 0)),
         ("sum", ((4, 0), (5, 0)), 288, (1, 288)),
         ("sum", ((6, 0),), 288, (2, 192))), (192, 576, 480))
    xi, yi, zi = swap_chip(xp), swap_dp(yp, 0), swap_dp(ozg, 1)
    cross_out_m, branch_m, gain2 = norm_back(after_cross, gains[2], cotangent, ta, swap_core(tb))

    branch, c_out, c_late, pm, pt, mm, mt = cross_bwd_first(core, cwin, branch_m, swap_core(branch_m), n2, mem,
                                                            w_cross_away, seg, sseg, ctx_c1, st_c1)
    xi, yi, zi, branch, c_out, c_late, pm, pt, mm, mt = sync(xi, yi, zi, branch, c_out, c_late, pm, pt, mm, mt)
    fx_k, fy_k, fz_k, cb_k, yp, zp = merge(
        bits, (fx_k, yi, oyk, xi, ozk, zi, c_late),
        (("split", ((0, 0), (1, 0)), 192, 1, (0, 0), (5, 0)),
         ("split", ((2, 0), (1, 192), (3, 0)), 288, 1, (1, 0), (5, 96)),
         ("split", ((4, 0), (5, 0), (3, 288)), 288, 0, (2, 0), (4, 0)),
         ("split", ((6, 0),), 384, 0, (3, 0), (4, 144))), (96, 144, 144, 192, 336, 240))
    xi, yi, zi = swap_chip(c_out), swap_dp(yp, 0), swap_dp(zp, 1)
    branch, zp = sync(branch, zp)
    c_a, c_own, pm, pt, mm, mt = cross_bwd_second(core, cwin, branch, (pm, pt, mm, mt), n2, mem, weights, seg, sseg,
                                                  ctx_c0, st_c0)
    xi, yi, zi, c_a, c_own, pm, pt, mm, mt = sync(xi, yi, zi, c_a, c_own, pm, pt, mm, mt)
    f_mid, ca_k, cb_o, xp, yp, zp = merge(
        bits, (fx_k, zi, fy_k, fz_k, yi, c_a, xi, cb_k, c_own),
        (("sum", ((0, 0), (1, 0)), 96, (0, 0)),
         ("sum", ((2, 0), (1, 96)), 144, (0, 96)),
         ("sum", ((3, 0), (4, 0)), 144, (0, 240)),
         ("split", ((5, 0), (6, 0)), 384, 1, (1, 0), (5, 0)),
         ("sum", ((7, 0), (4, 144)), 192, (3, 0)),
         ("split", ((8, 0),), 384, 0, (2, 0), (4, 0))), (384, 192, 192, 192, 192, 192))
    pt, f_mid, xp, yp, zp = sync(pt, f_mid, xp, yp, zp)
    xi, yi, zi, z2i = swap_chip(xp), swap_dp(yp, 0), swap_dp(zp, 1), swap_dp(f_mid, 2)
    self_out_m, branch_m, gain1 = norm_back(after_self, gains[1], cross_out_m, pm, swap_core(pt))

    branch, s_out, s_late, pm, pt, lanes_away = self_bwd_first(core, swin, table_away, branch_m, swap_core(branch_m), n1,
                                                               w_self_away, seg, ctx_s1, st_s1)
    z2i, xi, yi, zi, branch, s_out, s_late, pm, pt = sync(z2i, xi, yi, zi, branch, s_out, s_late, pm, pt)
    f_own, ca_k, cb_k, sb_k, yp, zp = merge(
        bits, (f_mid, z2i, ca_k, zi, cb_o, yi, xi, s_late),
        (("sum", ((0, 0), (1, 0)), 384, (0, 0)),
         ("sum", ((0, 0), (1, 0)), 240, (5, 0)),
         ("sum", ((0, 240), (1, 240)), 144, (4, 0)),
         ("split", ((2, 0), (3, 0)), 192, 0, (1, 0), (4, 144)),
         ("split", ((4, 0), (5, 0), (6, 0)), 192, 1, (2, 0), (5, 240)),
         ("split", ((7, 0),), 384, 0, (3, 0), (4, 240))), (384, 96, 96, 192, 432, 336))
    if dp_bits() > 3:
        f_own = past(f_own, 3)
        yp, zp = jnp.concatenate((f_own[240:], yp[144:])), jnp.concatenate((f_own[:240], zp[240:]))
    xi, yi, zi = swap_chip(s_out), swap_dp(yp, 0), swap_dp(zp, 1)
    branch, zp = sync(branch, zp)
    s_a, s_own, pm, pt, lanes_own = self_bwd_second(core, swin, bias_table, branch, pm, pt, n1, weights, seg, ctx_s0, st_s0)
    xi, yi, zi, s_a, s_own, pm, pt, lanes_own = sync(xi, yi, zi, s_a, s_own, pm, pt, lanes_own)

    f_fin, c_mid, sa_k, sb_o, xp, yp, zp = merge(
        bits, (f_own, zi, yi, ca_k, cb_k, s_a, xi, sb_k, s_own),
        (("join", (0, 0), (1, 0), 96, 1, (0, 0)),
         ("join", (0, 96), (1, 96), 144, 1, (0, 192)),
         ("join", (0, 240), (2, 0), 144, 0, (0, 480)),
         ("join", (0, 0), (1, 0), 96, 1, (5, 0)),
         ("join", (0, 96), (1, 96), 144, 1, (5, 192)),
         ("join", (0, 240), (2, 0), 144, 0, (6, 0)),
         ("sum", ((3, 0), (2, 144)), 96, (1, 0)),
         ("sum", ((4, 0), (1, 240)), 96, (1, 96)),
         ("split", ((5, 0), (6, 0)), 384, 1, (2, 0), (6, 288)),
         ("sum", ((7, 0), (2, 240)), 192, (4, 0)),
         ("split", ((8, 0),), 384, 0, (3, 0), (5, 480))), (768, 192, 192, 192, 192, 672, 480))
    pt_in, mt_in, ob_in = swap_core(pt), swap_core(mt), swap_core(ob)
    xi, yi, zi, z2i = swap_chip(xp), swap_dp(yp, 0), swap_dp(zp, 1), swap_dp(c_mid, 2)
    z2i, xi, yi, zi, pt_in, mt_in, ob_in, lanes_away = sync(z2i, xi, yi, zi, pt_in, mt_in, ob_in, lanes_away)
    c_own, sa_k, sb_k, yp, zp = merge(
        bits, (c_mid, z2i, sa_k, zi, sb_o, yi, xi),
        (("sum", ((0, 0), (1, 0)), 192, (0, 0)),
         ("sum", ((0, 0), (1, 0)), 96, (3, 0)),
         ("sum", ((0, 96), (1, 96)), 96, (4, 0)),
         ("split", ((2, 0), (3, 288)), 192, 0, (1, 0), (3, 96)),
         ("split", ((4, 0), (5, 480), (6, 0)), 192, 1, (2, 0), (4, 96))), (192, 96, 96, 192, 192))
    f_y, f_z = yi[:480], zi[:288]
    if dp_bits() > 3:
        c_own = past(c_own, 3)
        yp, zp = jnp.concatenate((c_own[:96], yp[96:])), jnp.concatenate((c_own[96:], zp[96:]))
    yi, zi = swap_dp(yp, 0), swap_dp(zp, 1)
    tokens_grad, _, gain0 = norm_back(tokens, gains[0], self_out_m, pm, pt_in)
    small = jnp.concatenate((gain0, gain1, gain2))
    memory_grad = mm + mt_in
    output_rows = (after_cross + (oa + ob_in)).astype(bf16)
    yi, zi, small, memory_grad, output_rows, lanes_away = sync(yi, zi, small, memory_grad, output_rows, lanes_away)
    c_fin, s_mid, yp, zp = merge(
        bits, (c_own, yi, zi, sa_k, sb_k),
        (("join", (0, 0), (1, 0), 96, 0, (0, 0)),
         ("join", (0, 96), (2, 0), 96, 1, (0, 192)),
         ("join", (0, 0), (1, 0), 96, 0, (3, 0)),
         ("join", (0, 96), (2, 0), 96, 1, (2, 0)),
         ("sum", ((3, 0), (1, 96)), 96, (1, 0)),
         ("sum", ((4, 0), (2, 96)), 96, (1, 96))), (384, 192, 192, 192))
    z2i, c_y, c_z = swap_dp(s_mid, 2), swap_dp(yp, 0), swap_dp(zp, 1)
    f_fin = sync(f_fin, yp, zp, s_mid)[0]
    inner_sum, outer_sum, ffn_model, unit_stats = ffn_finish(bits, f_fin, f_y, f_z)
    z2i, c_y, c_z, ffn_model = sync(z2i, c_y, c_z, ffn_model)
    (s_own,) = merge(bits, (s_mid, z2i), (("sum", ((0, 0), (1, 0)), 192, (0, 0)),), (192,))
    s_own = past(s_own, 3)
    yi, zi = swap_dp(s_own[:96], 0), swap_dp(s_own[96:], 1)
    small, lanes_away = sync(small, lanes_away, s_own)[:2]
    lanes_in = swap_chip(lanes_away)
    small = over_group(small)
    yi, zi, small, lanes_in = sync(yi, zi, small, lanes_in)
    small = jnp.concatenate((jnp.pad(small, ((0, 0), (0, 256))), lanes_own + lanes_in))
    s_fin, yp, zp = merge(
        bits, (s_own, yi, zi),
        (("join", (0, 0), (1, 0), 96, 0, (0, 0)),
         ("join", (0, 96), (2, 0), 96, 1, (0, 192)),
         ("join", (0, 0), (1, 0), 96, 0, (2, 0)),
         ("join", (0, 96), (2, 0), 96, 1, (1, 0))), (384, 192, 192))
    s_y, s_z, small = swap_dp(yp, 0), swap_dp(zp, 1), over_first_bits(small)
    s_y, s_z, small = sync(s_y, s_z, small)
    for bit in range(2, dp_bits()):
        small = small + swap_dp(small, bit)
    gains_total = small[:3, :D]
    table_sum = bucket_sums(small[3:])
    query_t, keyvalue_t, output_grad, model_part, head_stats, projection_stats = finish(
        bits, (s_fin, s_y, s_z), (c_fin, c_y, c_z), ffn_model)
    query_grad, keyvalue_grad = jnp.swapaxes(query_t, 1, 2), jnp.swapaxes(keyvalue_t, 2, 3)
    model_total = over_group(model_part)
    hidden_units = outer_weight.shape[0] * lax.axis_size("tensor")
    divisors = jnp.array([D] * 6 + [hidden_units] * 2 + [D] * 2 + [hidden_units], f32)
    model_stats = model_total / divisors[:, None]
    return (output_rows, tokens_grad, memory_grad, gains_total, query_grad, keyvalue_grad, output_grad, table_sum,
            inner_sum, outer_sum, model_stats, head_stats, projection_stats, unit_stats)


def solution(mesh):
    rows = P(("dp", "tensor"), None)
    in_specs = (rows, rows, rows, P(), P(None, None, "tensor"), P(None, None, None, "tensor"), P(None, "tensor", None),
                P(None, "tensor"), P(None, None, "tensor"), P("tensor", None), P("dp", None), P("dp", None))
    out_specs = (rows, rows, rows, P(), P(None, None, "tensor"), P(None, None, None, "tensor"),
                 P(None, "tensor", None), P(None, "tensor"), P(None, None, "tensor"), P("tensor", None), P(),
                 P(None, "tensor"), P(None, "tensor"), P(None, "tensor"))
    return jax.shard_map(on_device, mesh=mesh, in_specs=in_specs, out_specs=out_specs, check_vma=False)
```

```python
import math

import jax
import jax.numpy as jnp
import numpy as np
from jax import lax
from jax.experimental import pallas as pl
from jax.experimental.pallas import tpu as pltpu
from jax.sharding import PartitionSpec as P

D = 768
DH = 64
BUCKETS = 32
MAXDIST = 128
SLOT = 1024
MEM = 512
NORM_EPS = 1e-06
NEG_FILL = -1e30
DEAD = 1 << 20
BQ = 256
COST = 0.02
VM = pl.BlockSpec(memory_space=pltpu.VMEM)
SM = pl.BlockSpec(memory_space=pltpu.SMEM)
NT = (((1,), (1,)), ((), ()))
NN = (((1,), (0,)), ((), ()))
TN = (((0,), (0,)), ((), ()))
f32, bf16, i32 = jnp.float32, jnp.bfloat16, jnp.int32
SELF_W = (256, 384, 512, 768)
CROSS_W = (128, 256, 512)
sd = jax.ShapeDtypeStruct


def dg(a, b, dims):
    return lax.dot_general(a, b, dims, preferred_element_type=f32)


def blk(i):
    return pl.ds(pl.multiple_of(i * BQ, BQ), BQ)


def loop(count, body):
    def step(i, carry):
        body(i)
        return carry
    lax.fori_loop(0, count, step, 0)


def call(kernel, name, args, outs, scratch=(), scalars=0, vmem=12, flops=1e9, out_specs=None):
    byts = sum(int(np.prod(a.shape)) * a.dtype.itemsize for a in tuple(args) + tuple(outs))
    return pl.pallas_call(
        kernel,
        in_specs=[SM] * scalars + [VM] * (len(args) - scalars),
        out_specs=list(out_specs) if out_specs else [VM] * len(outs),
        out_shape=list(outs),
        scratch_shapes=list(scratch),
        name=name,
        compiler_params=pltpu.CompilerParams(vmem_limit_bytes=vmem << 20),
        cost_estimate=pl.CostEstimate(flops=int(flops * COST), bytes_accessed=int(byts * COST), transcendentals=0),
    )(*args)


def bucket_of(spread):
    exact_count = BUCKETS // 2
    if spread < exact_count:
        return spread
    larger = exact_count + math.floor(
        math.log(spread / exact_count) / math.log(MAXDIST / exact_count) * (BUCKETS - exact_count)
    )
    return min(larger, BUCKETS - 1)


def bucket_starts():
    buckets = [bucket_of(n) for n in range(SLOT)]
    return [next(n for n in range(SLOT + 1) if n == SLOT or buckets[n] >= b) for b in range(BUCKETS)]


def layout_kernel(slot, tl_ref, sl_ref, seg_ref, sseg_ref, swin, cwin):
    s = slot[0]
    docs = tl_ref.shape[1]
    tl = [tl_ref[s, j] for j in range(docs)]
    sl = [sl_ref[s, j] for j in range(docs)]
    ends, sends = [], []
    te, se = jnp.int32(0), jnp.int32(0)
    for j in range(docs):
        te, se = te + tl[j], se + sl[j]
        ends.append(te)
        sends.append(se)
    pos = lax.broadcasted_iota(i32, (1, SLOT), 1)
    spos = lax.broadcasted_iota(i32, sseg_ref.shape, 1)
    start, seg, mseg = jnp.zeros_like(pos), jnp.ones_like(pos), jnp.ones_like(spos)
    for j in range(docs):
        past = pos >= ends[j]
        start = jnp.where(past, ends[j], start)
        seg = seg + past.astype(i32)
        mseg = mseg + (spos >= sends[j]).astype(i32)
    live = pos < te
    seg_ref[...] = jnp.zeros(seg_ref.shape, i32)
    seg_ref[0:1, :] = jnp.where(live, start, DEAD)
    seg_ref[1:2, :] = jnp.where(live, seg, -1)
    sseg_ref[...] = jnp.where(spos < se, mseg, 0)
    for i in range(SLOT // BQ):
        q0 = i * BQ
        first, low, high = jnp.int32(0), jnp.int32(0), jnp.int32(0)
        last = jnp.minimum(q0 + BQ - 1, te - 1)
        for j in range(docs):
            before = ends[j] <= q0
            first = jnp.where(before, ends[j], first)
            low = low + jnp.where(before, sl[j], 0)
            high = high + jnp.where(ends[j] - tl[j] <= last, sl[j], 0)
        need = q0 + BQ - lax.shift_left(lax.shift_right_logical(first, 7), 7)
        width = jnp.int32(1)
        for w in SELF_W[:-1]:
            width = width + jnp.where(need > w, 1, 0)
        swin[i] = jnp.where(q0 < te, width, 0)
        at1 = lax.shift_left(lax.shift_right_logical(low, 7), 7)
        at2 = jnp.minimum(at1, MEM - 256)
        one, two = high - at1 <= 128, high - at2 <= 256
        cwin[0, i] = jnp.where(q0 < te, jnp.where(one, 1, jnp.where(two, 2, 3)), 0)
        cwin[1, i] = jnp.where(one, at1, jnp.where(two, at2, 0))


def slot_layout(slot, tl, sl):
    return call(layout_kernel, "layout", (slot, tl, sl),
                (sd((8, SLOT), i32), sd((1, MEM), i32), sd((4,), i32), sd((2, 4), i32)),
                scalars=3, flops=1e6, out_specs=(VM, VM, SM, SM))


def quarter_of(bits, step):
    y, z = bits[0], bits[1]
    return (1 - y if step & 1 else y), (1 - z if step & 2 else z)


def quarters_kernel(bits, q_ref, kv_ref, o_ref, out):
    mine = bits[0] + 2 * bits[1]
    for n, ref in enumerate((q_ref.at[0], kv_ref.at[0, 0], kv_ref.at[0, 1], o_ref.at[0])):
        @pl.when(mine == n)
        def _(ref=ref):
            out[0:192, :] = ref[...]

        @pl.when(mine == 3 - n)
        def _(ref=ref):
            out[192:384, :] = ref[...]


def weight_quarters(bits, layer, q, kv, o):
    one = pl.BlockSpec((1, 192, 768), lambda i, bits: (layer, 0, 0))
    if layer == 0:
        q, kv, o = (pltpu.with_memory_space_constraint(a, pltpu.HBM) for a in (q, kv, o))
    return pl.pallas_call(
        quarters_kernel,
        grid_spec=pltpu.PrefetchScalarGridSpec(
            num_scalar_prefetch=1, grid=(1,),
            in_specs=[one, pl.BlockSpec((1, 2, 192, 768), lambda i, bits: (layer, 0, 0, 0)), one],
            out_specs=pl.BlockSpec((384, 768), lambda i, bits: (0, 0))),
        out_shape=sd((384, 768), bf16),
        name="quarters",
        compiler_params=pltpu.CompilerParams(vmem_limit_bytes=8 << 20),
        cost_estimate=pl.CostEstimate(flops=0, bytes_accessed=1200000, transcendentals=0))(bits, q, kv, o)


def join_quarters(bits, pair, side_y, side_z, w_ref):
    for step, part in enumerate((pair[0:192, :], side_y[...], side_z[...], pair[192:384, :])):
        y, z = quarter_of(bits, step)
        w_ref[pl.ds(pl.multiple_of((y + 2 * z) * 192, 16), 192), :] = part


def pack_kernel(bits, wi_ref, wo_ref, f0_ref, f3_ref):
    for f_ref, step in ((f0_ref, 0), (f3_ref, 3)):
        y, z = quarter_of(bits, step)
        f_ref[0:384, :] = wi_ref[y, pl.ds(pl.multiple_of(z * 384, 128), 384), :]
        outer = wo_ref[pl.ds(pl.multiple_of((2 * y + z) * 128, 128), 128), :]
        f_ref[384:512, :] = outer[:, 0:512]
        f_ref[512:576, 0:256] = outer[0:64, 512:768]
        f_ref[512:576, 256:512] = outer[64:128, 512:768]


def packed(bits, wi, wo):
    return call(pack_kernel, "pack", (bits, wi, wo), (sd((576, 512), bf16),) * 2, (), 1)


def own_weights(which, q_ref, kv_ref, o_ref):
    return (q_ref.at[which], kv_ref.at[which, 0], kv_ref.at[which, 1], o_ref.at[which])


def away_weights(w_ref):
    return tuple(w_ref.at[192 * j:192 * j + 192] for j in range(4))


def norm_kernel(x_ref, gain_ref, n_ref):
    x = x_ref[...].astype(f32)
    r = lax.rsqrt(jnp.mean(x * x, axis=-1, keepdims=True) + NORM_EPS)
    n_ref[...] = (x * r * gain_ref[...]).astype(bf16)


def norm_rows(x, gain):
    return call(norm_kernel, "norm", (x, gain), (sd(x.shape, bf16),), flops=1e6)[0]


def add_norm_kernel(x_ref, a_ref, b_ref, gain_ref, y_ref, n_ref):
    y = x_ref[...].astype(f32) + (a_ref[...] + b_ref[...])
    y_ref[...] = y
    r = lax.rsqrt(jnp.mean(y * y, axis=-1, keepdims=True) + NORM_EPS)
    n_ref[...] = (y * r * gain_ref[...]).astype(bf16)


def add_norm(x, a, b, gain):
    return call(add_norm_kernel, "add_norm", (x, a, b, gain), (sd(x.shape, f32), sd(x.shape, bf16)), flops=1e6)


def norm_back_kernel(terms):
    def kernel(v_ref, gain_ref, up_ref, *refs):
        total_ref, branch_ref, sum_ref = refs[terms:]
        grad = refs[0][...].astype(f32)
        for ref in refs[1:terms]:
            grad = grad + ref[...].astype(f32)
        v = v_ref[...].astype(f32)
        r = lax.rsqrt(jnp.mean(v * v, axis=-1, keepdims=True) + NORM_EPS)
        scaled = grad * gain_ref[...]
        back = r * scaled - v * ((r * r * r) * jnp.mean(scaled * v, axis=-1, keepdims=True))
        total = up_ref[...].astype(f32) + back
        total_ref[...] = total
        branch_ref[...] = total.astype(bf16)
        sum_ref[...] = jnp.sum(grad * v * r, axis=0, keepdims=True)
    return kernel


def norm_back(v, gain, up, *grads):
    return call(norm_back_kernel(len(grads)), "norm_back", (v, gain, up) + grads,
                (sd(v.shape, f32), sd(v.shape, bf16), sd((1, v.shape[1]), f32)), flops=1e6)


LANES = (slice(0, 128), slice(0, 128), slice(128, 192))


def head_of(rows128, h):
    if h == 2:
        return rows128
    lane = lax.broadcasted_iota(i32, rows128.shape, 1)
    return jnp.where((lane < 64) == (h == 0), rows128, jnp.zeros_like(rows128))


def pair_of(first, second):
    lane = lax.broadcasted_iota(i32, first.shape, 1)
    return jnp.where(lane < 64, first, second)


def half_rows(ref, which):
    half = ref.shape[0] // 2
    return ref[pl.ds(pl.multiple_of(which * half, half), half), :]


def join_rows(core, mine_ref, theirs_ref, all_ref):
    half = mine_ref.shape[0]
    at = pl.multiple_of(core * half, half)
    all_ref[pl.ds(at, half), :] = mine_ref[...]
    all_ref[pl.ds(pl.multiple_of(half - at, half), half), :] = theirs_ref[...]


def out_split(core, mine_ref, theirs_ref, before, value_of):
    for pos, ref in enumerate((mine_ref, theirs_ref)):
        value = value_of(core if pos == 0 else 1 - core)
        ref[...] = value if before is None else value + before[pos][...]


def fill_bias(table, bias_scr):
    lane = lax.broadcasted_iota(i32, (1, 1024), 1)
    distance = 512 - jnp.where(lane < 768, lane, lane - 1024)
    for h in range(3):
        row = jnp.full((1, 1024), table[0, h], f32)
        for b, first in enumerate(bucket_starts()):
            if b > 0:
                row = jnp.where(distance >= first, table[b, h], row)
        row = jnp.where(distance < 0, NEG_FILL, row)
        wide = jnp.broadcast_to(row, (BQ, 1024))
        bias_scr[h] = pltpu.roll(wide, 0, 1, stride=1, stride_axis=0)[:, :768]


def attend(scores, v_ref, keys, rows, live, ctx_ref, st_ref):
    s = [scores(h) for h in range(3)]
    m = [jnp.max(x, axis=1, keepdims=True) for x in s]
    e = [jnp.exp(x - y) for x, y in zip(s, m)]
    total = [jnp.sum(x, axis=1, keepdims=True) for x in e]
    p = [(x * (1.0 / y)).astype(bf16) for x, y in zip(e, total)]
    c = [dg(p[h], v_ref[keys, LANES[h]], NN) for h in range(3)]
    ctx_ref[rows, 0:128] = jnp.where(live, pair_of(c[0], c[1]), 0.0).astype(bf16)
    ctx_ref[rows, 128:192] = jnp.where(live, c[2], 0.0).astype(bf16)
    for h in range(3):
        st_ref[rows, h:h + 1] = m[h] + jnp.log(total[h])


def attend_back(scores, q_ref, k_ref, v_ref, g, keys, rows, st_ref, dq, dk, dv, extra):
    gs = [head_of(g[:, LANES[h]], h) for h in range(3)]
    s = [scores(h) for h in range(3)]
    wg = [dg(gs[h], v_ref[keys, LANES[h]], NT) for h in range(3)]
    p = [jnp.exp(s[h] - st_ref[rows, h:h + 1]) for h in range(3)]
    inner = [jnp.sum(p[h] * wg[h], axis=1, keepdims=True) for h in range(3)]
    sg = [(p[h] * (wg[h] - inner[h])).astype(bf16) for h in range(3)]
    p16 = [x.astype(bf16) for x in p]
    dvs = [dg(p16[h], gs[h], TN) for h in range(3)]
    dks = [dg(sg[h], head_of(q_ref[rows, LANES[h]], h), TN) for h in range(3)]
    dqs = [dg(sg[h], k_ref[keys, LANES[h]], NN) for h in range(3)]
    dv[keys, 0:128] += dvs[0] + dvs[1]
    dv[keys, 128:192] += dvs[2]
    dk[keys, 0:128] += dks[0] + dks[1]
    dk[keys, 128:192] += dks[2]
    dq[rows, 0:128] = pair_of(dqs[0], dqs[1]).astype(bf16)
    dq[rows, 128:192] = dqs[2].astype(bf16)
    extra(sg)


def self_scores(q_ref, k_ref, bias_scr, ds, q0, rows, keys, width):
    kpos = lax.broadcasted_iota(i32, (BQ, width), 1) + (q0 + BQ - width)
    shut = jnp.where(kpos >= ds, 0.0, NEG_FILL)
    return lambda h: dg(head_of(q_ref[rows, LANES[h]], h), k_ref[keys, LANES[h]], NT) + (
        bias_scr[h, :, 768 - width:] + shut)


def cross_scores(q_ref, k_ref, tseg, sseg, rows, keys):
    shut = jnp.where(tseg == sseg, 0.0, NEG_FILL)
    return lambda h: dg(head_of(q_ref[rows, LANES[h]], h), k_ref[keys, LANES[h]], NT) + shut


def project(n_ref, ws, *outs):
    for j, out in outs:
        out[...] = dg(n_ref[...], ws[j][...], NT).astype(bf16)


def self_attend(core, win, table, n_ref, ws, cols, before, ctx_ref, st_ref, om, ot, bias_scr, q, k, v, st):
    fill_bias(table, bias_scr)
    project(n_ref, ws, (0, q), (1, k), (2, v))

    def block(i):
        q0 = pl.multiple_of(i * BQ, BQ)
        rows = pl.ds(q0, BQ)

        @pl.when(win[i] == 0)
        def _():
            ctx_ref[rows, :] = jnp.zeros((BQ, 192), bf16)
            st[rows, :] = jnp.zeros((BQ, 8), f32)

        for n, width in enumerate(SELF_W):
            @pl.when(win[i] == n + 1)
            def _(width=width):
                keys = pl.ds(pl.multiple_of(q0 + (BQ - width), 128), width)
                ds = cols[rows, 0:1]
                attend(self_scores(q, k, bias_scr, ds, q0, rows, keys, width), v, keys, rows, ds < DEAD, ctx_ref, st)
    loop(SLOT // BQ, block)
    st_ref[...] = jnp.transpose(st[...])
    out_split(core[0], om, ot, before, lambda c: dg(half_rows(ctx_ref, c), ws[3][...], NN))


def self_fwd_first_kernel(core, win, table, mine_in, theirs_in, wq, wkv, wo, seg, n_ref, ctx, st, om, ot, cols, *scr):
    cols[...] = jnp.transpose(seg[...])
    join_rows(core[0], mine_in, theirs_in, n_ref)
    self_attend(core, win, table, n_ref, own_weights(0, wq, wkv, wo), cols, None, ctx, st, om, ot, *scr)


def self_fwd_second_kernel(core, win, table, bits, n_ref, bm, bt, pair, wy, wz, seg, w_ref, ctx, st, om, ot, cols,
                           *scr):
    cols[...] = jnp.transpose(seg[...])
    join_quarters(bits, pair, wy, wz, w_ref)
    self_attend(core, win, table, n_ref, away_weights(w_ref), cols, (bm, bt), ctx, st, om, ot, *scr)


HALF32 = sd((SLOT // 2, 768), f32)
ATT = [sd((SLOT, 192), bf16), sd((8, SLOT), f32)]
STACK = sd((768, 768), bf16)
WIDE16, WIDE32 = pltpu.VMEM((SLOT, 192), bf16), pltpu.VMEM((SLOT, 192), f32)
MEM16, MEM32 = pltpu.VMEM((MEM, 192), bf16), pltpu.VMEM((MEM, 192), f32)
BIAS = pltpu.VMEM((3, BQ, 768), f32)
COLS, STATS = pltpu.VMEM((SLOT, 8), i32), pltpu.VMEM((SLOT, 8), f32)


def self_fwd_first(core, win, table, mine, theirs, weights, seg):
    return call(self_fwd_first_kernel, "self_fwd", (core, win, table, mine, theirs) + weights + (seg,),
                [sd((SLOT, 768), bf16)] + ATT + [HALF32, HALF32], [COLS, BIAS, WIDE16, WIDE16, WIDE16, STATS], 3, vmem=14)


def self_fwd_second(core, win, table, bits, n, bm, bt, parts, seg):
    return call(self_fwd_second_kernel, "self_fwd", (core, win, table, bits, n, bm, bt) + tuple(parts) + (seg,),
                [STACK] + ATT + [HALF32, HALF32], [COLS, BIAS, WIDE16, WIDE16, WIDE16, STATS], 4, vmem=14)


def diagonal_sums(scr, h):
    span = scr.shape[2]
    slabs = [scr[h, 8 * a:8 * a + 8, :] for a in range(BQ // 8)]
    step = 8
    while len(slabs) > 1:
        slabs = [slabs[j] + pltpu.roll(slabs[j + 1], span - step, 1) for j in range(0, len(slabs), 2)]
        step *= 2
    acc = slabs[0]
    row = lax.broadcasted_iota(i32, acc.shape, 0)
    for bit in (1, 2, 4):
        acc = jnp.where((row & bit) > 0, pltpu.roll(acc, span - bit, 1), acc)
    return jnp.sum(acc, axis=0, keepdims=True)


def weight_grads(dq, dk16, dv16, nq_ref, nk_ref, b_ref, ctx_ref, a_ref, put_late):
    a_ref[0:192, :] = dg(dq[...], nq_ref[...], TN).astype(bf16)
    a_ref[192:384, :] = dg(dk16[...], nk_ref[...], TN).astype(bf16)
    put_late(0, dg(dv16[...], nk_ref[...], TN).astype(bf16))
    put_late(1, dg(ctx_ref[...], b_ref[...], TN).astype(bf16))


def put_plain(ref, rows):
    def put(half, value):
        ref[rows * half:rows * half + rows, :] = value
    return put


def self_bwd_core(core, win, table, b_ref, n_ref, ws, seg, ctx_ref, st_ref, before, a_ref, put, om, ot, db_ref,
                  cols, st, bias_scr, dbias_scr, q, k, v, g_scr, dq, dk, dv, dk16, dv16):
    cols[...] = jnp.transpose(seg[...])
    st[...] = jnp.transpose(st_ref[...])
    fill_bias(table, bias_scr)
    project(n_ref, ws, (0, q), (1, k), (2, v))
    dbias_scr[...] = jnp.zeros(dbias_scr.shape, f32)
    dk[...] = jnp.zeros(dk.shape, f32)
    dv[...] = jnp.zeros(dv.shape, f32)
    g = dg(b_ref[...], ws[3][...], NT).astype(bf16)
    g_scr[...] = jnp.where(cols[:, 0:1] < DEAD, g, jnp.zeros_like(g))

    def block(i):
        q0 = pl.multiple_of(i * BQ, BQ)
        rows = pl.ds(q0, BQ)

        @pl.when(win[i] == 0)
        def _():
            dq[rows, :] = jnp.zeros((BQ, 192), bf16)

        for n, width in enumerate(SELF_W):
            @pl.when(win[i] == n + 1)
            def _(width=width):
                keys = pl.ds(pl.multiple_of(q0 + (BQ - width), 128), width)

                def extra(sg):
                    for h in range(3):
                        dbias_scr[h, :, 768 - width:768] += sg[h].astype(f32)
                attend_back(self_scores(q, k, bias_scr, cols[rows, 0:1], q0, rows, keys, width),
                            q, k, v, g_scr[rows, :], keys, rows, st, dq, dk, dv, extra)
    loop(SLOT // BQ, block)
    dk16[...] = dk[...].astype(bf16)
    dv16[...] = dv[...].astype(bf16)
    weight_grads(dq, dk16, dv16, n_ref, n_ref, b_ref, ctx_ref, a_ref, put)
    out_split(core[0], om, ot, before, lambda c: dg(half_rows(dq, c), ws[0][...], NN)
              + dg(half_rows(dk16, c), ws[1][...], NN) + dg(half_rows(dv16, c), ws[2][...], NN))
    for h in range(3):
        db_ref[h:h + 1, :] = diagonal_sums(dbias_scr, h)


SELF_BWD_SCRATCH = ([COLS, STATS, BIAS, pltpu.VMEM((3, BQ, 1024), f32)] + [WIDE16] * 5
                    + [WIDE32, WIDE32, WIDE16, WIDE16])
PART = sd((384, 768), bf16)


def self_bwd_first_kernel(core, win, table, mine_in, theirs_in, n_ref, w_ref, seg, ctx, st, b_ref, a_ref, late_ref,
                          om, ot, db_ref, *scr):
    join_rows(core[0], mine_in, theirs_in, b_ref)
    self_bwd_core(core, win, table, b_ref, n_ref, away_weights(w_ref), seg, ctx, st, None, a_ref, put_plain(late_ref, 192),
                  om, ot, db_ref, *scr)


def self_bwd_second_kernel(core, win, table, b_ref, bm, bt, n_ref, wq, wkv, wo, seg, ctx, st, a_ref, late_ref, om, ot,
                           db_ref, *scr):
    self_bwd_core(core, win, table, b_ref, n_ref, own_weights(0, wq, wkv, wo), seg, ctx, st, (bm, bt), a_ref,
                  put_plain(late_ref, 192), om, ot, db_ref, *scr)


def self_bwd_first(core, win, table, mine, theirs, n, w, seg, ctx, st):
    return call(self_bwd_first_kernel, "self_bwd", (core, win, table, mine, theirs, n, w, seg, ctx, st),
                [sd((SLOT, 768), bf16), PART, PART, HALF32, HALF32, sd((3, 1024), f32)], SELF_BWD_SCRATCH, 3, vmem=28)


def self_bwd_second(core, win, table, b, bm, bt, n, weights, seg, ctx, st):
    return call(self_bwd_second_kernel, "self_bwd", (core, win, table, b, bm, bt, n) + weights + (seg, ctx, st),
                [PART, PART, HALF32, HALF32, sd((3, 1024), f32)], SELF_BWD_SCRATCH, 3, vmem=28)


def cross_fwd_kernel(core, win, bits, mine_in, theirs_in, mem_mine, mem_theirs, wq, wkv, wo, pair, wy, wz, seg,
                     sseg_ref, n_ref, m_ref, w_ref, ctx0, st0, ctx1, st1, om, ot, cols, q, k, v, st):
    cols[...] = jnp.transpose(seg[...])
    join_rows(core[0], mine_in, theirs_in, n_ref)
    join_rows(core[0], mem_mine, mem_theirs, m_ref)
    join_quarters(bits, pair, wy, wz, w_ref)
    own, away = own_weights(1, wq, wkv, wo), away_weights(w_ref)
    for ws, ctx_ref, st_ref in ((own, ctx0, st0), (away, ctx1, st1)):
        project(n_ref, ws, (0, q))
        project(m_ref, ws, (1, k), (2, v))

        def block(i, ctx_ref=ctx_ref):
            rows = blk(i)

            @pl.when(win[0, i] == 0)
            def _():
                ctx_ref[rows, :] = jnp.zeros((BQ, 192), bf16)
                st[rows, :] = jnp.zeros((BQ, 8), f32)

            for n, width in enumerate(CROSS_W):
                @pl.when(win[0, i] == n + 1)
                def _(width=width):
                    keys = pl.ds(pl.multiple_of(win[1, i], 128), width)
                    tseg, sseg = cols[rows, 1:2], sseg_ref[:, keys]
                    attend(cross_scores(q, k, tseg, sseg, rows, keys), v, keys, rows, tseg > 0, ctx_ref, st)
        loop(SLOT // BQ, block)
        st_ref[...] = jnp.transpose(st[...])
    out_split(core[0], om, ot, None, lambda c: dg(half_rows(ctx0, c), own[3][...], NN)
              + dg(half_rows(ctx1, c), away[3][...], NN))


def cross_fwd(core, win, bits, mine, theirs, mem_mine, mem_theirs, weights, parts, seg, sseg):
    return call(cross_fwd_kernel, "cross_fwd",
                (core, win, bits, mine, theirs, mem_mine, mem_theirs) + weights + tuple(parts) + (seg, sseg),
                [sd((SLOT, 768), bf16), sd((MEM, 768), bf16), STACK] + ATT + ATT + [HALF32, HALF32],
                [COLS, WIDE16, MEM16, MEM16, STATS], 3, vmem=12)


def cross_bwd_core(core, win, b_ref, n_ref, m_ref, ws, seg, sseg_ref, ctx_ref, st_ref, before, mem_before, a_ref, put,
                   om, ot, mm, mt, cols, st, q, k, v, g_scr, dq, dk, dv, dk16, dv16):
    cols[...] = jnp.transpose(seg[...])
    st[...] = jnp.transpose(st_ref[...])
    project(n_ref, ws, (0, q))
    project(m_ref, ws, (1, k), (2, v))
    dk[...] = jnp.zeros(dk.shape, f32)
    dv[...] = jnp.zeros(dv.shape, f32)
    g = dg(b_ref[...], ws[3][...], NT).astype(bf16)
    g_scr[...] = jnp.where(cols[:, 1:2] > 0, g, jnp.zeros_like(g))

    def block(i):
        rows = blk(i)

        @pl.when(win[0, i] == 0)
        def _():
            dq[rows, :] = jnp.zeros((BQ, 192), bf16)

        for n, width in enumerate(CROSS_W):
            @pl.when(win[0, i] == n + 1)
            def _(width=width):
                keys = pl.ds(pl.multiple_of(win[1, i], 128), width)
                attend_back(cross_scores(q, k, cols[rows, 1:2], sseg_ref[:, keys], rows, keys),
                            q, k, v, g_scr[rows, :], keys, rows, st, dq, dk, dv, lambda sg: None)
    loop(SLOT // BQ, block)
    dk16[...] = dk[...].astype(bf16)
    dv16[...] = dv[...].astype(bf16)
    weight_grads(dq, dk16, dv16, n_ref, m_ref, b_ref, ctx_ref, a_ref, put)
    out_split(core[0], om, ot, before, lambda c: dg(half_rows(dq, c), ws[0][...], NN))
    out_split(core[0], mm, mt, mem_before, lambda c: dg(half_rows(dk16, c), ws[1][...], NN)
              + dg(half_rows(dv16, c), ws[2][...], NN))


CROSS_BWD_SCRATCH = [COLS, STATS, WIDE16, MEM16, MEM16, WIDE16, WIDE16, MEM32, MEM32, MEM16, MEM16]
HALFMEM = sd((MEM // 2, 768), f32)


def cross_bwd_first_kernel(core, win, mine_in, theirs_in, n_ref, m_ref, w_ref, seg, sseg, ctx, st, b_ref, a_ref, late_ref,
                           om, ot, mm, mt, *scr):
    join_rows(core[0], mine_in, theirs_in, b_ref)
    cross_bwd_core(core, win, b_ref, n_ref, m_ref, away_weights(w_ref), seg, sseg, ctx, st, None, None, a_ref,
                   put_plain(late_ref, 192), om, ot, mm, mt, *scr)


def cross_bwd_second_kernel(core, win, b_ref, bm, bt, cm, ct, n_ref, m_ref, wq, wkv, wo, seg, sseg, ctx, st,
                            a_ref, late_ref, om, ot, mm, mt, *scr):
    cross_bwd_core(core, win, b_ref, n_ref, m_ref, own_weights(1, wq, wkv, wo), seg, sseg, ctx, st, (bm, bt), (cm, ct),
                   a_ref, put_plain(late_ref, 192), om, ot, mm, mt, *scr)


def cross_bwd_first(core, win, mine, theirs, n, mem, w, seg, sseg, ctx, st):
    return call(cross_bwd_first_kernel, "cross_bwd", (core, win, mine, theirs, n, mem, w, seg, sseg, ctx, st),
                [sd((SLOT, 768), bf16), PART, PART, HALF32, HALF32, HALFMEM, HALFMEM], CROSS_BWD_SCRATCH, 2, vmem=18)


def cross_bwd_second(core, win, b, before, n, mem, weights, seg, sseg, ctx, st):
    return call(cross_bwd_second_kernel, "cross_bwd",
                (core, win, b) + tuple(before) + (n, mem) + weights + (seg, sseg, ctx, st),
                [PART, PART, HALF32, HALF32, HALFMEM, HALFMEM], CROSS_BWD_SCRATCH, 2, vmem=18)


GELU_C = math.sqrt(2.0 / math.pi)


def ffn_rows(n_ref, c_ref, wg, wu, wo, o_ref, t_ref, before, h_ref, g_ref, u_ref, base):
    def block(i):
        rows = slice(i * BQ, i * BQ + BQ)
        keep = slice(base + i * BQ, base + i * BQ + BQ)
        n = n_ref[rows, :]
        gate, up = dg(n, wg[...], NN), dg(n, wu[...], NN)
        hid = dg(c_ref[rows, :], wo[...], NT)
        square = gate * gate
        th = jnp.tanh(GELU_C * (gate + 0.044715 * (gate * square)))
        half = 0.5 * (1.0 + th)
        gelu = gate * half
        slope = half + (0.5 * GELU_C) * gate * (1.0 - th * th) * (1.0 + (3 * 0.044715) * square)
        h = (gelu * up).astype(bf16)
        gg = (hid * up * slope).astype(bf16)
        ug = (hid * gelu).astype(bf16)
        h_ref[keep, :], g_ref[keep, :], u_ref[keep, :] = h, gg, ug
        out = dg(h, wo[...], NN)
        third = dg(gg, wg[...], NT) + dg(ug, wu[...], NT)
        if before is not None:
            out, third = out + before[0][rows, :], third + before[1][rows, :]
        o_ref[rows, :], t_ref[rows, :] = out, third
    for i in range(n_ref.shape[0] // BQ):
        block(i)


def ffn_core(bits, na, nb, ca, cb, wg, wu, wo, before_a, before_b, outs, h_ref, g_ref, u_ref, dw):
    oa, ob, ta, tb, x_ref, y_keep, y_give, z_keep, z_give = outs
    half = na.shape[0]
    ffn_rows(na, ca, wg, wu, wo, oa, ta, before_a, h_ref, g_ref, u_ref, 0)
    ffn_rows(nb, cb, wg, wu, wo, ob, tb, before_b, h_ref, g_ref, u_ref, half)
    for j, (left, ra, rb) in enumerate(((g_ref, na, nb), (u_ref, na, nb), (h_ref, ca, cb))):
        dw[512 * j:512 * j + 512, :] = (dg(left[0:half, :], ra[...], TN) + dg(left[half:2 * half, :], rb[...], TN)).astype(
            bf16)
    x_ref[...] = dw[0:384, :]
    for base, bit, keep, give in ((384, bits[0], y_keep, y_give), (960, bits[1], z_keep, z_give)):
        keep[...] = dw[pl.ds(pl.multiple_of(base + bit * 288, 16), 288), :]
        give[...] = dw[pl.ds(pl.multiple_of(base + (1 - bit) * 288, 16), 288), :]


def ffn_away_kernel(bits, na, nb, ca, cb, f0, fy, fz, f3, *refs):
    w2, wo = refs[-2:]
    for step, part in enumerate((f0, fy, fz, f3)):
        y, z = quarter_of(bits, step)
        w2[y, pl.ds(pl.multiple_of(z * 384, 128), 384), :] = part[0:384, :]
        at = pl.multiple_of((2 * y + z) * 128, 128)
        wo[pl.ds(at, 128), 0:512] = part[384:512, :]
        wo[pl.ds(at, 64), 512:768] = part[512:576, 0:256]
        wo[pl.ds(pl.multiple_of(at + 64, 64), 64), 512:768] = part[512:576, 256:512]
    ffn_core(bits, na, nb, ca, cb, w2.at[0], w2.at[1], wo, None, None, refs[:9], *refs[9:13])


def ffn_own_kernel(bits, na, nb, ca, cb, wi, wo, pa, pb, sa, sb, *refs):
    ffn_core(bits, na, nb, ca, cb, wi.at[0], wi.at[1], wo, (pa, sa), (pb, sb), refs[:9], *refs[9:13])


def ffn_outs(rows):
    return [sd((rows, 768), f32)] * 4 + [sd((384, 768), bf16)] + [sd((288, 768), bf16)] * 4


def ffn_scratch(rows, units):
    return [pltpu.VMEM((2 * rows, units), bf16)] * 3 + [pltpu.VMEM((3 * units, 768), bf16)]


def ffn_away(bits, na, nb, ca, cb, weights):
    rows, units = na.shape[0], weights[0].shape[1]
    scratch = ffn_scratch(rows, units) + [pltpu.VMEM((2, 768, units), bf16), pltpu.VMEM((units, 768), bf16)]
    return call(ffn_away_kernel, "ffn_away", (bits, na, nb, ca, cb) + tuple(weights), ffn_outs(rows), scratch, 1, vmem=22)


def ffn_own(bits, na, nb, ca, cb, wi, wo, before):
    rows, units = na.shape[0], wo.shape[0]
    return call(ffn_own_kernel, "ffn_own", (bits, na, nb, ca, cb, wi, wo) + tuple(before), ffn_outs(rows),
                ffn_scratch(rows, units), 1, vmem=20)


def merge_kernel(actions, outs):
    def kernel(bits, *refs):
        ins, dest = refs[:len(refs) - outs], refs[len(refs) - outs:]

        def total(terms, extra, count):
            value = None
            for src, at in terms:
                part = ins[src][pl.ds(pl.multiple_of(at + extra, 16), count), :].astype(f32)
                value = part if value is None else value + part
            return value.astype(bf16)

        for action in actions:
            if action[0] == "split":
                _, terms, count, bit, (keep, kat), (give, gat) = action
                half = count // 2
                dest[keep][kat:kat + half, :] = total(terms, bits[bit] * half, half)
                dest[give][gat:gat + half, :] = total(terms, (1 - bits[bit]) * half, half)
            elif action[0] == "sum":
                _, terms, count, (out, at) = action
                dest[out][at:at + count, :] = total(terms, 0, count)
            else:
                _, (own, own_at), (other, other_at), count, bit, (out, at) = action
                dest[out][pl.ds(pl.multiple_of(at + bits[bit] * count, 16), count), :] = ins[own][own_at:own_at + count, :]
                dest[out][pl.ds(pl.multiple_of(at + (1 - bits[bit]) * count, 16), count), :] = (
                    ins[other][other_at:other_at + count, :])
    return kernel


def merge(bits, ins, actions, sizes):
    outs = [sd((rows, 768), bf16) for rows in sizes]
    return call(merge_kernel(actions, len(outs)), "merge", (bits,) + tuple(ins), outs, (), 1, vmem=16)


def ffn_finish_kernel(bits, fin, y_in, z_in, gi, go, model, unit, scr):
    for base, half, bit, own, other in ((0, 192, bits[0], fin[0:192, :], y_in[0:192, :]),
                                        (384, 288, bits[0], fin[192:480, :], y_in[192:480, :]),
                                        (960, 288, bits[1], fin[480:768, :], z_in[...])):
        scr[pl.ds(pl.multiple_of(base + bit * half, 16), half), :] = own
        scr[pl.ds(pl.multiple_of(base + (1 - bit) * half, 16), half), :] = other
    for j in range(3):
        g = scr[512 * j:512 * j + 512, :].astype(f32)
        if j < 2:
            gi[j] = jnp.transpose(g)
        else:
            go[...] = g
        sq = g * g
        model[j:j + 1, :] = jnp.sum(sq, axis=0, keepdims=True)
        unit[j:j + 1, :] = jnp.transpose(jnp.sum(sq, axis=1, keepdims=True)) * (1.0 / D)


def ffn_finish(bits, fin, y_in, z_in):
    units = 512
    return call(ffn_finish_kernel, "ffn_finish", (bits, fin, y_in, z_in),
                [sd((2, 768, units), f32), sd((units, 768), f32), sd((3, 768), f32), sd((3, units), f32)],
                [pltpu.VMEM((3 * units, 768), bf16)], 1, vmem=20)


def finish_part(a, bits, fin, y_in, z_in, put, model, head, proj, rows, scr):
    for base, bit, own, other in ((0, bits[1], fin[0:192, :], z_in), (384, bits[0], fin[192:384, :], y_in)):
        scr[pl.ds(pl.multiple_of(base + bit * 192, 16), 192), :] = own
        scr[pl.ds(pl.multiple_of(base + (1 - bit) * 192, 16), 192), :] = other[...]
    for j in range(4):
        w = scr[192 * j:192 * j + 192, :].astype(f32)
        put(j, w)
        sq = w * w
        model[rows[j]:rows[j] + 1, :] = jnp.sum(sq, axis=0, keepdims=True)
        side = jnp.transpose(jnp.sum(sq, axis=1, keepdims=True)) * (1.0 / D)
        if j < 3:
            head[rows[j]:rows[j] + 1, :] = side
        else:
            proj[a:a + 1, :] = side


def early_kernel(bits, c_fin, c_y, c_z, fm_ref, qg, kvg, og, model, head, proj, scr):
    def put(j, w):
        if j == 0:
            qg[0] = w
        elif j == 3:
            og[0] = w
        else:
            kvg[0, j - 1] = w
    model[...] = jnp.zeros(model.shape, f32)
    head[...] = jnp.zeros(head.shape, f32)
    proj[...] = jnp.zeros(proj.shape, f32)
    finish_part(1, bits, c_fin, c_y, c_z, put, model, head, proj, (1, 4, 5, 9), scr)
    model[6:8, :] = fm_ref[0:2, :]
    model[10:11, :] = fm_ref[2:3, :]


def late_kernel(bits, s_fin, s_y, s_z, model_in, head_in, proj_in, _q, _kv, _o, qg, kvg, og, model, head, proj, scr):
    def put(j, w):
        if j == 0:
            qg[0] = w
        elif j == 3:
            og[0] = w
        else:
            kvg[0, j - 1] = w
    model[...] = model_in[...]
    head[...] = head_in[...]
    proj[...] = proj_in[...]
    finish_part(0, bits, s_fin, s_y, s_z, put, model, head, proj, (0, 2, 3, 8), scr)


def finish_call(kernel, layer, args, extra, aliases):
    def whole(a):
        return pl.BlockSpec(a.shape, lambda i, bits, n=len(a.shape): (0,) * n)
    outs = [sd((2, 192, 768), f32), sd((2, 2, 192, 768), f32), sd((2, 192, 768), f32), sd((11, 768), f32),
            sd((6, 192), f32), sd((2, 192), f32)]
    one = pl.BlockSpec((1, 192, 768), lambda i, bits: (layer, 0, 0))
    pair = pl.BlockSpec((1, 2, 192, 768), lambda i, bits: (layer, 0, 0, 0))
    return pl.pallas_call(
        kernel,
        grid_spec=pltpu.PrefetchScalarGridSpec(
            num_scalar_prefetch=1, grid=(1,),
            in_specs=[whole(a) for a in args[1:]] + [pl.BlockSpec(memory_space=pl.ANY)] * len(extra),
            out_specs=[one, pair, one] + [whole(a) for a in outs[3:]],
            scratch_shapes=[pltpu.VMEM((768, 768), bf16)]),
        out_shape=outs,
        input_output_aliases=aliases,
        name="finish",
        compiler_params=pltpu.CompilerParams(vmem_limit_bytes=16 << 20),
        cost_estimate=pl.CostEstimate(flops=0, bytes_accessed=4000000, transcendentals=0))(*args, *extra)


def finish_early(bits, cross_parts, ffn_model):
    return finish_call(early_kernel, 1, (bits,) + tuple(cross_parts) + (ffn_model,), (), {})


def finish_late(bits, self_parts, early):
    return finish_call(late_kernel, 0, (bits,) + tuple(self_parts) + tuple(early[3:]), tuple(early[:3]),
                       {7: 0, 8: 1, 9: 2})


CORE = [(i, i ^ 1) for i in range(4)]
CHIP = [(i, i ^ 2) for i in range(4)]


def swap_core(v):
    return lax.ppermute(v, "tensor", CORE)


def swap_chip(v):
    return lax.ppermute(v, "tensor", CHIP)


def swap_dp(v, bit):
    return lax.ppermute(v, "dp", [(i, i ^ (1 << bit)) for i in range(lax.axis_size("dp"))])


def dp_bits():
    return int(math.log2(lax.axis_size("dp")))


def after(value, *earlier):
    return lax.optimization_barrier((value,) + earlier)[0]


def sync(*values):
    return lax.optimization_barrier(values)


def over_group(v):
    diagonal = lax.ppermute(v, "tensor", [(i, i ^ 3) for i in range(4)])
    return (v + swap_core(v)) + (swap_chip(v) + diagonal)


def over_first_bits(v):
    diagonal = lax.ppermute(v, "dp", [(i, i ^ 3) for i in range(lax.axis_size("dp"))])
    return (v + swap_dp(v, 0)) + (swap_dp(v, 1) + diagonal)


def past(value, bit):
    for one in range(bit, dp_bits()):
        value = (value.astype(f32) + swap_dp(value, one).astype(f32)).astype(bf16)
    return value


def bucket_sums(lane_sums):
    lane = np.arange(1024)
    distance = 512 - np.where(lane < 768, lane, lane - 1024)
    buckets = jnp.asarray(np.array([bucket_of(max(int(n), 0)) for n in distance], np.int32))
    onehot = (buckets[:, None] == jnp.arange(BUCKETS)[None, :]) & jnp.asarray(distance >= 0)[:, None]
    return lax.dot_general(onehot.astype(f32), lane_sums, (((0,), (1,)), ((), ())), precision=lax.Precision.HIGHEST,
                           preferred_element_type=f32)


def on_device(tokens, memory, cotangent, norm_gains, query_weight, keyvalue_weight, output_weight, bias_table,
              inner_weight, outer_weight, target_lengths, source_lengths):
    t, d = lax.axis_index("tensor"), lax.axis_index("dp")
    core = (t & 1).reshape(1).astype(i32)
    slot = lax.shift_right_logical(t, 1).reshape(1).astype(i32)
    bits = (lax.shift_right_logical(d, jnp.arange(3)) & 1).astype(i32)
    gains = [norm_gains[i:i + 1] for i in range(3)]
    weights = (jnp.swapaxes(query_weight, 1, 2), jnp.swapaxes(keyvalue_weight, 2, 3), output_weight)

    table_away = swap_chip(bias_table)
    q_self = weight_quarters(bits, 0, *weights)
    table_away, q_self, tokens, bits2 = sync(table_away, q_self, tokens, bits)
    s0 = swap_chip(q_self)
    q_cross = weight_quarters(bits2, 1, *weights)
    n1m = norm_rows(tokens, gains[0])
    n1t = swap_core(n1m)
    seg, sseg, swin, cwin = slot_layout(slot, target_lengths, source_lengths)
    n1, ctx_s0, st_s0, pm, pt = self_fwd_first(core, swin, bias_table, n1m, n1t, weights, seg)
    s0, n1, q_cross, memory, cotangent = sync(s0, n1, q_cross, memory, cotangent)
    sy, sz = swap_dp(s0[:192], 0), swap_dp(s0[:192], 1)
    c0 = swap_chip(q_cross)
    mem_t, cot_t = swap_core(memory), swap_core(cotangent)
    fq0, fq3 = packed(bits, inner_weight, outer_weight)
    sy, sz, n1, fq0, fq3, c0 = sync(sy, sz, n1, fq0, fq3, c0)
    f0 = swap_chip(fq0)
    cy, cz = swap_dp(c0[:192], 0), swap_dp(c0[:192], 1)
    w_self_away, ctx_s1, st_s1, pm, pt = self_fwd_second(core, swin, table_away, bits, n1, pm, pt, (s0, sy, sz), seg)
    f0, cy, cz, pm, pt, fq3 = sync(f0, cy, cz, pm, pt, fq3)
    f3 = swap_chip(fq3)
    fy, fz = swap_dp(f0, 0), swap_dp(f0, 1)
    after_self, n2m = add_norm(tokens, pm, swap_core(pt), gains[1])

    n2, mem, w_cross_away, ctx_c0, st_c0, ctx_c1, st_c1, pm, pt = cross_fwd(
        core, cwin, bits, n2m, swap_core(n2m), memory, mem_t, weights, (c0, cy, cz), seg, sseg)
    f3, fy, fz, pm, pt = sync(f3, fy, fz, pm, pt)
    after_cross, n3m = add_norm(after_self, pm, swap_core(pt), gains[2])

    n3t = swap_core(n3m)
    oa, ob, ta, tb, px, pyk, pyg, pzk, pzg = ffn_away(bits, n3m, n3t, cotangent, cot_t, (f0, fy, fz, f3))
    n3m, px, pyg, pzg = sync(n3m, px, pyg, pzg)
    xi, yi, zi = swap_chip(px), swap_dp(pyg, 0), swap_dp(pzg, 1)
    oa, ob, ta, tb, ox, oyk, oyg, ozk, ozg = ffn_own(bits, n3m, n3t, cotangent, cot_t, inner_weight, outer_weight,
                                                     (oa, ob, ta, tb))
    xi, yi, zi, oa, ob, ta, tb, ox, oyg, ozg = sync(xi, yi, zi, oa, ob, ta, tb, ox, oyg, ozg)
    fx_k, xp, yp = merge(
        bits, (ox, xi, pyk, yi, pzk, zi, oyg),
        (("split", ((0, 0), (1, 0)), 384, 0, (0, 0), (2, 0)),
         ("sum", ((2, 0), (3, 0)), 288, (1, 0)),
         ("sum", ((4, 0), (5, 0)), 288, (1, 288)),
         ("sum", ((6, 0),), 288, (2, 192))), (192, 576, 480))
    xi, yi, zi = swap_chip(xp), swap_dp(yp, 0), swap_dp(ozg, 1)
    cross_out_m, branch_m, gain2 = norm_back(after_cross, gains[2], cotangent, ta, swap_core(tb))

    branch, c_out, c_late, pm, pt, mm, mt = cross_bwd_first(core, cwin, branch_m, swap_core(branch_m), n2, mem,
                                                            w_cross_away, seg, sseg, ctx_c1, st_c1)
    xi, yi, zi, branch, c_out, c_late, pm, pt, mm, mt = sync(xi, yi, zi, branch, c_out, c_late, pm, pt, mm, mt)
    fx_k, fy_k, fz_k, cb_k, yp, zp = merge(
        bits, (fx_k, yi, oyk, xi, ozk, zi, c_late),
        (("split", ((0, 0), (1, 0)), 192, 1, (0, 0), (5, 0)),
         ("split", ((2, 0), (1, 192), (3, 0)), 288, 1, (1, 0), (5, 96)),
         ("split", ((4, 0), (5, 0), (3, 288)), 288, 0, (2, 0), (4, 0)),
         ("split", ((6, 0),), 384, 0, (3, 0), (4, 144))), (96, 144, 144, 192, 336, 240))
    xi, yi, zi = swap_chip(c_out), swap_dp(yp, 0), swap_dp(zp, 1)
    branch, zp = sync(branch, zp)
    c_a, c_own, pm, pt, mm, mt = cross_bwd_second(core, cwin, branch, (pm, pt, mm, mt), n2, mem, weights, seg, sseg,
                                                  ctx_c0, st_c0)
    xi, yi, zi, c_a, c_own, pm, pt, mm, mt = sync(xi, yi, zi, c_a, c_own, pm, pt, mm, mt)
    f_mid, ca_k, cb_o, xp, yp, zp = merge(
        bits, (fx_k, zi, fy_k, fz_k, yi, c_a, xi, cb_k, c_own),
        (("sum", ((0, 0), (1, 0)), 96, (0, 0)),
         ("sum", ((2, 0), (1, 96)), 144, (0, 96)),
         ("sum", ((3, 0), (4, 0)), 144, (0, 240)),
         ("split", ((5, 0), (6, 0)), 384, 1, (1, 0), (5, 0)),
         ("sum", ((7, 0), (4, 144)), 192, (3, 0)),
         ("split", ((8, 0),), 384, 0, (2, 0), (4, 0))), (384, 192, 192, 192, 192, 192))
    pt, f_mid, xp, yp, zp = sync(pt, f_mid, xp, yp, zp)
    xi, yi, zi, z2i = swap_chip(xp), swap_dp(yp, 0), swap_dp(zp, 1), swap_dp(f_mid, 2)
    self_out_m, branch_m, gain1 = norm_back(after_self, gains[1], cross_out_m, pm, swap_core(pt))

    branch, s_out, s_late, pm, pt, lanes_away = self_bwd_first(core, swin, table_away, branch_m, swap_core(branch_m), n1,
                                                               w_self_away, seg, ctx_s1, st_s1)
    z2i, xi, yi, zi, branch, s_out, s_late, pm, pt = sync(z2i, xi, yi, zi, branch, s_out, s_late, pm, pt)
    f_own, ca_k, cb_k, sb_k, yp, zp = merge(
        bits, (f_mid, z2i, ca_k, zi, cb_o, yi, xi, s_late),
        (("sum", ((0, 0), (1, 0)), 384, (0, 0)),
         ("sum", ((0, 0), (1, 0)), 240, (5, 0)),
         ("sum", ((0, 240), (1, 240)), 144, (4, 0)),
         ("split", ((2, 0), (3, 0)), 192, 0, (1, 0), (4, 144)),
         ("split", ((4, 0), (5, 0), (6, 0)), 192, 1, (2, 0), (5, 240)),
         ("split", ((7, 0),), 384, 0, (3, 0), (4, 240))), (384, 96, 96, 192, 432, 336))
    if dp_bits() > 3:
        f_own = past(f_own, 3)
        yp, zp = jnp.concatenate((f_own[240:], yp[144:])), jnp.concatenate((f_own[:240], zp[240:]))
    xi, yi, zi = swap_chip(s_out), swap_dp(yp, 0), swap_dp(zp, 1)
    branch, zp = sync(branch, zp)
    s_a, s_own, pm, pt, lanes_own = self_bwd_second(core, swin, bias_table, branch, pm, pt, n1, weights, seg, ctx_s0, st_s0)
    xi, yi, zi, s_a, s_own, pm, pt, lanes_own = sync(xi, yi, zi, s_a, s_own, pm, pt, lanes_own)

    f_fin, c_mid, sa_k, sb_o, xp, yp, zp = merge(
        bits, (f_own, zi, yi, ca_k, cb_k, s_a, xi, sb_k, s_own),
        (("join", (0, 0), (1, 0), 96, 1, (0, 0)),
         ("join", (0, 96), (1, 96), 144, 1, (0, 192)),
         ("join", (0, 240), (2, 0), 144, 0, (0, 480)),
         ("join", (0, 0), (1, 0), 96, 1, (5, 0)),
         ("join", (0, 96), (1, 96), 144, 1, (5, 192)),
         ("join", (0, 240), (2, 0), 144, 0, (6, 0)),
         ("sum", ((3, 0), (2, 144)), 96, (1, 0)),
         ("sum", ((4, 0), (1, 240)), 96, (1, 96)),
         ("split", ((5, 0), (6, 0)), 384, 1, (2, 0), (6, 288)),
         ("sum", ((7, 0), (2, 240)), 192, (4, 0)),
         ("split", ((8, 0),), 384, 0, (3, 0), (5, 480))), (768, 192, 192, 192, 192, 672, 480))
    pt_in, mt_in, ob_in = swap_core(pt), swap_core(mt), swap_core(ob)
    xi, yi, zi, z2i = swap_chip(xp), swap_dp(yp, 0), swap_dp(zp, 1), swap_dp(c_mid, 2)
    z2i, xi, yi, zi, pt_in, mt_in, ob_in, lanes_away = sync(z2i, xi, yi, zi, pt_in, mt_in, ob_in, lanes_away)
    c_own, sa_k, sb_k, yp, zp = merge(
        bits, (c_mid, z2i, sa_k, zi, sb_o, yi, xi),
        (("sum", ((0, 0), (1, 0)), 192, (0, 0)),
         ("sum", ((0, 0), (1, 0)), 96, (3, 0)),
         ("sum", ((0, 96), (1, 96)), 96, (4, 0)),
         ("split", ((2, 0), (3, 288)), 192, 0, (1, 0), (3, 96)),
         ("split", ((4, 0), (5, 480), (6, 0)), 192, 1, (2, 0), (4, 96))), (192, 96, 96, 192, 192))
    f_y, f_z = yi[:480], zi[:288]
    if dp_bits() > 3:
        c_own = past(c_own, 3)
        yp, zp = jnp.concatenate((c_own[:96], yp[96:])), jnp.concatenate((c_own[96:], zp[96:]))
    yi, zi = swap_dp(yp, 0), swap_dp(zp, 1)
    tokens_grad, _, gain0 = norm_back(tokens, gains[0], self_out_m, pm, pt_in)
    small = jnp.concatenate((gain0, gain1, gain2))
    memory_grad = mm + mt_in
    output_rows = (after_cross + (oa + ob_in)).astype(bf16)
    yi, zi, small, memory_grad, output_rows, lanes_away = sync(yi, zi, small, memory_grad, output_rows, lanes_away)
    c_fin, s_mid, yp, zp = merge(
        bits, (c_own, yi, zi, sa_k, sb_k),
        (("join", (0, 0), (1, 0), 96, 0, (0, 0)),
         ("join", (0, 96), (2, 0), 96, 1, (0, 192)),
         ("join", (0, 0), (1, 0), 96, 0, (3, 0)),
         ("join", (0, 96), (2, 0), 96, 1, (2, 0)),
         ("sum", ((3, 0), (1, 96)), 96, (1, 0)),
         ("sum", ((4, 0), (2, 96)), 96, (1, 96))), (384, 192, 192, 192))
    z2i, c_y, c_z = swap_dp(s_mid, 2), swap_dp(yp, 0), swap_dp(zp, 1)
    f_fin = sync(f_fin, yp, zp, s_mid)[0]
    inner_sum, outer_sum, ffn_model, unit_stats = ffn_finish(bits, f_fin, f_y, f_z)
    z2i, c_y, c_z, ffn_model = sync(z2i, c_y, c_z, ffn_model)
    (s_own,) = merge(bits, (s_mid, z2i), (("sum", ((0, 0), (1, 0)), 192, (0, 0)),), (192,))
    s_own = past(s_own, 3)
    yi, zi = swap_dp(s_own[:96], 0), swap_dp(s_own[96:], 1)
    small, lanes_away = sync(small, lanes_away, s_own)[:2]
    lanes_in = swap_chip(lanes_away)
    small = over_group(small)
    yi, zi, small, lanes_in = sync(yi, zi, small, lanes_in)
    small = jnp.concatenate((jnp.pad(small, ((0, 0), (0, 256))), lanes_own + lanes_in))
    s_fin, yp, zp = merge(
        bits, (s_own, yi, zi),
        (("join", (0, 0), (1, 0), 96, 0, (0, 0)),
         ("join", (0, 96), (2, 0), 96, 1, (0, 192)),
         ("join", (0, 0), (1, 0), 96, 0, (2, 0)),
         ("join", (0, 96), (2, 0), 96, 1, (1, 0))), (384, 192, 192))
    s_y, s_z, small = swap_dp(yp, 0), swap_dp(zp, 1), over_first_bits(small)
    early = finish_early(bits, (c_fin, c_y, c_z), sync(ffn_model, yp)[0])
    s_y, s_z, small, *early = sync(s_y, s_z, small, *early)
    for bit in range(2, dp_bits()):
        small = small + swap_dp(small, bit)
    gains_total = small[:3, :D]
    table_sum = bucket_sums(small[3:])
    query_t, keyvalue_t, output_grad, model_part, head_stats, projection_stats = finish_late(bits, (s_fin, s_y, s_z), early)
    query_grad, keyvalue_grad = jnp.swapaxes(query_t, 1, 2), jnp.swapaxes(keyvalue_t, 2, 3)
    model_total = over_group(model_part)
    hidden_units = outer_weight.shape[0] * lax.axis_size("tensor")
    divisors = jnp.array([D] * 6 + [hidden_units] * 2 + [D] * 2 + [hidden_units], f32)
    model_stats = model_total / divisors[:, None]
    return (output_rows, tokens_grad, memory_grad, gains_total, query_grad, keyvalue_grad, output_grad, table_sum,
            inner_sum, outer_sum, model_stats, head_stats, projection_stats, unit_stats)


def solution(mesh):
    rows = P(("dp", "tensor"), None)
    in_specs = (rows, rows, rows, P(), P(None, None, "tensor"), P(None, None, None, "tensor"), P(None, "tensor", None),
                P(None, "tensor"), P(None, None, "tensor"), P("tensor", None), P("dp", None), P("dp", None))
    out_specs = (rows, rows, rows, P(), P(None, None, "tensor"), P(None, None, None, "tensor"),
                 P(None, "tensor", None), P(None, "tensor"), P(None, None, "tensor"), P("tensor", None), P(),
                 P(None, "tensor"), P(None, "tensor"), P(None, "tensor"))
    return jax.shard_map(on_device, mesh=mesh, in_specs=in_specs, out_specs=out_specs, check_vma=False)
```

```python
import math

import jax
import jax.numpy as jnp
import numpy as np
from jax import lax
from jax.experimental import pallas as pl
from jax.experimental.pallas import tpu as pltpu
from jax.sharding import PartitionSpec as P

D = 768
DH = 64
BUCKETS = 32
MAXDIST = 128
SLOT = 1024
MEM = 512
NORM_EPS = 1e-06
NEG_FILL = -1e30
DEAD = 1 << 20
BQ = 256
COST = 0.02
VM = pl.BlockSpec(memory_space=pltpu.VMEM)
SM = pl.BlockSpec(memory_space=pltpu.SMEM)
NT = (((1,), (1,)), ((), ()))
NN = (((1,), (0,)), ((), ()))
TN = (((0,), (0,)), ((), ()))
f32, bf16, i32 = jnp.float32, jnp.bfloat16, jnp.int32
SELF_W = (256, 384, 512, 768)
CROSS_W = (128, 256, 512)
sd = jax.ShapeDtypeStruct


def dg(a, b, dims):
    return lax.dot_general(a, b, dims, preferred_element_type=f32)


def blk(i):
    return pl.ds(pl.multiple_of(i * BQ, BQ), BQ)


def loop(count, body):
    def step(i, carry):
        body(i)
        return carry
    lax.fori_loop(0, count, step, 0)


def call(kernel, name, args, outs, scratch=(), scalars=0, vmem=12, flops=1e9, out_specs=None):
    byts = sum(int(np.prod(a.shape)) * a.dtype.itemsize for a in tuple(args) + tuple(outs))
    return pl.pallas_call(
        kernel,
        in_specs=[SM] * scalars + [VM] * (len(args) - scalars),
        out_specs=list(out_specs) if out_specs else [VM] * len(outs),
        out_shape=list(outs),
        scratch_shapes=list(scratch),
        name=name,
        compiler_params=pltpu.CompilerParams(vmem_limit_bytes=vmem << 20),
        cost_estimate=pl.CostEstimate(flops=int(flops * COST), bytes_accessed=int(byts * COST), transcendentals=0),
    )(*args)


def bucket_of(spread):
    exact_count = BUCKETS // 2
    if spread < exact_count:
        return spread
    larger = exact_count + math.floor(
        math.log(spread / exact_count) / math.log(MAXDIST / exact_count) * (BUCKETS - exact_count)
    )
    return min(larger, BUCKETS - 1)


def bucket_starts():
    buckets = [bucket_of(n) for n in range(SLOT)]
    return [next(n for n in range(SLOT + 1) if n == SLOT or buckets[n] >= b) for b in range(BUCKETS)]


def layout_kernel(slot, tl_ref, sl_ref, seg_ref, sseg_ref, swin, cwin):
    s = slot[0]
    docs = tl_ref.shape[1]
    tl = [tl_ref[s, j] for j in range(docs)]
    sl = [sl_ref[s, j] for j in range(docs)]
    ends, sends = [], []
    te, se = jnp.int32(0), jnp.int32(0)
    for j in range(docs):
        te, se = te + tl[j], se + sl[j]
        ends.append(te)
        sends.append(se)
    pos = lax.broadcasted_iota(i32, (1, SLOT), 1)
    spos = lax.broadcasted_iota(i32, sseg_ref.shape, 1)
    start, seg, mseg = jnp.zeros_like(pos), jnp.ones_like(pos), jnp.ones_like(spos)
    for j in range(docs):
        past = pos >= ends[j]
        start = jnp.where(past, ends[j], start)
        seg = seg + past.astype(i32)
        mseg = mseg + (spos >= sends[j]).astype(i32)
    live = pos < te
    seg_ref[...] = jnp.zeros(seg_ref.shape, i32)
    seg_ref[0:1, :] = jnp.where(live, start, DEAD)
    seg_ref[1:2, :] = jnp.where(live, seg, -1)
    sseg_ref[...] = jnp.where(spos < se, mseg, 0)
    for i in range(SLOT // BQ):
        q0 = i * BQ
        first, low, high = jnp.int32(0), jnp.int32(0), jnp.int32(0)
        last = jnp.minimum(q0 + BQ - 1, te - 1)
        for j in range(docs):
            before = ends[j] <= q0
            first = jnp.where(before, ends[j], first)
            low = low + jnp.where(before, sl[j], 0)
            high = high + jnp.where(ends[j] - tl[j] <= last, sl[j], 0)
        need = q0 + BQ - lax.shift_left(lax.shift_right_logical(first, 7), 7)
        width = jnp.int32(1)
        for w in SELF_W[:-1]:
            width = width + jnp.where(need > w, 1, 0)
        swin[i] = jnp.where(q0 < te, width, 0)
        at1 = lax.shift_left(lax.shift_right_logical(low, 7), 7)
        at2 = jnp.minimum(at1, MEM - 256)
        one, two = high - at1 <= 128, high - at2 <= 256
        cwin[0, i] = jnp.where(q0 < te, jnp.where(one, 1, jnp.where(two, 2, 3)), 0)
        cwin[1, i] = jnp.where(one, at1, jnp.where(two, at2, 0))


def slot_layout(slot, tl, sl):
    return call(layout_kernel, "layout", (slot, tl, sl),
                (sd((8, SLOT), i32), sd((1, MEM), i32), sd((4,), i32), sd((2, 4), i32)),
                scalars=3, flops=1e6, out_specs=(VM, VM, SM, SM))


def quarter_of(bits, step):
    y, z = bits[0], bits[1]
    return (1 - y if step & 1 else y), (1 - z if step & 2 else z)


def quarters_kernel(bits, q_ref, kv_ref, o_ref, out):
    mine = bits[0] + 2 * bits[1]
    for n, ref in enumerate((q_ref.at[0], kv_ref.at[0, 0], kv_ref.at[0, 1], o_ref.at[0])):
        @pl.when(mine == n)
        def _(ref=ref):
            out[0:192, :] = ref[...]

        @pl.when(mine == 3 - n)
        def _(ref=ref):
            out[192:384, :] = ref[...]


def weight_quarters(bits, layer, q, kv, o):
    one = pl.BlockSpec((1, 192, 768), lambda i, bits: (layer, 0, 0))
    if layer == 0:
        q, kv, o = (pltpu.with_memory_space_constraint(a, pltpu.HBM) for a in (q, kv, o))
    return pl.pallas_call(
        quarters_kernel,
        grid_spec=pltpu.PrefetchScalarGridSpec(
            num_scalar_prefetch=1, grid=(1,),
            in_specs=[one, pl.BlockSpec((1, 2, 192, 768), lambda i, bits: (layer, 0, 0, 0)), one],
            out_specs=pl.BlockSpec((384, 768), lambda i, bits: (0, 0))),
        out_shape=sd((384, 768), bf16),
        name="quarters",
        compiler_params=pltpu.CompilerParams(vmem_limit_bytes=8 << 20),
        cost_estimate=pl.CostEstimate(flops=0, bytes_accessed=1200000, transcendentals=0))(bits, q, kv, o)


def join_quarters(bits, pair, side_y, side_z, w_ref):
    for step, part in enumerate((pair[0:192, :], side_y[...], side_z[...], pair[192:384, :])):
        y, z = quarter_of(bits, step)
        w_ref[pl.ds(pl.multiple_of((y + 2 * z) * 192, 16), 192), :] = part


def pack_kernel(bits, wi_ref, wo_ref, f0_ref, f3_ref):
    for f_ref, step in ((f0_ref, 0), (f3_ref, 3)):
        y, z = quarter_of(bits, step)
        f_ref[0:384, :] = wi_ref[y, pl.ds(pl.multiple_of(z * 384, 128), 384), :]
        outer = wo_ref[pl.ds(pl.multiple_of((2 * y + z) * 128, 128), 128), :]
        f_ref[384:512, :] = outer[:, 0:512]
        f_ref[512:576, 0:256] = outer[0:64, 512:768]
        f_ref[512:576, 256:512] = outer[64:128, 512:768]


def packed(bits, wi, wo):
    return call(pack_kernel, "pack", (bits, wi, wo), (sd((576, 512), bf16),) * 2, (), 1)


def own_weights(which, q_ref, kv_ref, o_ref):
    return (q_ref.at[which], kv_ref.at[which, 0], kv_ref.at[which, 1], o_ref.at[which])


def away_weights(w_ref):
    return tuple(w_ref.at[192 * j:192 * j + 192] for j in range(4))


def norm_kernel(x_ref, gain_ref, n_ref):
    x = x_ref[...].astype(f32)
    r = lax.rsqrt(jnp.mean(x * x, axis=-1, keepdims=True) + NORM_EPS)
    n_ref[...] = (x * r * gain_ref[0:1, :]).astype(bf16)


def norm_rows(x, gain):
    return call(norm_kernel, "norm", (x, gain), (sd(x.shape, bf16),), flops=1e6)[0]


def add_norm_kernel(which):
    def kernel(x_ref, a_ref, b_ref, gain_ref, y_ref, n_ref):
        y = x_ref[...].astype(f32) + (a_ref[...] + b_ref[...])
        y_ref[...] = y
        r = lax.rsqrt(jnp.mean(y * y, axis=-1, keepdims=True) + NORM_EPS)
        n_ref[...] = (y * r * gain_ref[which:which + 1, :]).astype(bf16)
    return kernel


def add_norm(x, a, b, gain, which):
    return call(add_norm_kernel(which), "add_norm", (x, a, b, gain), (sd(x.shape, f32), sd(x.shape, bf16)), flops=1e6)


def norm_back_kernel(terms, which):
    def kernel(v_ref, gain_ref, up_ref, *refs):
        total_ref, branch_ref, sum_ref = refs[terms:]
        grad = refs[0][...].astype(f32)
        for ref in refs[1:terms]:
            grad = grad + ref[...].astype(f32)
        v = v_ref[...].astype(f32)
        r = lax.rsqrt(jnp.mean(v * v, axis=-1, keepdims=True) + NORM_EPS)
        scaled = grad * gain_ref[which:which + 1, :]
        back = r * scaled - v * ((r * r * r) * jnp.mean(scaled * v, axis=-1, keepdims=True))
        total = up_ref[...].astype(f32) + back
        total_ref[...] = total
        branch_ref[...] = total.astype(bf16)
        sum_ref[...] = jnp.sum(grad * v * r, axis=0, keepdims=True)
    return kernel


def norm_back(v, gain, which, up, *grads):
    return call(norm_back_kernel(len(grads), which), "norm_back", (v, gain, up) + grads,
                (sd(v.shape, f32), sd(v.shape, bf16), sd((1, v.shape[1]), f32)), flops=1e6)


LANES = (slice(0, 128), slice(0, 128), slice(128, 192))


def head_of(rows128, h):
    if h == 2:
        return rows128
    lane = lax.broadcasted_iota(i32, rows128.shape, 1)
    return jnp.where((lane < 64) == (h == 0), rows128, jnp.zeros_like(rows128))


def pair_of(first, second):
    lane = lax.broadcasted_iota(i32, first.shape, 1)
    return jnp.where(lane < 64, first, second)


def half_rows(ref, which):
    half = ref.shape[0] // 2
    return ref[pl.ds(pl.multiple_of(which * half, half), half), :]


def join_rows(core, mine_ref, theirs_ref, all_ref):
    half = mine_ref.shape[0]
    at = pl.multiple_of(core * half, half)
    all_ref[pl.ds(at, half), :] = mine_ref[...]
    all_ref[pl.ds(pl.multiple_of(half - at, half), half), :] = theirs_ref[...]


def out_split(core, mine_ref, theirs_ref, before, value_of):
    for pos, ref in enumerate((mine_ref, theirs_ref)):
        value = value_of(core if pos == 0 else 1 - core)
        ref[...] = value if before is None else value + before[pos][...]


def fill_bias(table, bias_scr):
    lane = lax.broadcasted_iota(i32, (1, 1024), 1)
    distance = 512 - jnp.where(lane < 768, lane, lane - 1024)
    for h in range(3):
        row = jnp.full((1, 1024), table[0, h], f32)
        for b, first in enumerate(bucket_starts()):
            if b > 0:
                row = jnp.where(distance >= first, table[b, h], row)
        row = jnp.where(distance < 0, NEG_FILL, row)
        wide = jnp.broadcast_to(row, (BQ, 1024))
        bias_scr[h] = pltpu.roll(wide, 0, 1, stride=1, stride_axis=0)[:, :768]


def attend(scores, v_ref, keys, rows, live, ctx_ref, st_ref):
    s = [scores(h) for h in range(3)]
    m = [jnp.max(x, axis=1, keepdims=True) for x in s]
    e = [jnp.exp(x - y) for x, y in zip(s, m)]
    total = [jnp.sum(x, axis=1, keepdims=True) for x in e]
    p = [(x * (1.0 / y)).astype(bf16) for x, y in zip(e, total)]
    c = [dg(p[h], v_ref[keys, LANES[h]], NN) for h in range(3)]
    ctx_ref[rows, 0:128] = jnp.where(live, pair_of(c[0], c[1]), 0.0).astype(bf16)
    ctx_ref[rows, 128:192] = jnp.where(live, c[2], 0.0).astype(bf16)
    for h in range(3):
        st_ref[rows, h:h + 1] = m[h] + jnp.log(total[h])


def attend_back(scores, q_ref, k_ref, v_ref, g, keys, rows, st_ref, dq, dk, dv, extra):
    gs = [head_of(g[:, LANES[h]], h) for h in range(3)]
    s = [scores(h) for h in range(3)]
    wg = [dg(gs[h], v_ref[keys, LANES[h]], NT) for h in range(3)]
    p = [jnp.exp(s[h] - st_ref[rows, h:h + 1]) for h in range(3)]
    inner = [jnp.sum(p[h] * wg[h], axis=1, keepdims=True) for h in range(3)]
    sg = [(p[h] * (wg[h] - inner[h])).astype(bf16) for h in range(3)]
    p16 = [x.astype(bf16) for x in p]
    dvs = [dg(p16[h], gs[h], TN) for h in range(3)]
    dks = [dg(sg[h], head_of(q_ref[rows, LANES[h]], h), TN) for h in range(3)]
    dqs = [dg(sg[h], k_ref[keys, LANES[h]], NN) for h in range(3)]
    dv[keys, 0:128] += dvs[0] + dvs[1]
    dv[keys, 128:192] += dvs[2]
    dk[keys, 0:128] += dks[0] + dks[1]
    dk[keys, 128:192] += dks[2]
    dq[rows, 0:128] = pair_of(dqs[0], dqs[1]).astype(bf16)
    dq[rows, 128:192] = dqs[2].astype(bf16)
    extra(sg)


def self_scores(q_ref, k_ref, bias_scr, ds, q0, rows, keys, width):
    kpos = lax.broadcasted_iota(i32, (BQ, width), 1) + (q0 + BQ - width)
    shut = jnp.where(kpos >= ds, 0.0, NEG_FILL)
    return lambda h: dg(head_of(q_ref[rows, LANES[h]], h), k_ref[keys, LANES[h]], NT) + (
        bias_scr[h, :, 768 - width:] + shut)


def cross_scores(q_ref, k_ref, tseg, sseg, rows, keys):
    shut = jnp.where(tseg == sseg, 0.0, NEG_FILL)
    return lambda h: dg(head_of(q_ref[rows, LANES[h]], h), k_ref[keys, LANES[h]], NT) + shut


def project(n_ref, ws, *outs):
    for j, out in outs:
        out[...] = dg(n_ref[...], ws[j][...], NT).astype(bf16)


def self_attend(core, win, table, n_ref, ws, cols, before, ctx_ref, st_ref, om, ot, bias_scr, q, k, v, st):
    fill_bias(table, bias_scr)
    project(n_ref, ws, (0, q), (1, k), (2, v))

    def block(i):
        q0 = pl.multiple_of(i * BQ, BQ)
        rows = pl.ds(q0, BQ)

        @pl.when(win[i] == 0)
        def _():
            ctx_ref[rows, :] = jnp.zeros((BQ, 192), bf16)
            st[rows, :] = jnp.zeros((BQ, 8), f32)

        for n, width in enumerate(SELF_W):
            @pl.when(win[i] == n + 1)
            def _(width=width):
                keys = pl.ds(pl.multiple_of(q0 + (BQ - width), 128), width)
                ds = cols[rows, 0:1]
                attend(self_scores(q, k, bias_scr, ds, q0, rows, keys, width), v, keys, rows, ds < DEAD, ctx_ref, st)
    loop(SLOT // BQ, block)
    st_ref[...] = jnp.transpose(st[...])
    out_split(core[0], om, ot, before, lambda c: dg(half_rows(ctx_ref, c), ws[3][...], NN))


def self_fwd_first_kernel(core, win, table, mine_in, theirs_in, wq, wkv, wo, seg, n_ref, ctx, st, om, ot, cols, *scr):
    cols[...] = jnp.transpose(seg[...])
    join_rows(core[0], mine_in, theirs_in, n_ref)
    self_attend(core, win, table, n_ref, own_weights(0, wq, wkv, wo), cols, None, ctx, st, om, ot, *scr)


def self_fwd_second_kernel(core, win, table, bits, n_ref, bm, bt, pair, wy, wz, seg, w_ref, ctx, st, om, ot, cols,
                           *scr):
    cols[...] = jnp.transpose(seg[...])
    join_quarters(bits, pair, wy, wz, w_ref)
    self_attend(core, win, table, n_ref, away_weights(w_ref), cols, (bm, bt), ctx, st, om, ot, *scr)


HALF32 = sd((SLOT // 2, 768), f32)
ATT = [sd((SLOT, 192), bf16), sd((8, SLOT), f32)]
STACK = sd((768, 768), bf16)
WIDE16, WIDE32 = pltpu.VMEM((SLOT, 192), bf16), pltpu.VMEM((SLOT, 192), f32)
MEM16, MEM32 = pltpu.VMEM((MEM, 192), bf16), pltpu.VMEM((MEM, 192), f32)
BIAS = pltpu.VMEM((3, BQ, 768), f32)
COLS, STATS = pltpu.VMEM((SLOT, 8), i32), pltpu.VMEM((SLOT, 8), f32)


def self_fwd_first(core, win, table, mine, theirs, weights, seg):
    return call(self_fwd_first_kernel, "self_fwd", (core, win, table, mine, theirs) + weights + (seg,),
                [sd((SLOT, 768), bf16)] + ATT + [HALF32, HALF32], [COLS, BIAS, WIDE16, WIDE16, WIDE16, STATS], 3, vmem=14)


def self_fwd_second(core, win, table, bits, n, bm, bt, parts, seg):
    return call(self_fwd_second_kernel, "self_fwd", (core, win, table, bits, n, bm, bt) + tuple(parts) + (seg,),
                [STACK] + ATT + [HALF32, HALF32], [COLS, BIAS, WIDE16, WIDE16, WIDE16, STATS], 4, vmem=14)


def diagonal_sums(scr, h):
    span = scr.shape[2]
    slabs = [scr[h, 8 * a:8 * a + 8, :] for a in range(BQ // 8)]
    step = 8
    while len(slabs) > 1:
        slabs = [slabs[j] + pltpu.roll(slabs[j + 1], span - step, 1) for j in range(0, len(slabs), 2)]
        step *= 2
    acc = slabs[0]
    row = lax.broadcasted_iota(i32, acc.shape, 0)
    for bit in (1, 2, 4):
        acc = jnp.where((row & bit) > 0, pltpu.roll(acc, span - bit, 1), acc)
    return jnp.sum(acc, axis=0, keepdims=True)


def weight_grads(dq, dk16, dv16, nq_ref, nk_ref, b_ref, ctx_ref, a_ref, put_late):
    a_ref[0:192, :] = dg(dq[...], nq_ref[...], TN).astype(bf16)
    a_ref[192:384, :] = dg(dk16[...], nk_ref[...], TN).astype(bf16)
    put_late(0, dg(dv16[...], nk_ref[...], TN).astype(bf16))
    put_late(1, dg(ctx_ref[...], b_ref[...], TN).astype(bf16))


def put_plain(ref, rows):
    def put(half, value):
        ref[rows * half:rows * half + rows, :] = value
    return put


def self_bwd_core(core, win, table, b_ref, n_ref, ws, seg, ctx_ref, st_ref, before, a_ref, put, om, ot, db_ref,
                  cols, st, bias_scr, dbias_scr, q, k, v, g_scr, dq, dk, dv, dk16, dv16):
    cols[...] = jnp.transpose(seg[...])
    st[...] = jnp.transpose(st_ref[...])
    fill_bias(table, bias_scr)
    project(n_ref, ws, (0, q), (1, k), (2, v))
    dbias_scr[...] = jnp.zeros(dbias_scr.shape, f32)
    dk[...] = jnp.zeros(dk.shape, f32)
    dv[...] = jnp.zeros(dv.shape, f32)
    g = dg(b_ref[...], ws[3][...], NT).astype(bf16)
    g_scr[...] = jnp.where(cols[:, 0:1] < DEAD, g, jnp.zeros_like(g))

    def block(i):
        q0 = pl.multiple_of(i * BQ, BQ)
        rows = pl.ds(q0, BQ)

        @pl.when(win[i] == 0)
        def _():
            dq[rows, :] = jnp.zeros((BQ, 192), bf16)

        for n, width in enumerate(SELF_W):
            @pl.when(win[i] == n + 1)
            def _(width=width):
                keys = pl.ds(pl.multiple_of(q0 + (BQ - width), 128), width)

                def extra(sg):
                    for h in range(3):
                        dbias_scr[h, :, 768 - width:768] += sg[h].astype(f32)
                attend_back(self_scores(q, k, bias_scr, cols[rows, 0:1], q0, rows, keys, width),
                            q, k, v, g_scr[rows, :], keys, rows, st, dq, dk, dv, extra)
    loop(SLOT // BQ, block)
    dk16[...] = dk[...].astype(bf16)
    dv16[...] = dv[...].astype(bf16)
    weight_grads(dq, dk16, dv16, n_ref, n_ref, b_ref, ctx_ref, a_ref, put)
    out_split(core[0], om, ot, before, lambda c: dg(half_rows(dq, c), ws[0][...], NN)
              + dg(half_rows(dk16, c), ws[1][...], NN) + dg(half_rows(dv16, c), ws[2][...], NN))
    for h in range(3):
        db_ref[h:h + 1, :] = diagonal_sums(dbias_scr, h)


SELF_BWD_SCRATCH = ([COLS, STATS, BIAS, pltpu.VMEM((3, BQ, 1024), f32)] + [WIDE16] * 5
                    + [WIDE32, WIDE32, WIDE16, WIDE16])
PART = sd((384, 768), bf16)


def self_bwd_first_kernel(core, win, table, mine_in, theirs_in, n_ref, w_ref, seg, ctx, st, b_ref, a_ref, late_ref,
                          om, ot, db_ref, *scr):
    join_rows(core[0], mine_in, theirs_in, b_ref)
    self_bwd_core(core, win, table, b_ref, n_ref, away_weights(w_ref), seg, ctx, st, None, a_ref, put_plain(late_ref, 192),
                  om, ot, db_ref, *scr)


def self_bwd_second_kernel(core, win, table, b_ref, bm, bt, n_ref, wq, wkv, wo, seg, ctx, st, a_ref, late_ref, om, ot,
                           db_ref, *scr):
    self_bwd_core(core, win, table, b_ref, n_ref, own_weights(0, wq, wkv, wo), seg, ctx, st, (bm, bt), a_ref,
                  put_plain(late_ref, 192), om, ot, db_ref, *scr)


def self_bwd_first(core, win, table, mine, theirs, n, w, seg, ctx, st):
    return call(self_bwd_first_kernel, "self_bwd", (core, win, table, mine, theirs, n, w, seg, ctx, st),
                [sd((SLOT, 768), bf16), PART, PART, HALF32, HALF32, sd((3, 1024), f32)], SELF_BWD_SCRATCH, 3, vmem=28)


def self_bwd_second(core, win, table, b, bm, bt, n, weights, seg, ctx, st):
    return call(self_bwd_second_kernel, "self_bwd", (core, win, table, b, bm, bt, n) + weights + (seg, ctx, st),
                [PART, PART, HALF32, HALF32, sd((3, 1024), f32)], SELF_BWD_SCRATCH, 3, vmem=28)


def cross_fwd_kernel(core, win, bits, mine_in, theirs_in, mem_mine, mem_theirs, wq, wkv, wo, pair, wy, wz, seg,
                     sseg_ref, n_ref, m_ref, w_ref, ctx0, st0, ctx1, st1, om, ot, cols, q, k, v, st):
    cols[...] = jnp.transpose(seg[...])
    join_rows(core[0], mine_in, theirs_in, n_ref)
    join_rows(core[0], mem_mine, mem_theirs, m_ref)
    join_quarters(bits, pair, wy, wz, w_ref)
    own, away = own_weights(1, wq, wkv, wo), away_weights(w_ref)
    for ws, ctx_ref, st_ref in ((own, ctx0, st0), (away, ctx1, st1)):
        project(n_ref, ws, (0, q))
        project(m_ref, ws, (1, k), (2, v))

        def block(i, ctx_ref=ctx_ref):
            rows = blk(i)

            @pl.when(win[0, i] == 0)
            def _():
                ctx_ref[rows, :] = jnp.zeros((BQ, 192), bf16)
                st[rows, :] = jnp.zeros((BQ, 8), f32)

            for n, width in enumerate(CROSS_W):
                @pl.when(win[0, i] == n + 1)
                def _(width=width):
                    keys = pl.ds(pl.multiple_of(win[1, i], 128), width)
                    tseg, sseg = cols[rows, 1:2], sseg_ref[:, keys]
                    attend(cross_scores(q, k, tseg, sseg, rows, keys), v, keys, rows, tseg > 0, ctx_ref, st)
        loop(SLOT // BQ, block)
        st_ref[...] = jnp.transpose(st[...])
    out_split(core[0], om, ot, None, lambda c: dg(half_rows(ctx0, c), own[3][...], NN)
              + dg(half_rows(ctx1, c), away[3][...], NN))


def cross_fwd(core, win, bits, mine, theirs, mem_mine, mem_theirs, weights, parts, seg, sseg):
    return call(cross_fwd_kernel, "cross_fwd",
                (core, win, bits, mine, theirs, mem_mine, mem_theirs) + weights + tuple(parts) + (seg, sseg),
                [sd((SLOT, 768), bf16), sd((MEM, 768), bf16), STACK] + ATT + ATT + [HALF32, HALF32],
                [COLS, WIDE16, MEM16, MEM16, STATS], 3, vmem=12)


def cross_bwd_core(core, win, b_ref, n_ref, m_ref, ws, seg, sseg_ref, ctx_ref, st_ref, before, mem_before, a_ref, put,
                   om, ot, mm, mt, cols, st, q, k, v, g_scr, dq, dk, dv, dk16, dv16):
    cols[...] = jnp.transpose(seg[...])
    st[...] = jnp.transpose(st_ref[...])
    project(n_ref, ws, (0, q))
    project(m_ref, ws, (1, k), (2, v))
    dk[...] = jnp.zeros(dk.shape, f32)
    dv[...] = jnp.zeros(dv.shape, f32)
    g = dg(b_ref[...], ws[3][...], NT).astype(bf16)
    g_scr[...] = jnp.where(cols[:, 1:2] > 0, g, jnp.zeros_like(g))

    def block(i):
        rows = blk(i)

        @pl.when(win[0, i] == 0)
        def _():
            dq[rows, :] = jnp.zeros((BQ, 192), bf16)

        for n, width in enumerate(CROSS_W):
            @pl.when(win[0, i] == n + 1)
            def _(width=width):
                keys = pl.ds(pl.multiple_of(win[1, i], 128), width)
                attend_back(cross_scores(q, k, cols[rows, 1:2], sseg_ref[:, keys], rows, keys),
                            q, k, v, g_scr[rows, :], keys, rows, st, dq, dk, dv, lambda sg: None)
    loop(SLOT // BQ, block)
    dk16[...] = dk[...].astype(bf16)
    dv16[...] = dv[...].astype(bf16)
    weight_grads(dq, dk16, dv16, n_ref, m_ref, b_ref, ctx_ref, a_ref, put)
    out_split(core[0], om, ot, before, lambda c: dg(half_rows(dq, c), ws[0][...], NN))
    out_split(core[0], mm, mt, mem_before, lambda c: dg(half_rows(dk16, c), ws[1][...], NN)
              + dg(half_rows(dv16, c), ws[2][...], NN))


CROSS_BWD_SCRATCH = [COLS, STATS, WIDE16, MEM16, MEM16, WIDE16, WIDE16, MEM32, MEM32, MEM16, MEM16]
HALFMEM = sd((MEM // 2, 768), f32)


def cross_bwd_first_kernel(core, win, mine_in, theirs_in, n_ref, m_ref, w_ref, seg, sseg, ctx, st, b_ref, a_ref, late_ref,
                           om, ot, mm, mt, *scr):
    join_rows(core[0], mine_in, theirs_in, b_ref)
    cross_bwd_core(core, win, b_ref, n_ref, m_ref, away_weights(w_ref), seg, sseg, ctx, st, None, None, a_ref,
                   put_plain(late_ref, 192), om, ot, mm, mt, *scr)


def cross_bwd_second_kernel(core, win, b_ref, bm, bt, cm, ct, n_ref, m_ref, wq, wkv, wo, seg, sseg, ctx, st,
                            a_ref, late_ref, om, ot, mm, mt, *scr):
    cross_bwd_core(core, win, b_ref, n_ref, m_ref, own_weights(1, wq, wkv, wo), seg, sseg, ctx, st, (bm, bt), (cm, ct),
                   a_ref, put_plain(late_ref, 192), om, ot, mm, mt, *scr)


def cross_bwd_first(core, win, mine, theirs, n, mem, w, seg, sseg, ctx, st):
    return call(cross_bwd_first_kernel, "cross_bwd", (core, win, mine, theirs, n, mem, w, seg, sseg, ctx, st),
                [sd((SLOT, 768), bf16), PART, PART, HALF32, HALF32, HALFMEM, HALFMEM], CROSS_BWD_SCRATCH, 2, vmem=18)


def cross_bwd_second(core, win, b, before, n, mem, weights, seg, sseg, ctx, st):
    return call(cross_bwd_second_kernel, "cross_bwd",
                (core, win, b) + tuple(before) + (n, mem) + weights + (seg, sseg, ctx, st),
                [PART, PART, HALF32, HALF32, HALFMEM, HALFMEM], CROSS_BWD_SCRATCH, 2, vmem=18)


GELU_C = math.sqrt(2.0 / math.pi)


def ffn_rows(n_ref, c_ref, wg, wu, wo, o_ref, t_ref, before, h_ref, g_ref, u_ref, base):
    def block(i):
        rows = slice(i * BQ, i * BQ + BQ)
        keep = slice(base + i * BQ, base + i * BQ + BQ)
        n = n_ref[rows, :]
        gate, up = dg(n, wg[...], NN), dg(n, wu[...], NN)
        hid = dg(c_ref[rows, :], wo[...], NT)
        square = gate * gate
        th = jnp.tanh(GELU_C * (gate + 0.044715 * (gate * square)))
        half = 0.5 * (1.0 + th)
        gelu = gate * half
        slope = half + (0.5 * GELU_C) * gate * (1.0 - th * th) * (1.0 + (3 * 0.044715) * square)
        h = (gelu * up).astype(bf16)
        gg = (hid * up * slope).astype(bf16)
        ug = (hid * gelu).astype(bf16)
        h_ref[keep, :], g_ref[keep, :], u_ref[keep, :] = h, gg, ug
        out = dg(h, wo[...], NN)
        third = dg(gg, wg[...], NT) + dg(ug, wu[...], NT)
        if before is not None:
            out, third = out + before[0][rows, :], third + before[1][rows, :]
        o_ref[rows, :], t_ref[rows, :] = out, third
    for i in range(n_ref.shape[0] // BQ):
        block(i)


def ffn_core(bits, na, nb, ca, cb, wg, wu, wo, before_a, before_b, outs, h_ref, g_ref, u_ref, dw):
    oa, ob, ta, tb, x_ref, y_keep, y_give, z_keep, z_give = outs
    half = na.shape[0]
    ffn_rows(na, ca, wg, wu, wo, oa, ta, before_a, h_ref, g_ref, u_ref, 0)
    ffn_rows(nb, cb, wg, wu, wo, ob, tb, before_b, h_ref, g_ref, u_ref, half)
    for j, (left, ra, rb) in enumerate(((g_ref, na, nb), (u_ref, na, nb), (h_ref, ca, cb))):
        dw[512 * j:512 * j + 512, :] = (dg(left[0:half, :], ra[...], TN) + dg(left[half:2 * half, :], rb[...], TN)).astype(
            bf16)
    x_ref[...] = dw[0:384, :]
    for base, bit, keep, give in ((384, bits[0], y_keep, y_give), (960, bits[1], z_keep, z_give)):
        keep[...] = dw[pl.ds(pl.multiple_of(base + bit * 288, 16), 288), :]
        give[...] = dw[pl.ds(pl.multiple_of(base + (1 - bit) * 288, 16), 288), :]


def ffn_away_kernel(bits, na, nb, ca, cb, f0, fy, fz, f3, *refs):
    w2, wo = refs[-2:]
    for step, part in enumerate((f0, fy, fz, f3)):
        y, z = quarter_of(bits, step)
        w2[y, pl.ds(pl.multiple_of(z * 384, 128), 384), :] = part[0:384, :]
        at = pl.multiple_of((2 * y + z) * 128, 128)
        wo[pl.ds(at, 128), 0:512] = part[384:512, :]
        wo[pl.ds(at, 64), 512:768] = part[512:576, 0:256]
        wo[pl.ds(pl.multiple_of(at + 64, 64), 64), 512:768] = part[512:576, 256:512]
    ffn_core(bits, na, nb, ca, cb, w2.at[0], w2.at[1], wo, None, None, refs[:9], *refs[9:13])


def ffn_own_kernel(bits, na, nb, ca, cb, wi, wo, pa, pb, sa, sb, *refs):
    ffn_core(bits, na, nb, ca, cb, wi.at[0], wi.at[1], wo, (pa, sa), (pb, sb), refs[:9], *refs[9:13])


def ffn_outs(rows):
    return [sd((rows, 768), f32)] * 4 + [sd((384, 768), bf16)] + [sd((288, 768), bf16)] * 4


def ffn_scratch(rows, units):
    return [pltpu.VMEM((2 * rows, units), bf16)] * 3 + [pltpu.VMEM((3 * units, 768), bf16)]


def ffn_away(bits, na, nb, ca, cb, weights):
    rows, units = na.shape[0], weights[0].shape[1]
    scratch = ffn_scratch(rows, units) + [pltpu.VMEM((2, 768, units), bf16), pltpu.VMEM((units, 768), bf16)]
    return call(ffn_away_kernel, "ffn_away", (bits, na, nb, ca, cb) + tuple(weights), ffn_outs(rows), scratch, 1, vmem=22)


def ffn_own(bits, na, nb, ca, cb, wi, wo, before):
    rows, units = na.shape[0], wo.shape[0]
    return call(ffn_own_kernel, "ffn_own", (bits, na, nb, ca, cb, wi, wo) + tuple(before), ffn_outs(rows),
                ffn_scratch(rows, units), 1, vmem=20)


def merge_kernel(actions, outs):
    def kernel(bits, *refs):
        ins, dest = refs[:len(refs) - outs], refs[len(refs) - outs:]

        def total(terms, extra, count):
            value = None
            for src, at in terms:
                part = ins[src][pl.ds(pl.multiple_of(at + extra, 16), count), :].astype(f32)
                value = part if value is None else value + part
            return value.astype(bf16)

        for action in actions:
            if action[0] == "split":
                _, terms, count, bit, (keep, kat), (give, gat) = action
                half = count // 2
                dest[keep][kat:kat + half, :] = total(terms, bits[bit] * half, half)
                dest[give][gat:gat + half, :] = total(terms, (1 - bits[bit]) * half, half)
            elif action[0] == "sum":
                _, terms, count, (out, at) = action
                dest[out][at:at + count, :] = total(terms, 0, count)
            else:
                _, (own, own_at), (other, other_at), count, bit, (out, at) = action
                dest[out][pl.ds(pl.multiple_of(at + bits[bit] * count, 16), count), :] = ins[own][own_at:own_at + count, :]
                dest[out][pl.ds(pl.multiple_of(at + (1 - bits[bit]) * count, 16), count), :] = (
                    ins[other][other_at:other_at + count, :])
    return kernel


def merge(bits, ins, actions, sizes):
    outs = [sd((rows, 768), bf16) for rows in sizes]
    return call(merge_kernel(actions, len(outs)), "merge", (bits,) + tuple(ins), outs, (), 1, vmem=16)


def ffn_finish_kernel(bits, fin, y_in, z_in, gi, go, model, unit, scr):
    for base, half, bit, own, other in ((0, 192, bits[0], fin[0:192, :], y_in[0:192, :]),
                                        (384, 288, bits[0], fin[192:480, :], y_in[192:480, :]),
                                        (960, 288, bits[1], fin[480:768, :], z_in[...])):
        scr[pl.ds(pl.multiple_of(base + bit * half, 16), half), :] = own
        scr[pl.ds(pl.multiple_of(base + (1 - bit) * half, 16), half), :] = other
    for j in range(3):
        g = scr[512 * j:512 * j + 512, :].astype(f32)
        if j < 2:
            gi[j] = jnp.transpose(g)
        else:
            go[...] = g
        sq = g * g
        model[j:j + 1, :] = jnp.sum(sq, axis=0, keepdims=True)
        unit[j:j + 1, :] = jnp.transpose(jnp.sum(sq, axis=1, keepdims=True)) * (1.0 / D)


def ffn_finish(bits, fin, y_in, z_in):
    units = 512
    return call(ffn_finish_kernel, "ffn_finish", (bits, fin, y_in, z_in),
                [sd((2, 768, units), f32), sd((units, 768), f32), sd((3, 768), f32), sd((3, units), f32)],
                [pltpu.VMEM((3 * units, 768), bf16)], 1, vmem=20)


def finish_part(a, bits, fin, y_in, z_in, put, model, head, proj, rows, scr):
    for base, bit, own, other in ((0, bits[1], fin[0:192, :], z_in), (384, bits[0], fin[192:384, :], y_in)):
        scr[pl.ds(pl.multiple_of(base + bit * 192, 16), 192), :] = own
        scr[pl.ds(pl.multiple_of(base + (1 - bit) * 192, 16), 192), :] = other[...]
    for j in range(4):
        w = scr[192 * j:192 * j + 192, :].astype(f32)
        put(j, w)
        sq = w * w
        model[rows[j]:rows[j] + 1, :] = jnp.sum(sq, axis=0, keepdims=True)
        side = jnp.transpose(jnp.sum(sq, axis=1, keepdims=True)) * (1.0 / D)
        if j < 3:
            head[rows[j]:rows[j] + 1, :] = side
        else:
            proj[a:a + 1, :] = side


def early_kernel(bits, c_fin, c_y, c_z, fm_ref, qg, kvg, og, model, head, proj, scr):
    def put(j, w):
        if j == 0:
            qg[0] = w
        elif j == 3:
            og[0] = w
        else:
            kvg[0, j - 1] = w
    model[...] = jnp.zeros(model.shape, f32)
    head[...] = jnp.zeros(head.shape, f32)
    proj[...] = jnp.zeros(proj.shape, f32)
    finish_part(1, bits, c_fin, c_y, c_z, put, model, head, proj, (1, 4, 5, 9), scr)
    model[6:8, :] = fm_ref[0:2, :]
    model[10:11, :] = fm_ref[2:3, :]


def late_kernel(bits, s_fin, s_y, s_z, model_in, head_in, proj_in, _q, _kv, _o, qg, kvg, og, model, head, proj, scr):
    def put(j, w):
        if j == 0:
            qg[0] = w
        elif j == 3:
            og[0] = w
        else:
            kvg[0, j - 1] = w
    model[...] = model_in[...]
    head[...] = head_in[...]
    proj[...] = proj_in[...]
    finish_part(0, bits, s_fin, s_y, s_z, put, model, head, proj, (0, 2, 3, 8), scr)


def finish_call(kernel, layer, args, extra, aliases):
    def whole(a):
        return pl.BlockSpec(a.shape, lambda i, bits, n=len(a.shape): (0,) * n)
    outs = [sd((2, 192, 768), f32), sd((2, 2, 192, 768), f32), sd((2, 192, 768), f32), sd((11, 768), f32),
            sd((6, 192), f32), sd((2, 192), f32)]
    one = pl.BlockSpec((1, 192, 768), lambda i, bits: (layer, 0, 0))
    pair = pl.BlockSpec((1, 2, 192, 768), lambda i, bits: (layer, 0, 0, 0))
    return pl.pallas_call(
        kernel,
        grid_spec=pltpu.PrefetchScalarGridSpec(
            num_scalar_prefetch=1, grid=(1,),
            in_specs=[whole(a) for a in args[1:]] + [pl.BlockSpec(memory_space=pl.ANY)] * len(extra),
            out_specs=[one, pair, one] + [whole(a) for a in outs[3:]],
            scratch_shapes=[pltpu.VMEM((768, 768), bf16)]),
        out_shape=outs,
        input_output_aliases=aliases,
        name="finish",
        compiler_params=pltpu.CompilerParams(vmem_limit_bytes=16 << 20),
        cost_estimate=pl.CostEstimate(flops=0, bytes_accessed=4000000, transcendentals=0))(*args, *extra)


def finish_early(bits, cross_parts, ffn_model):
    return finish_call(early_kernel, 1, (bits,) + tuple(cross_parts) + (ffn_model,), (), {})


def finish_late(bits, self_parts, early):
    return finish_call(late_kernel, 0, (bits,) + tuple(self_parts) + tuple(early[3:]), tuple(early[:3]),
                       {7: 0, 8: 1, 9: 2})


CORE = [(i, i ^ 1) for i in range(4)]
CHIP = [(i, i ^ 2) for i in range(4)]


def swap_core(v):
    return lax.ppermute(v, "tensor", CORE)


def swap_chip(v):
    return lax.ppermute(v, "tensor", CHIP)


def swap_dp(v, bit):
    return lax.ppermute(v, "dp", [(i, i ^ (1 << bit)) for i in range(lax.axis_size("dp"))])


def dp_bits():
    return int(math.log2(lax.axis_size("dp")))


def after(value, *earlier):
    return lax.optimization_barrier((value,) + earlier)[0]


def sync(*values):
    return lax.optimization_barrier(values)


def over_group(v):
    diagonal = lax.ppermute(v, "tensor", [(i, i ^ 3) for i in range(4)])
    return (v + swap_core(v)) + (swap_chip(v) + diagonal)


def over_first_bits(v):
    diagonal = lax.ppermute(v, "dp", [(i, i ^ 3) for i in range(lax.axis_size("dp"))])
    return (v + swap_dp(v, 0)) + (swap_dp(v, 1) + diagonal)


def past(value, bit):
    for one in range(bit, dp_bits()):
        value = (value.astype(f32) + swap_dp(value, one).astype(f32)).astype(bf16)
    return value


def bucket_sums(lane_sums):
    lane = np.arange(1024)
    distance = 512 - np.where(lane < 768, lane, lane - 1024)
    buckets = jnp.asarray(np.array([bucket_of(max(int(n), 0)) for n in distance], np.int32))
    onehot = (buckets[:, None] == jnp.arange(BUCKETS)[None, :]) & jnp.asarray(distance >= 0)[:, None]
    return lax.dot_general(onehot.astype(f32), lane_sums, (((0,), (1,)), ((), ())), precision=lax.Precision.HIGHEST,
                           preferred_element_type=f32)


def on_device(tokens, memory, cotangent, norm_gains, query_weight, keyvalue_weight, output_weight, bias_table,
              inner_weight, outer_weight, target_lengths, source_lengths):
    t, d = lax.axis_index("tensor"), lax.axis_index("dp")
    core = (t & 1).reshape(1).astype(i32)
    slot = lax.shift_right_logical(t, 1).reshape(1).astype(i32)
    bits = (lax.shift_right_logical(d, jnp.arange(3)) & 1).astype(i32)
    weights = (jnp.swapaxes(query_weight, 1, 2), jnp.swapaxes(keyvalue_weight, 2, 3), output_weight)

    table_away = swap_chip(bias_table)
    q_self = weight_quarters(bits, 0, *weights)
    table_away, q_self, tokens, bits2 = sync(table_away, q_self, tokens, bits)
    s0 = swap_chip(q_self)
    q_cross = weight_quarters(bits2, 1, *weights)
    n1m = norm_rows(tokens, norm_gains)
    n1t = swap_core(n1m)
    seg, sseg, swin, cwin = slot_layout(slot, target_lengths, source_lengths)
    n1, ctx_s0, st_s0, pm, pt = self_fwd_first(core, swin, bias_table, n1m, n1t, weights, seg)
    s0, n1, q_cross, memory, cotangent = sync(s0, n1, q_cross, memory, cotangent)
    sy, sz = swap_dp(s0[:192], 0), swap_dp(s0[:192], 1)
    c0 = swap_chip(q_cross)
    mem_t, cot_t = swap_core(memory), swap_core(cotangent)
    fq0, fq3 = packed(bits, inner_weight, outer_weight)
    sy, sz, n1, fq0, fq3, c0 = sync(sy, sz, n1, fq0, fq3, c0)
    f0 = swap_chip(fq0)
    cy, cz = swap_dp(c0[:192], 0), swap_dp(c0[:192], 1)
    w_self_away, ctx_s1, st_s1, pm, pt = self_fwd_second(core, swin, table_away, bits, n1, pm, pt, (s0, sy, sz), seg)
    f0, cy, cz, pm, pt, fq3 = sync(f0, cy, cz, pm, pt, fq3)
    f3 = swap_chip(fq3)
    fy, fz = swap_dp(f0, 0), swap_dp(f0, 1)
    after_self, n2m = add_norm(tokens, pm, swap_core(pt), norm_gains, 1)

    n2, mem, w_cross_away, ctx_c0, st_c0, ctx_c1, st_c1, pm, pt = cross_fwd(
        core, cwin, bits, n2m, swap_core(n2m), memory, mem_t, weights, (c0, cy, cz), seg, sseg)
    f3, fy, fz, pm, pt = sync(f3, fy, fz, pm, pt)
    after_cross, n3m = add_norm(after_self, pm, swap_core(pt), norm_gains, 2)

    n3t = swap_core(n3m)
    oa, ob, ta, tb, px, pyk, pyg, pzk, pzg = ffn_away(bits, n3m, n3t, cotangent, cot_t, (f0, fy, fz, f3))
    n3m, px, pyg, pzg = sync(n3m, px, pyg, pzg)
    xi, yi, zi = swap_chip(px), swap_dp(pyg, 0), swap_dp(pzg, 1)
    oa, ob, ta, tb, ox, oyk, oyg, ozk, ozg = ffn_own(bits, n3m, n3t, cotangent, cot_t, inner_weight, outer_weight,
                                                     (oa, ob, ta, tb))
    xi, yi, zi, oa, ob, ta, tb, ox, oyg, ozg = sync(xi, yi, zi, oa, ob, ta, tb, ox, oyg, ozg)
    fx_k, xp, yp = merge(
        bits, (ox, xi, pyk, yi, pzk, zi, oyg),
        (("split", ((0, 0), (1, 0)), 384, 0, (0, 0), (2, 0)),
         ("sum", ((2, 0), (3, 0)), 288, (1, 0)),
         ("sum", ((4, 0), (5, 0)), 288, (1, 288)),
         ("sum", ((6, 0),), 288, (2, 192))), (192, 576, 480))
    xi, yi, zi = swap_chip(xp), swap_dp(yp, 0), swap_dp(ozg, 1)
    cross_out_m, branch_m, gain2 = norm_back(after_cross, norm_gains, 2, cotangent, ta, swap_core(tb))

    branch, c_out, c_late, pm, pt, mm, mt = cross_bwd_first(core, cwin, branch_m, swap_core(branch_m), n2, mem,
                                                            w_cross_away, seg, sseg, ctx_c1, st_c1)
    xi, yi, zi, branch, c_out, c_late, pm, pt, mm, mt = sync(xi, yi, zi, branch, c_out, c_late, pm, pt, mm, mt)
    fx_k, fy_k, fz_k, cb_k, yp, zp = merge(
        bits, (fx_k, yi, oyk, xi, ozk, zi, c_late),
        (("split", ((0, 0), (1, 0)), 192, 1, (0, 0), (5, 0)),
         ("split", ((2, 0), (1, 192), (3, 0)), 288, 1, (1, 0), (5, 96)),
         ("split", ((4, 0), (5, 0), (3, 288)), 288, 0, (2, 0), (4, 0)),
         ("split", ((6, 0),), 384, 0, (3, 0), (4, 144))), (96, 144, 144, 192, 336, 240))
    xi, yi, zi = swap_chip(c_out), swap_dp(yp, 0), swap_dp(zp, 1)
    branch, zp = sync(branch, zp)
    c_a, c_own, pm, pt, mm, mt = cross_bwd_second(core, cwin, branch, (pm, pt, mm, mt), n2, mem, weights, seg, sseg,
                                                  ctx_c0, st_c0)
    xi, yi, zi, c_a, c_own, pm, pt, mm, mt = sync(xi, yi, zi, c_a, c_own, pm, pt, mm, mt)
    f_mid, ca_k, cb_o, xp, yp, zp = merge(
        bits, (fx_k, zi, fy_k, fz_k, yi, c_a, xi, cb_k, c_own),
        (("sum", ((0, 0), (1, 0)), 96, (0, 0)),
         ("sum", ((2, 0), (1, 96)), 144, (0, 96)),
         ("sum", ((3, 0), (4, 0)), 144, (0, 240)),
         ("split", ((5, 0), (6, 0)), 384, 1, (1, 0), (5, 0)),
         ("sum", ((7, 0), (4, 144)), 192, (3, 0)),
         ("split", ((8, 0),), 384, 0, (2, 0), (4, 0))), (384, 192, 192, 192, 192, 192))
    pt, f_mid, xp, yp, zp = sync(pt, f_mid, xp, yp, zp)
    xi, yi, zi, z2i = swap_chip(xp), swap_dp(yp, 0), swap_dp(zp, 1), swap_dp(f_mid, 2)
    self_out_m, branch_m, gain1 = norm_back(after_self, norm_gains, 1, cross_out_m, pm, swap_core(pt))

    branch, s_out, s_late, pm, pt, lanes_away = self_bwd_first(core, swin, table_away, branch_m, swap_core(branch_m), n1,
                                                               w_self_away, seg, ctx_s1, st_s1)
    z2i, xi, yi, zi, branch, s_out, s_late, pm, pt = sync(z2i, xi, yi, zi, branch, s_out, s_late, pm, pt)
    f_own, ca_k, cb_k, sb_k, yp, zp = merge(
        bits, (f_mid, z2i, ca_k, zi, cb_o, yi, xi, s_late),
        (("sum", ((0, 0), (1, 0)), 384, (0, 0)),
         ("sum", ((0, 0), (1, 0)), 240, (5, 0)),
         ("sum", ((0, 240), (1, 240)), 144, (4, 0)),
         ("split", ((2, 0), (3, 0)), 192, 0, (1, 0), (4, 144)),
         ("split", ((4, 0), (5, 0), (6, 0)), 192, 1, (2, 0), (5, 240)),
         ("split", ((7, 0),), 384, 0, (3, 0), (4, 240))), (384, 96, 96, 192, 432, 336))
    if dp_bits() > 3:
        f_own = past(f_own, 3)
        yp, zp = jnp.concatenate((f_own[240:], yp[144:])), jnp.concatenate((f_own[:240], zp[240:]))
    xi, yi, zi = swap_chip(s_out), swap_dp(yp, 0), swap_dp(zp, 1)
    branch, zp = sync(branch, zp)
    s_a, s_own, pm, pt, lanes_own = self_bwd_second(core, swin, bias_table, branch, pm, pt, n1, weights, seg, ctx_s0, st_s0)
    xi, yi, zi, s_a, s_own, pm, pt, lanes_own = sync(xi, yi, zi, s_a, s_own, pm, pt, lanes_own)

    f_fin, c_mid, sa_k, sb_o, xp, yp, zp = merge(
        bits, (f_own, zi, yi, ca_k, cb_k, s_a, xi, sb_k, s_own),
        (("join", (0, 0), (1, 0), 96, 1, (0, 0)),
         ("join", (0, 96), (1, 96), 144, 1, (0, 192)),
         ("join", (0, 240), (2, 0), 144, 0, (0, 480)),
         ("join", (0, 0), (1, 0), 96, 1, (5, 0)),
         ("join", (0, 96), (1, 96), 144, 1, (5, 192)),
         ("join", (0, 240), (2, 0), 144, 0, (6, 0)),
         ("sum", ((3, 0), (2, 144)), 96, (1, 0)),
         ("sum", ((4, 0), (1, 240)), 96, (1, 96)),
         ("split", ((5, 0), (6, 0)), 384, 1, (2, 0), (6, 288)),
         ("sum", ((7, 0), (2, 240)), 192, (4, 0)),
         ("split", ((8, 0),), 384, 0, (3, 0), (5, 480))), (768, 192, 192, 192, 192, 672, 480))
    pt_in, mt_in, ob_in = swap_core(pt), swap_core(mt), swap_core(ob)
    xi, yi, zi, z2i = swap_chip(xp), swap_dp(yp, 0), swap_dp(zp, 1), swap_dp(c_mid, 2)
    z2i, xi, yi, zi, pt_in, mt_in, ob_in, lanes_away = sync(z2i, xi, yi, zi, pt_in, mt_in, ob_in, lanes_away)
    c_own, sa_k, sb_k, yp, zp = merge(
        bits, (c_mid, z2i, sa_k, zi, sb_o, yi, xi),
        (("sum", ((0, 0), (1, 0)), 192, (0, 0)),
         ("sum", ((0, 0), (1, 0)), 96, (3, 0)),
         ("sum", ((0, 96), (1, 96)), 96, (4, 0)),
         ("split", ((2, 0), (3, 288)), 192, 0, (1, 0), (3, 96)),
         ("split", ((4, 0), (5, 480), (6, 0)), 192, 1, (2, 0), (4, 96))), (192, 96, 96, 192, 192))
    f_y, f_z = yi[:480], zi[:288]
    if dp_bits() > 3:
        c_own = past(c_own, 3)
        yp, zp = jnp.concatenate((c_own[:96], yp[96:])), jnp.concatenate((c_own[96:], zp[96:]))
    yi, zi = swap_dp(yp, 0), swap_dp(zp, 1)
    tokens_grad, _, gain0 = norm_back(tokens, norm_gains, 0, self_out_m, pm, pt_in)
    small = jnp.concatenate((gain0, gain1, gain2))
    memory_grad = mm + mt_in
    output_rows = (after_cross + (oa + ob_in)).astype(bf16)
    yi, zi, small, memory_grad, output_rows, lanes_away = sync(yi, zi, small, memory_grad, output_rows, lanes_away)
    c_fin, s_mid, yp, zp = merge(
        bits, (c_own, yi, zi, sa_k, sb_k),
        (("join", (0, 0), (1, 0), 96, 0, (0, 0)),
         ("join", (0, 96), (2, 0), 96, 1, (0, 192)),
         ("join", (0, 0), (1, 0), 96, 0, (3, 0)),
         ("join", (0, 96), (2, 0), 96, 1, (2, 0)),
         ("sum", ((3, 0), (1, 96)), 96, (1, 0)),
         ("sum", ((4, 0), (2, 96)), 96, (1, 96))), (384, 192, 192, 192))
    z2i, c_y, c_z = swap_dp(s_mid, 2), swap_dp(yp, 0), swap_dp(zp, 1)
    f_fin = sync(f_fin, yp, zp, s_mid)[0]
    inner_sum, outer_sum, ffn_model, unit_stats = ffn_finish(bits, f_fin, f_y, f_z)
    z2i, c_y, c_z, ffn_model = sync(z2i, c_y, c_z, ffn_model)
    (s_own,) = merge(bits, (s_mid, z2i), (("sum", ((0, 0), (1, 0)), 192, (0, 0)),), (192,))
    s_own = past(s_own, 3)
    yi, zi = swap_dp(s_own[:96], 0), swap_dp(s_own[96:], 1)
    small, lanes_away = sync(small, lanes_away, s_own)[:2]
    lanes_in = swap_chip(lanes_away)
    small = over_group(small)
    yi, zi, small, lanes_in = sync(yi, zi, small, lanes_in)
    small = jnp.concatenate((jnp.pad(small, ((0, 0), (0, 256))), lanes_own + lanes_in))
    s_fin, yp, zp = merge(
        bits, (s_own, yi, zi),
        (("join", (0, 0), (1, 0), 96, 0, (0, 0)),
         ("join", (0, 96), (2, 0), 96, 1, (0, 192)),
         ("join", (0, 0), (1, 0), 96, 0, (2, 0)),
         ("join", (0, 96), (2, 0), 96, 1, (1, 0))), (384, 192, 192))
    s_y, s_z, small = swap_dp(yp, 0), swap_dp(zp, 1), over_first_bits(small)
    early = finish_early(bits, (c_fin, c_y, c_z), sync(ffn_model, yp)[0])
    s_y, s_z, small, *early = sync(s_y, s_z, small, *early)
    for bit in range(2, dp_bits()):
        small = small + swap_dp(small, bit)
    gains_total = small[:3, :D]
    table_sum = bucket_sums(small[3:])
    query_t, keyvalue_t, output_grad, model_part, head_stats, projection_stats = finish_late(bits, (s_fin, s_y, s_z), early)
    query_grad, keyvalue_grad = jnp.swapaxes(query_t, 1, 2), jnp.swapaxes(keyvalue_t, 2, 3)
    model_total = over_group(model_part)
    hidden_units = outer_weight.shape[0] * lax.axis_size("tensor")
    divisors = jnp.array([D] * 6 + [hidden_units] * 2 + [D] * 2 + [hidden_units], f32)
    model_stats = model_total / divisors[:, None]
    return (output_rows, tokens_grad, memory_grad, gains_total, query_grad, keyvalue_grad, output_grad, table_sum,
            inner_sum, outer_sum, model_stats, head_stats, projection_stats, unit_stats)


def solution(mesh):
    rows = P(("dp", "tensor"), None)
    in_specs = (rows, rows, rows, P(), P(None, None, "tensor"), P(None, None, None, "tensor"), P(None, "tensor", None),
                P(None, "tensor"), P(None, None, "tensor"), P("tensor", None), P("dp", None), P("dp", None))
    out_specs = (rows, rows, rows, P(), P(None, None, "tensor"), P(None, None, None, "tensor"),
                 P(None, "tensor", None), P(None, "tensor"), P(None, None, "tensor"), P("tensor", None), P(),
                 P(None, "tensor"), P(None, "tensor"), P(None, "tensor"))
    return jax.shard_map(on_device, mesh=mesh, in_specs=in_specs, out_specs=out_specs, check_vma=False)
```
